32 devices in a mesh: gx: 4 (over y, core), gy: 8 (over z, x).
Axes of the slice: x: 2, y: 2, z: 4, core: 2. Of those that a mesh axis runs over, the one named last changes fastest.
Arguments:
- perturbation: float32 [5, 16, 512], P(None, 'gx', 'gy'), may hold values from -6 to 6
- mean_velocity: float32 [16, 512], P('gx', 'gy'), may hold values from 0.2 to 0.9
- mean_shear: float32 [16, 512], P('gx', 'gy'), may hold values from -4 to 4
- cotangent: float32 [5, 16, 512], P(None, 'gx', 'gy'), may hold values from -6 to 6
- kernel_in: bfloat16 [64, 135], replicated, may hold values from -0.5 to 0.5
- kernel_mid: bfloat16 [64, 1728], replicated, may hold values from -0.15625 to 0.15625
- kernel_out: bfloat16 [5, 1728], replicated, may hold values from -0.15625 to 0.15625
Outputs:
- advanced: float32 [5, 16, 512], P(None, 'gx', 'gy')
- grad_in: float32 [64, 135], replicated
- grad_mid: float32 [64, 1728], replicated
- grad_out: float32 [5, 1728], replicated
The draws below stay inside these ranges and needn't reach their ends.
All inputs are finite; a program needn't handle non-finite values.
Results may differ from the reference program's by a relative error of at most 0.0065.
Values may be sent and summed in bfloat16 or wider, within the bound.
A program may use at most 64 MiB of HBM per device.

```python
import math
import jax
import jax.numpy as jnp
from jax import lax

NZ = 8
HID = 64
FIELDS = 5
STEPS = 2
NX = 16
NY = 64


def level_of(key, extent, split, least, largest):
    def one(dim, shards_of):
        heights = jax.random.uniform(jax.random.fold_in(jax.random.fold_in(key, 6), dim), (shards_of,), jnp.float32, least / len(split), largest / len(split))
        return jnp.repeat(jnp.exp(heights), extent[dim] // shards_of).reshape((-1,) + (1,) * (len(extent) - dim - 1))

    factor_of = one(*split[0])
    for cut in split[1:]:
        factor_of = factor_of * one(*cut)
    return factor_of


def gaussian(key, shape, width, bound, shards=(), dtype=jnp.bfloat16):
    array = jax.random.normal(key, shape, jnp.float32) * width
    if len(shards) > 0:
        array = level_of(key, shape, shards, -0.22, 0.18) * array
    return jnp.clip(array, min=-bound, max=bound).astype(dtype)


def setup_inputs(seed: int = 0) -> dict:
    splits = jax.random.split(jax.random.key(seed), 8)
    return {
        "perturbation": gaussian(splits[0], (FIELDS, NX, NY * NZ), 1.0, 6.0, ((1, 4), (2, 8)), jnp.float32),
        "mean_velocity": jnp.clip(0.2 + 0.7 * jax.random.uniform(splits[1], (NX, NY * NZ), jnp.float32) ** level_of(splits[1], (NX, NY * NZ), ((0, 4), (1, 8)), -0.2, 0.2), 0.2, 0.9),
        "mean_shear": gaussian(splits[2], (NX, NY * NZ), 1.0, 4.0, ((0, 4), (1, 8)), jnp.float32),
        "cotangent": gaussian(splits[3], (FIELDS, NX, NY * NZ), 1.0, 6.0, ((1, 4), (2, 8)), jnp.float32),
        "kernel_in": gaussian(splits[4], (HID, FIELDS * 27), (FIELDS * 27) ** -0.5, 0.5),
        "kernel_mid": gaussian(splits[5], (HID, HID * 27), (HID * 27) ** -0.5, 0.15625),
        "kernel_out": gaussian(splits[6], (FIELDS, HID * 27), (HID * 27) ** -0.5, 0.15625),
    }


TIME_STEP = 0.25
STENCIL_WEIGHTS = (0.75, -0.15, 1.0 / 60.0)

def wrap_depth(grid_field, margin):
    size_z = grid_field.shape[3]
    return jnp.concatenate([grid_field[:, :, :, size_z - margin:], grid_field, grid_field[:, :, :, :margin]], axis=3)

def difference(padded, direction, margin, length):
    summed = None
    for offset, weight in zip((1, 2, 3), STENCIL_WEIGHTS):
        upper_cells = lax.slice_in_dim(padded, margin + offset, margin + offset + length, axis=direction)
        lower_cells = lax.slice_in_dim(padded, margin - offset, margin - offset + length, axis=direction)
        contrib = weight * (upper_cells - lower_cells)
        summed = contrib if summed is None else summed + contrib
    return summed

def rates_from(padded, margin, velocity, shear_rate):
    size_x = padded.shape[1] - 2 * margin
    size_y = padded.shape[2] - 2 * margin
    interior = padded[:, margin:margin + size_x, margin:margin + size_y]
    slope_x = difference(padded[:, :, margin:margin + size_y], 1, margin, size_x)
    slope_y = difference(padded[:, margin:margin + size_x], 2, margin, size_y)
    slope_z = difference(wrap_depth(interior, 3), 3, 3, interior.shape[3])
    divergence = slope_x[1] + slope_y[2] + slope_z[3]
    return jnp.stack([-velocity * slope_x[0] - divergence, -velocity * slope_x[1] - shear_rate * interior[2] - slope_x[4], -velocity * slope_x[2] - slope_y[4], -velocity * slope_x[3] - slope_z[4], -velocity * slope_x[4] - divergence])

def adjoint_fields(adjoint_in, velocity):
    acoustic = adjoint_in[0] + adjoint_in[4]
    return jnp.stack([velocity * adjoint_in[0], velocity * adjoint_in[1] + acoustic, velocity * adjoint_in[2], velocity * adjoint_in[3], velocity * adjoint_in[4] + adjoint_in[1], acoustic, adjoint_in[2], adjoint_in[3]])

def adjoint_from(padded, margin, adjoint_in, shear_rate):
    size_x = padded.shape[1] - 2 * margin
    size_y = padded.shape[2] - 2 * margin
    interior = padded[:, margin:margin + size_x, margin:margin + size_y]
    slope_x = difference(padded[:5, :, margin:margin + size_y], 1, margin, size_x)
    slope_y = difference(padded[5:, margin:margin + size_x], 2, margin, size_y)
    slope_z = difference(wrap_depth(interior[5:], 3), 3, 3, interior.shape[3])
    return jnp.stack([slope_x[0], slope_x[1], slope_x[2] - shear_rate * adjoint_in[1] + slope_y[0], slope_x[3] + slope_z[0], slope_x[4] + slope_y[1] + slope_z[2]])

def conv_valid(padded, kernel):
    return lax.conv_general_dilated(padded[None], kernel, (1, 1, 1), 'VALID', dimension_numbers=('NCDHW', 'OIDHW', 'NCDHW'), preferred_element_type=jnp.float32)[0]

def flip_kernel(kernel):
    return jnp.transpose(jnp.flip(kernel, (2, 3, 4)), (1, 0, 2, 3, 4))

def kernel_grad(padded, gradient):
    channels = padded.shape[0]
    size_x, size_y, size_z = (gradient.shape[1], gradient.shape[2], gradient.shape[3])
    flat_grad = gradient.reshape(gradient.shape[0], -1)
    pieces = []
    for shift_x in range(3):
        for shift_y in range(3):
            for shift_z in range(3):
                window = padded[:, shift_x:shift_x + size_x, shift_y:shift_y + size_y, shift_z:shift_z + size_z]
                pieces.append(lax.dot_general(flat_grad, window.reshape(channels, -1), (((1,), (1,)), ((), ())), preferred_element_type=jnp.float32))
    stacked = jnp.stack(pieces)
    return jnp.transpose(stacked, (1, 2, 0)).reshape(gradient.shape[0], channels * 27)

def closure_forward(grid_field, kernels, padding_fn):
    kernel_in, kernel_mid, kernel_out = kernels
    padded_in = padding_fn(grid_field.astype(jnp.bfloat16))
    hidden_one = jnp.tanh(conv_valid(padded_in, kernel_in)).astype(jnp.bfloat16)
    padded_one = padding_fn(hidden_one)
    hidden_two = jnp.tanh(conv_valid(padded_one, kernel_mid)).astype(jnp.bfloat16)
    padded_two = padding_fn(hidden_two)
    source = conv_valid(padded_two, kernel_out)
    return (source, (padded_in, hidden_one, padded_one, hidden_two, padded_two))

def closure_backward(saved, source_grad, kernels, need_input, padding_fn):
    kernel_in, kernel_mid, kernel_out = kernels
    padded_in, hidden_one, padded_one, hidden_two, padded_two = saved
    error_out = source_grad.astype(jnp.bfloat16)
    grad_out = kernel_grad(padded_two, error_out)
    back_mid = conv_valid(padding_fn(error_out), flip_kernel(kernel_out)) * (1.0 - jnp.square(hidden_two.astype(jnp.float32)))
    error_mid = back_mid.astype(jnp.bfloat16)
    grad_mid = kernel_grad(padded_one, error_mid)
    back_in = conv_valid(padding_fn(error_mid), flip_kernel(kernel_mid)) * (1.0 - jnp.square(hidden_one.astype(jnp.float32)))
    error_in = back_in.astype(jnp.bfloat16)
    grad_in = kernel_grad(padded_in, error_in)
    state_grad = conv_valid(padding_fn(error_in), flip_kernel(kernel_in)) if need_input else None
    return ((grad_in, grad_mid, grad_out), state_grad)

def retreat(adjoint_in, adjoint_fn):
    into_second = 2.0 / 3.0 * adjoint_in + 2.0 / 3.0 * TIME_STEP * adjoint_fn(adjoint_in)
    direct = 1.0 / 3.0 * adjoint_in
    into_first = 0.25 * into_second + 0.25 * TIME_STEP * adjoint_fn(into_second)
    direct = direct + 0.75 * into_second
    carried = direct + into_first + TIME_STEP * adjoint_fn(into_first)
    source_grad = TIME_STEP * (2.0 / 3.0 * adjoint_in + 0.25 * into_second + into_first)
    return (carried, source_grad)

def zero_pad(grid_field):
    return wrap_depth(jnp.pad(grid_field, ((0, 0), (1, 1), (1, 1), (0, 0))), 1)

def reference(perturbation, mean_velocity, mean_shear, cotangent, kernel_in, kernel_mid, kernel_out):
    channels = perturbation.shape[0]
    hidden = kernel_in.shape[0]
    current = perturbation.reshape(channels, NX, NY, NZ)
    velocity = mean_velocity.reshape(NX, NY, NZ)
    shear_rate = mean_shear.reshape(NX, NY, NZ)
    kernels = (kernel_in.reshape(hidden, channels, 3, 3, 3), kernel_mid.reshape(hidden, hidden, 3, 3, 3), kernel_out.reshape(channels, hidden, 3, 3, 3))

    def section_rates(grid_field):
        return rates_from(jnp.pad(grid_field, ((0, 0), (3, 3), (3, 3), (0, 0))), 3, velocity, shear_rate)

    def adjoint_rates(adjoint_in):
        padded = jnp.pad(adjoint_fields(adjoint_in, velocity), ((0, 0), (3, 3), (3, 3), (0, 0)))
        return adjoint_from(padded, 3, adjoint_in, shear_rate)
    history = []
    for step_index in range(STEPS):
        source = closure_forward(current, kernels, zero_pad)[0]
        history.append(current)
        section_one = current + TIME_STEP * (section_rates(current) + source)
        section_two = 0.75 * current + 0.25 * (section_one + TIME_STEP * (section_rates(section_one) + source))
        current = 1.0 / 3.0 * current + 2.0 / 3.0 * (section_two + TIME_STEP * (section_rates(section_two) + source))
    adjoint_in = cotangent.reshape(channels, NX, NY, NZ) * (1.0 / math.sqrt(NX * NY * NZ))
    totals = None
    for step_index in reversed(range(STEPS)):
        carried, source_grad = retreat(adjoint_in, adjoint_rates)
        saved = closure_forward(history[step_index], kernels, zero_pad)[1]
        kernel_grads, state_grad = closure_backward(saved, source_grad, kernels, step_index > 0, zero_pad)
        totals = kernel_grads if totals is None else tuple((sum_old + sum_new for sum_old, sum_new in zip(totals, kernel_grads)))
        if step_index > 0:
            adjoint_in = carried + state_grad
    return (current.reshape(channels, NX, NY * NZ), totals[0], totals[1], totals[2])
```

```python
import functools
import math

import jax
import jax.numpy as jnp
from jax import lax
from jax.experimental import pallas as pl
from jax.experimental.pallas import tpu as pltpu
from jax.sharding import PartitionSpec as P

NZ = 8
LANES = 128
FIELD_ROWS = 8
BLOCK_ROWS = 2 * FIELD_ROWS
RIM = 4
REACH_X = 5
REACH_Y = 3

TIME_STEP = 0.25
STENCIL_WEIGHTS = (0.75, -0.15, 1.0 / 60.0)
MESH = pl.DeviceIdType.MESH
WIRE = jnp.bfloat16
F32 = jnp.float32


def dot(a, b):
    return lax.dot_general(a, b, (((1,), (0,)), ((), ())), preferred_element_type=F32)


def dot_nt(a, b):
    return lax.dot_general(a, b, (((1,), (1,)), ((), ())), preferred_element_type=F32)


def iota(shape, axis):
    return lax.broadcasted_iota(jnp.int32, shape, axis)


def shifted_by(values, size):
    return lax.shift_right_logical(values, size.bit_length() - 1)


def steps_of(values, size, count):
    return sum((values >= size * n).astype(jnp.int32) for n in range(1, count))


def one_hot(condition):
    return jnp.where(condition, 1.0, 0.0).astype(jnp.bfloat16)


def span_of(count, reach):
    span = min(count, 2 * reach + 2)
    return span, span // 2


def slopes(origin_x, origin_yz, grid_x, grid_yz, shape):
    row = iota(shape, 0) + origin_x
    lane = iota(shape, 1) + origin_yz
    depth = lane & (NZ - 1)

    def moved(field, offset, axis):
        return pltpu.roll(field, (-offset) % field.shape[axis], axis)

    def edged(field, axis, position, unit):
        size = (grid_x, grid_yz)[axis]
        result = None
        for offset, weight in zip((1, 2, 3), STENCIL_WEIGHTS):
            step = offset * unit
            upper = jnp.where(position < size - step, moved(field, step, axis), 0.0)
            lower = jnp.where(position >= step, moved(field, -step, axis), 0.0)
            contrib = weight * (upper - lower)
            result = contrib if result is None else result + contrib
        return result

    def along_x(field):
        return edged(field, 0, row, 1)

    def along_y(field):
        return edged(field, 1, lane, NZ)

    def along_z(field):
        result = None
        for offset, weight in zip((1, 2, 3), STENCIL_WEIGHTS):
            upper = jnp.where(
                depth < NZ - offset, moved(field, offset, 1), moved(field, offset - NZ, 1)
            )
            lower = jnp.where(depth >= offset, moved(field, -offset, 1), moved(field, NZ - offset, 1))
            contrib = weight * (upper - lower)
            result = contrib if result is None else result + contrib
        return result

    return along_x, along_y, along_z


def advance(now, velocity, shear, source, channels, slope, write):
    fields = range(channels)
    dx, dy, dz = slope

    def rates(f):
        across = [dx(c) for c in f]
        divergence = across[1] + dy(f[2]) + dz(f[3])
        return (
            -velocity * across[0] - divergence,
            -velocity * across[1] - shear * f[2] - across[4],
            -velocity * across[2] - dy(f[4]),
            -velocity * across[3] - dz(f[4]),
            -velocity * across[4] - divergence,
        )

    rate = rates([now(i) for i in fields])
    one = [now(i) + TIME_STEP * (rate[i] + source(i)) for i in fields]
    rate = rates(one)
    two = [0.75 * now(i) + 0.25 * (one[i] + TIME_STEP * (rate[i] + source(i))) for i in fields]
    rate = rates(two)
    for i in fields:
        write(i, 1.0 / 3.0 * now(i) + 2.0 / 3.0 * (two[i] + TIME_STEP * (rate[i] + source(i))))


def retreat(last, velocity, shear, channels, slope, write_error, write_carried):
    fields = range(channels)
    dx, dy, dz = slope

    def rates(g):
        acoustic = g[0] + g[4]
        return (
            dx(velocity * g[0]),
            dx(velocity * g[1] + acoustic),
            dx(velocity * g[2]) - shear * g[1] + dy(acoustic),
            dx(velocity * g[3]) + dz(acoustic),
            dx(velocity * g[4] + g[1]) + dy(g[2]) + dz(g[3]),
        )

    rate = rates(last)
    second = [2.0 / 3.0 * last[i] + 2.0 / 3.0 * TIME_STEP * rate[i] for i in fields]
    rate = rates(second)
    first = [0.25 * second[i] + 0.25 * TIME_STEP * rate[i] for i in fields]
    for i in fields:
        write_error(i, TIME_STEP * (2.0 / 3.0 * last[i] + 0.25 * second[i] + first[i]))
    if write_carried is None:
        return
    rate = rates(first)
    for i in fields:
        write_carried(i, 1.0 / 3.0 * last[i] + 0.75 * second[i] + first[i] + TIME_STEP * rate[i])


def for_peers(total, body):
    lax.fori_loop(1, total, lambda k, c: (body(k), c)[1], 0, unroll=total <= 32)


def whole_kernel(
    plan, first_ref, second_ref, w1, w2, w3, w3t, w2t, w1t, out_state, out_table,
    block, arrived, fields, sources, flow, carried, zx0, zx1, z1s0, z1s1, z2s0, z2s1, zin, ze2, ze1,
    e1s, e2s, e3s, xs, spread_mat, enter_mat, pick_mat, leave_mat, table, wire, from_core, halved, from_rest,
    send_sems, recv_sems, core_sems, rest_sems, own_sems,
):
    count_x, count_y, channels, hidden, size_x, size_yz = plan
    total = count_x * count_y
    span_x, lead_x = span_of(count_x, REACH_X)
    span_y, lead_y = span_of(count_y, REACH_Y)
    held = span_x * span_y
    all_x, all_y = count_x * size_x, count_y * size_yz // NZ
    grid_x, grid_yz = span_x * size_x, span_y * size_yz
    size_y = size_yz // NZ
    width = size_y + 2 * RIM
    planes = size_x + 2 * RIM
    index_x, index_y = lax.axis_index("gx"), lax.axis_index("gy")
    me = index_y * count_x + index_x
    origin_x = 0 if span_x == count_x else index_x - lead_x
    origin_y = 0 if span_y == count_y else index_y - lead_y
    tiles = grid_yz // LANES
    tile_rows = 2 * span_x * BLOCK_ROWS
    flat = channels * grid_x

    def device(place):
        return {"gx": lax.rem(place, count_x), "gy": lax.div(place, count_x)}

    barrier = pltpu.get_barrier_semaphore()
    for_peers(
        total,
        lambda k: pl.semaphore_signal(
            barrier, inc=1, device_id=device(lax.rem(me + k, total)), device_id_type=MESH
        ),
    )

    rows = FIELD_ROWS * grid_x
    r, k = iota((rows, tile_rows), 0), iota((rows, tile_rows), 1)
    field = steps_of(r, grid_x, FIELD_ROWS)
    at_x = r - field * grid_x
    part = steps_of(k, tile_rows // 2, 2)
    rest = k - part * (tile_rows // 2)
    owner = shifted_by(rest, BLOCK_ROWS)
    inner = rest & (BLOCK_ROWS - 1)
    odd = at_x & 1
    row = (shifted_by(at_x, 2) & 1) * FIELD_ROWS + field
    same = (owner == shifted_by(at_x, size_x)) & (inner == row)
    spread_mat[:rows] = one_hot(same & (part == odd))
    spread_mat[rows:] = one_hot(same & (part != odd))
    r, k = iota((grid_yz, LANES), 0), iota((grid_yz, LANES), 1)
    enter_mat[...] = one_hot(
        ((r & (NZ - 1)) == shifted_by(k, width))
        & (shifted_by(r, NZ) + origin_y * size_y == index_y * size_y - RIM + (k & (width - 1)))
        & (shifted_by(r, NZ) + origin_y * size_y >= 0)
        & (shifted_by(r, NZ) + origin_y * size_y < all_y)
    )
    r, k = iota((planes * 16, 3 * flat), 0), iota((planes * 16, 3 * flat), 1)
    inner = r & 15
    side = steps_of(inner, channels, 3)
    part = steps_of(k, flat, 3)
    rest = k - part * flat
    field = steps_of(rest, grid_x, channels)
    pick_mat[...] = one_hot(
        (inner < 3 * channels)
        & (part == side)
        & (field == inner - channels * side)
        & (
            rest - field * grid_x + origin_x * size_x
            == index_x * size_x - RIM + shifted_by(r, 16)
        )
        & (rest - field * grid_x + origin_x * size_x >= 0)
        & (rest - field * grid_x + origin_x * size_x < all_x)
    )
    r, k = iota((2 * LANES, LANES), 0), iota((2 * LANES, LANES), 1)
    inner, lane = r & (LANES - 1), k & (size_yz - 1)
    leave_mat[...] = one_hot(
        (shifted_by(r, LANES) == steps_of(k, size_yz, 2))
        & (shifted_by(inner, width) == (lane & (NZ - 1)))
        & ((inner & (width - 1)) == shifted_by(lane, NZ) + RIM)
    )
    place = iota((8, LANES), 1) & (width - 1)
    at_y = place + (index_y * size_y - RIM)
    valid_y = jnp.where((at_y >= 0) & (at_y < all_y), 1.0, 0.0)
    mine = jnp.where((place >= RIM) & (place < RIM + size_y), 1.0, 0.0)

    def inside(p):
        at = index_x * size_x - RIM + p
        scale = jnp.where((at >= 0) & (at < all_x), 1.0, 0.0).astype(F32)
        return (valid_y * scale)[:1]

    block[0] = first_ref[...]
    block[1] = second_ref[...]
    pl.semaphore_wait(barrier, total - 1)

    own_slot = (index_y - origin_y) * span_x + index_x - origin_x

    def remote(turn, k):
        place = lax.rem(lead_y * span_x + lead_x + k, held)
        shift_x, shift_y = lax.rem(place, span_x) - lead_x, lax.div(place, span_x) - lead_y
        slot_x = index_x if span_x == count_x else lead_x - shift_x
        slot_y = index_y if span_y == count_y else lead_y - shift_y
        return pltpu.make_async_remote_copy(
            src_ref=block.at[turn],
            dst_ref=arrived.at[turn, slot_y * span_x + slot_x],
            send_sem=send_sems.at[turn, k - 1],
            recv_sem=recv_sems.at[turn, k - 1],
            device_id={
                "gx": lax.rem(index_x + shift_x + count_x, count_x),
                "gy": lax.rem(index_y + shift_y + count_y, count_y),
            },
            device_id_type=MESH,
        )

    def keep_own(turn):
        return pltpu.make_async_copy(block.at[turn], arrived.at[turn, own_slot], own_sems.at[turn])

    def send(turn):
        for_peers(held, lambda k: remote(turn, k).start())
        keep_own(turn).start()

    def receive(turn, number, target):
        for_peers(held, lambda k: remote(turn, k).wait_recv())
        keep_own(turn).wait()
        height = number * grid_x
        half = steps_of(iota((height, LANES), 1), size_yz, 2)
        keep = half == (iota((height, LANES), 0) & 1)
        matrix = jnp.concatenate([spread_mat[:height], spread_mat[rows : rows + height]], axis=0)
        for t in range(tiles):
            slots = arrived[turn, t * 2 * span_x : (t + 1) * 2 * span_x].reshape(tile_rows, LANES)
            both = dot(matrix, slots)
            target[:height, t * LANES : (t + 1) * LANES] = jnp.where(
                keep, both[:height], pltpu.roll(both[height:], size_yz, 1)
            )

    def at(ref, i, start=0):
        return ref[(start + i) * grid_x : (start + i + 1) * grid_x, :]

    def put(ref):
        def write(i, value):
            ref[i * grid_x : (i + 1) * grid_x, :] = value.astype(ref.dtype)

        return write

    def enter(values):
        return dot(values, enter_mat[...])

    def stacked(window, target):
        three = jnp.concatenate(
            [pltpu.roll(window, width, 1), window, pltpu.roll(window, LANES - width, 1)], axis=0
        )
        target[...] = dot(pick_mat[...], three.astype(jnp.bfloat16)).astype(jnp.bfloat16)

    def conv(weights, source, unit, first, count, emit):
        matrix = weights[...]
        outs = matrix.shape[0] // 3
        for p in range(first, first + count, 2):
            columns = jnp.concatenate(
                [source[(p - 1 + q) * unit : (p + 2 + q) * unit, :] for q in (0, 1)], axis=1
            )
            product = dot(matrix, columns)
            for q in (0, 1):
                part = product[:, q * LANES : (q + 1) * LANES]
                emit(
                    p + q,
                    pltpu.roll(part[:outs], 1, 1)
                    + part[outs : 2 * outs]
                    + pltpu.roll(part[2 * outs :], LANES - 1, 1),
                )

    def store_stack(target, p, value):
        base = p * 3 * hidden
        for c, turned in enumerate((width, 0, LANES - width)):
            moved = pltpu.roll(value, turned, 1) if turned else value
            target[base + c * hidden : base + (c + 1) * hidden, :] = moved.astype(jnp.bfloat16)

    def middle(source, p):
        return source[(3 * p + 1) * hidden : (3 * p + 2) * hidden, :].astype(F32)

    def store_error(target, p, value):
        if not RIM <= p < RIM + size_x:
            return
        kept = value * mine[:1]
        for b, turned in enumerate((LANES - 1, 0, 1)):
            moved = pltpu.roll(kept, turned, 1) if turned else kept
            target[
                b * hidden : (b + 1) * hidden, (p - RIM) * LANES : (p - RIM + 1) * LANES
            ] = moved.astype(jnp.bfloat16)

    def forward(zx, z1, z2, margin, turn):
        conv(
            w1, zx, 16, RIM - margin + 1, size_x + 2 * margin - 2,
            lambda p, v: store_stack(z1, p, jnp.tanh(v) * inside(p)),
        )
        conv(
            w2, z1, 3 * hidden, RIM - margin + 2, size_x + 2 * margin - 4,
            lambda p, v: store_stack(z2, p, jnp.tanh(v) * inside(p)),
        )
        leave(w3, z2, turn)

    def leave(weights, source, turn):
        kept = {}
        conv(weights, source, 3 * hidden, RIM, size_x, lambda p, v: kept.update({p - RIM: v}))
        sides = [
            jnp.concatenate([kept[q + 2 * i] for i in range(size_x // 2)], axis=0) for q in (0, 1)
        ]
        both = jnp.concatenate(sides, axis=1).astype(jnp.bfloat16)
        block[turn] = dot(both, leave_mat[...]).astype(WIRE)
        send(turn)

    def backward(ref, zx, z1, z2, margin):
        window = enter(ref[...])
        stacked(window, zin)
        kept = window * mine[:1]
        three = jnp.concatenate(
            [pltpu.roll(kept, LANES - 1, 1), kept, pltpu.roll(kept, 1, 1)], axis=0
        )
        own = dot(
            pick_mat[RIM * 16 : (RIM + size_x) * 16, :], three.astype(jnp.bfloat16)
        ).astype(jnp.bfloat16)
        for p in range(size_x):
            e3s[:, p * LANES : (p + 1) * LANES] = own[p * 16 : (p + 1) * 16]
        span = margin - 2

        def second(p, v):
            slope = 1.0 - jnp.square(middle(z2, p))
            value = v * slope * inside(p)
            store_stack(ze2, p, value)
            store_error(e2s, p, value)

        def first(p, v):
            slope = 1.0 - jnp.square(middle(z1, p))
            value = v * slope * inside(p)
            if span > 1:
                store_stack(ze1, p, value)
            store_error(e1s, p, value)

        conv(w3t, zin, 16, RIM - span, size_x + 2 * span, second)
        conv(w2t, ze2, 3 * hidden, RIM - span + 1, size_x + 2 * span - 2, first)

    def gradients(zx, z1, z2, save):
        def wide(source, unit, low, high):
            return jnp.concatenate(
                [
                    source[(RIM + p - 1) * unit + low : (RIM + p - 1) * unit + high, :]
                    for p in range(size_x)
                ],
                axis=1,
            )

        deep = 9 * hidden
        zero = jnp.zeros((hidden, size_x * LANES), jnp.bfloat16)
        e2 = e2s[...]
        values = wide(z1, 3 * hidden, 0, deep)
        save(0, dot_nt(values, e2[: 2 * hidden]))
        last = e2[2 * hidden :]
        save(
            deep,
            dot_nt(values[: deep // 2], jnp.concatenate([last, zero], axis=0))
            + dot_nt(values[deep // 2 :], jnp.concatenate([zero, last], axis=0)),
        )
        start = deep + deep // 2
        e1 = e1s[...]
        values = wide(zx, 16, 0, 48)
        save(start, dot_nt(values, e1[: 2 * hidden]))
        start += 48
        tail = dot_nt(values, jnp.concatenate([e1[2 * hidden :], zero], axis=0))
        e3 = e3s[...]
        product = dot_nt(e3, wide(z2, 3 * hidden, 0, 8 * hidden))
        for j in range(8 * hidden // LANES):
            save(start, product[:, j * LANES : (j + 1) * LANES])
            start += 16
        late = dot_nt(
            e3, jnp.concatenate([zero, wide(z2, 3 * hidden, 8 * hidden, deep)], axis=0)
        )
        save(start, tail[:16] + late)
        save(start + 16, tail[16:])

    slope = slopes(
        origin_x * size_x, origin_y * size_yz, all_x, all_y * NZ, (grid_x, grid_yz)
    )
    send(0)
    send(1)
    receive(0, channels, fields)
    stacked(enter(fields[...].astype(jnp.bfloat16)), zx0)
    forward(zx0, z1s0, z2s0, 3, 2)

    receive(1, channels + 2, flow)
    velocity, shear = at(flow, 0), at(flow, 1)
    error = xs
    retreat(
        [at(flow, i, 2) for i in range(channels)], velocity, shear, channels, slope,
        put(error), put(carried),
    )
    receive(2, channels, sources)
    advance(
        lambda i: at(fields, i), velocity, shear, lambda i: at(sources, i), channels, slope,
        put(fields),
    )
    stacked(enter(fields[...].astype(jnp.bfloat16)), zx1)
    forward(zx1, z1s1, z2s1, 4, 3)
    backward(error, zx1, z1s1, z2s1, 4)
    leave(w1t, ze1, 4)

    def save(start, value):
        table[start : start + value.shape[0], :] = value

    gradients(zx1, z1s1, z2s1, save)
    receive(3, channels, sources)
    advance(
        lambda i: at(fields, i), velocity, shear, lambda i: at(sources, i), channels, slope,
        put(fields),
    )
    slot = index_y - origin_y
    tile = lax.div(slot, 2)
    for i in range(channels):
        value = fields[i * grid_x : (i + 1) * grid_x, pl.ds(pl.multiple_of(tile * LANES, LANES), LANES)]
        value = jnp.where(lax.rem(slot, 2) == 0, value, pltpu.roll(value, size_yz, 1))
        value = pltpu.roll(value, lax.rem(grid_x - (index_x - origin_x) * size_x, grid_x), 0)
        out_state[i * size_x : (i + 1) * size_x, :] = value[:size_x]
    receive(4, channels, sources)
    retreat(
        [at(carried, i) + at(sources, i) for i in range(channels)],
        velocity, shear, channels, slope, put(error), None,
    )
    backward(error, zx0, z1s0, z2s0, 3)

    def finish(start, value):
        wire[start : start + value.shape[0], :] = (
            table[start : start + value.shape[0], :] + value
        ).astype(WIRE)

    height = wire.shape[0]
    used = table.shape[0]
    if height > used:
        wire[used:, :] = jnp.zeros((height - used, LANES), WIRE)
    gradients(zx0, z1s0, z2s0, finish)

    pairs = total // 2
    chunk = height // total
    core = lax.rem(index_x, 2)
    pair = index_y * (count_x // 2) + lax.div(index_x, 2)

    def at_pair(place, side):
        return {
            "gx": lax.rem(place, count_x // 2) * 2 + side, "gy": lax.div(place, count_x // 2)
        }

    half = height // 2
    copy = pltpu.make_async_remote_copy(
        src_ref=wire.at[pl.ds(pl.multiple_of((1 - core) * half, 16), half)],
        dst_ref=from_core,
        send_sem=core_sems.at[0],
        recv_sem=core_sems.at[1],
        device_id=at_pair(pair, 1 - core),
        device_id_type=MESH,
    )
    copy.start()
    copy.wait()
    halved[...] = (
        wire[pl.ds(pl.multiple_of(core * half, 16), half), :].astype(F32)
        + from_core[...].astype(F32)
    ).astype(WIRE)

    def scatter(k):
        other = lax.rem(pair + k, pairs)
        return pltpu.make_async_remote_copy(
            src_ref=halved.at[pl.ds(pl.multiple_of(other * chunk, 16), chunk)],
            dst_ref=from_rest.at[k - 1],
            send_sem=rest_sems.at[0, k - 1],
            recv_sem=rest_sems.at[1, k - 1],
            device_id=at_pair(other, core),
            device_id_type=MESH,
        )

    for_peers(pairs, lambda k: scatter(k).start())
    for_peers(pairs, lambda k: scatter(k).wait_recv())
    summed = halved[pl.ds(pl.multiple_of(pair * chunk, 16), chunk), :].astype(F32)
    for k in range(pairs - 1):
        summed = summed + from_rest[k].astype(F32)
    spot = pl.ds(pl.multiple_of(core * half + pair * chunk, 16), chunk)
    out_table[spot, :] = summed.astype(WIRE)

    def gather(k):
        other = lax.rem(pair + k, pairs)
        return pltpu.make_async_remote_copy(
            src_ref=out_table.at[spot],
            dst_ref=out_table.at[spot],
            send_sem=rest_sems.at[2, k - 1],
            recv_sem=rest_sems.at[3, k - 1],
            device_id=at_pair(other, core),
            device_id_type=MESH,
        )

    for_peers(pairs, lambda k: gather(k).start())
    for_peers(pairs, lambda k: gather(k).wait_recv())
    side = pl.ds(pl.multiple_of(core * half, 16), half)
    copy = pltpu.make_async_remote_copy(
        src_ref=out_table.at[side],
        dst_ref=out_table.at[side],
        send_sem=core_sems.at[2],
        recv_sem=core_sems.at[3],
        device_id=at_pair(pair, 1 - core),
        device_id_type=MESH,
    )
    copy.start()
    copy.wait()
    for_peers(pairs, lambda k: scatter(k).wait_send())
    for_peers(pairs, lambda k: gather(k).wait_send())
    for turn in range(5):
        for_peers(held, lambda k: remote(turn, k).wait_send())


def kernel_rows(kernel, outs_to):
    outs, ins = kernel.shape[:2]
    kernel = jnp.pad(kernel, ((0, outs_to - outs),) + ((0, 0),) * 4)
    matrix = jnp.transpose(kernel, (3, 0, 2, 4, 1)).reshape(3 * outs_to, 3, 3 * ins)
    if 3 * ins < 16:
        matrix = jnp.pad(matrix, ((0, 0), (0, 0), (0, 16 - 3 * ins)))
    return matrix.reshape(3 * outs_to, -1)


def turn_kernel(kernel):
    return jnp.transpose(jnp.flip(kernel, (2, 3, 4)), (1, 0, 2, 3, 4))


def body(perturbation, mean_velocity, mean_shear, cotangent, kernel_in, kernel_mid, kernel_out):
    channels, size_x, size_yz = perturbation.shape
    hidden = kernel_in.shape[0]
    count_x, count_y = lax.axis_size("gx"), lax.axis_size("gy")
    total = count_x * count_y
    span_x, span_y = span_of(count_x, REACH_X)[0], span_of(count_y, REACH_Y)[0]
    held = span_x * span_y
    grid_x, grid_yz = span_x * size_x, span_y * size_yz
    planes = size_x + 2 * RIM
    kernels = (
        kernel_in.reshape(hidden, channels, 3, 3, 3),
        kernel_mid.reshape(hidden, hidden, 3, 3, 3),
        kernel_out.reshape(channels, hidden, 3, 3, 3),
    )
    tall = (hidden, hidden, FIELD_ROWS)
    weights = [kernel_rows(k, t) for k, t in zip(kernels, tall)]
    weights += [
        kernel_rows(turn_kernel(kernels[n]), t)
        for n, t in ((2, hidden), (1, hidden), (0, FIELD_ROWS))
    ]

    def packed(arrays):
        more = FIELD_ROWS - arrays.shape[0]
        arrays = jnp.pad(arrays.astype(WIRE), ((0, more), (0, 0), (0, 0)))
        arrays = arrays.reshape(FIELD_ROWS, 2, LANES)
        return jnp.transpose(arrays, (1, 0, 2)).reshape(BLOCK_ROWS, LANES)

    scaled = cotangent * (1.0 / math.sqrt(total * size_x * size_yz))
    operands = [
        packed(perturbation),
        packed(jnp.concatenate([mean_velocity[None], mean_shear[None], scaled])),
    ] + weights
    used = 1024
    unit = total * 16
    height = -(-used // unit) * unit
    deep, wide = 3 * hidden, size_x * LANES
    b16 = jnp.bfloat16
    vmem = pltpu.VMEM
    scratch = [
        vmem((5, BLOCK_ROWS, LANES), WIRE),
        vmem((5, held, BLOCK_ROWS, LANES), WIRE),
        vmem((channels * grid_x, grid_yz), F32),
        vmem((channels * grid_x, grid_yz), F32),
        vmem(((channels + 2) * grid_x, grid_yz), F32),
        vmem((channels * grid_x, grid_yz), F32),
        vmem((planes * 16, LANES), b16),
        vmem((planes * 16, LANES), b16),
        vmem((planes * deep, LANES), b16),
        vmem((planes * deep, LANES), b16),
        vmem((planes * deep, LANES), b16),
        vmem((planes * deep, LANES), b16),
        vmem((planes * 16, LANES), b16),
        vmem((planes * deep, LANES), b16),
        vmem((planes * deep, LANES), b16),
        vmem((deep, wide), b16),
        vmem((deep, wide), b16),
        vmem((16, wide), b16),
        vmem((channels * grid_x, grid_yz), b16),
        vmem((2 * FIELD_ROWS * grid_x, 2 * span_x * BLOCK_ROWS), b16),
        vmem((grid_yz, LANES), b16),
        vmem((planes * 16, 3 * channels * grid_x), b16),
        vmem((2 * LANES, LANES), b16),
        vmem((used, LANES), F32),
        vmem((height, LANES), WIRE),
        vmem((height // 2, LANES), WIRE),
        vmem((height // 2, LANES), WIRE),
        vmem((total // 2 - 1, height // total, LANES), WIRE),
        pltpu.SemaphoreType.DMA((5, held - 1)),
        pltpu.SemaphoreType.DMA((5, held - 1)),
        pltpu.SemaphoreType.DMA((4,)),
        pltpu.SemaphoreType.DMA((4, total // 2 - 1)),
        pltpu.SemaphoreType.DMA((5,)),
    ]
    state, table = pl.pallas_call(
        functools.partial(whole_kernel, (count_x, count_y, channels, hidden, size_x, size_yz)),
        out_shape=[
            jax.ShapeDtypeStruct((channels * size_x, LANES), F32),
            jax.ShapeDtypeStruct((height, LANES), WIRE),
        ],
        in_specs=[pl.BlockSpec(memory_space=pltpu.VMEM)] * len(operands),
        out_specs=[pl.BlockSpec(memory_space=pltpu.VMEM)] * 2,
        scratch_shapes=scratch,
        compiler_params=pltpu.CompilerParams(
            collective_id=0, has_side_effects=True, vmem_limit_bytes=56 * 2**20
        ),
    )(*operands)

    advanced = state.reshape(channels, size_x, LANES)[:, :, :size_yz]
    table = table.astype(F32)
    deep = 9 * hidden
    ahead = table[:deep].reshape(3, 3, hidden, 2, hidden)
    folded = table[deep : deep + deep // 2]
    behind = jnp.concatenate([folded[:, :hidden], folded[:, hidden:]], axis=0)
    behind = behind.reshape(3, 3, hidden, 1, hidden)
    grad_mid = jnp.transpose(jnp.concatenate([ahead, behind], axis=3), (4, 2, 0, 3, 1))
    start = deep + deep // 2
    end = start + 48 + 8 * hidden // LANES * 16
    lead = jnp.concatenate([table[start : start + 48], table[end : end + 48, :hidden]], axis=1)
    lead = lead.reshape(3, 16, 3, hidden)[:, : 3 * channels].reshape(3, 3, channels, 3, hidden)
    grad_in = jnp.transpose(lead, (4, 2, 0, 3, 1))
    trail = table[start + 48 : end].reshape(-1, 16, LANES)
    trail = jnp.transpose(trail, (1, 0, 2)).reshape(16, 8 * hidden)
    trail = jnp.concatenate([trail, table[end : end + 16, hidden:]], axis=1)
    trail = trail[: 3 * channels].reshape(3, channels, 3, 3, hidden)
    grad_out = jnp.transpose(trail, (1, 4, 2, 0, 3))
    return (
        advanced,
        grad_in.reshape(hidden, channels * 27),
        grad_mid.reshape(hidden, hidden * 27),
        grad_out.reshape(channels, hidden * 27),
    )


def solution(mesh):
    return jax.shard_map(
        body,
        mesh=mesh,
        in_specs=(
            P(None, "gx", "gy"),
            P("gx", "gy"),
            P("gx", "gy"),
            P(None, "gx", "gy"),
            P(),
            P(),
            P(),
        ),
        out_specs=(P(None, "gx", "gy"), P(), P(), P()),
        check_vma=False,
    )
```

```python
import functools
import math

import jax
import jax.numpy as jnp
from jax import lax
from jax.experimental import pallas as pl
from jax.experimental.pallas import tpu as pltpu
from jax.sharding import PartitionSpec as P

NZ = 8
LANES = 128
FIELD_ROWS = 8
BLOCK_ROWS = 2 * FIELD_ROWS
RIM = 4
REACH_X = 5
REACH_Y = 3

TIME_STEP = 0.25
STENCIL_WEIGHTS = (0.75, -0.15, 1.0 / 60.0)
MESH = pl.DeviceIdType.MESH
WIRE = jnp.bfloat16
F32 = jnp.float32


def dot(a, b):
    return lax.dot_general(a, b, (((1,), (0,)), ((), ())), preferred_element_type=F32)


def dot_nt(a, b):
    return lax.dot_general(a, b, (((1,), (1,)), ((), ())), preferred_element_type=F32)


def iota(shape, axis):
    return lax.broadcasted_iota(jnp.int32, shape, axis)


def shifted_by(values, size):
    return lax.shift_right_logical(values, size.bit_length() - 1)


def steps_of(values, size, count):
    return sum((values >= size * n).astype(jnp.int32) for n in range(1, count))


def one_hot(condition):
    return jnp.where(condition, 1.0, 0.0).astype(jnp.bfloat16)


def span_of(count, reach):
    span = min(count, 2 * reach + 2)
    return span, span // 2


def slopes(origin_x, origin_yz, grid_x, grid_yz, shape):
    row = iota(shape, 0) + origin_x
    lane = iota(shape, 1) + origin_yz
    depth = lane & (NZ - 1)

    def moved(field, offset, axis):
        return pltpu.roll(field, (-offset) % field.shape[axis], axis)

    def edged(field, axis, position, unit):
        size = (grid_x, grid_yz)[axis]
        result = None
        for offset, weight in zip((1, 2, 3), STENCIL_WEIGHTS):
            step = offset * unit
            upper = jnp.where(position < size - step, moved(field, step, axis), 0.0)
            lower = jnp.where(position >= step, moved(field, -step, axis), 0.0)
            contrib = weight * (upper - lower)
            result = contrib if result is None else result + contrib
        return result

    def along_x(field):
        return edged(field, 0, row, 1)

    def along_y(field):
        return edged(field, 1, lane, NZ)

    def along_z(field):
        result = None
        for offset, weight in zip((1, 2, 3), STENCIL_WEIGHTS):
            upper = jnp.where(
                depth < NZ - offset, moved(field, offset, 1), moved(field, offset - NZ, 1)
            )
            lower = jnp.where(depth >= offset, moved(field, -offset, 1), moved(field, NZ - offset, 1))
            contrib = weight * (upper - lower)
            result = contrib if result is None else result + contrib
        return result

    return along_x, along_y, along_z


def advance(now, velocity, shear, source, channels, slope, write):
    fields = range(channels)
    dx, dy, dz = slope

    def rates(f):
        across = [dx(c) for c in f]
        divergence = across[1] + dy(f[2]) + dz(f[3])
        return (
            -velocity * across[0] - divergence,
            -velocity * across[1] - shear * f[2] - across[4],
            -velocity * across[2] - dy(f[4]),
            -velocity * across[3] - dz(f[4]),
            -velocity * across[4] - divergence,
        )

    rate = rates([now(i) for i in fields])
    one = [now(i) + TIME_STEP * (rate[i] + source(i)) for i in fields]
    rate = rates(one)
    two = [0.75 * now(i) + 0.25 * (one[i] + TIME_STEP * (rate[i] + source(i))) for i in fields]
    rate = rates(two)
    for i in fields:
        write(i, 1.0 / 3.0 * now(i) + 2.0 / 3.0 * (two[i] + TIME_STEP * (rate[i] + source(i))))


def retreat(last, velocity, shear, channels, slope, write_error, write_carried):
    fields = range(channels)
    dx, dy, dz = slope

    def rates(g):
        acoustic = g[0] + g[4]
        return (
            dx(velocity * g[0]),
            dx(velocity * g[1] + acoustic),
            dx(velocity * g[2]) - shear * g[1] + dy(acoustic),
            dx(velocity * g[3]) + dz(acoustic),
            dx(velocity * g[4] + g[1]) + dy(g[2]) + dz(g[3]),
        )

    rate = rates(last)
    second = [2.0 / 3.0 * last[i] + 2.0 / 3.0 * TIME_STEP * rate[i] for i in fields]
    rate = rates(second)
    first = [0.25 * second[i] + 0.25 * TIME_STEP * rate[i] for i in fields]
    for i in fields:
        write_error(i, TIME_STEP * (2.0 / 3.0 * last[i] + 0.25 * second[i] + first[i]))
    if write_carried is None:
        return
    rate = rates(first)
    for i in fields:
        write_carried(i, 1.0 / 3.0 * last[i] + 0.75 * second[i] + first[i] + TIME_STEP * rate[i])


def for_peers(total, body):
    lax.fori_loop(1, total, lambda k, c: (body(k), c)[1], 0, unroll=total <= 32)


def whole_kernel(
    plan, state_ref, velocity_ref, shear_ref, cotangent_ref, kernel_in, kernel_mid, kernel_out,
    out_state, grad_in, grad_mid, grad_out,
    block, arrived, fields, sources, flow, carried, zx0, zx1, z1s0, z1s1, z2s0, z2s1, zin, ze2, ze1,
    e1s, e2s, e3s, xs, packs, laid, turned_kernels, w1, w23, w3t, w2t, w1t, spread_mat, enter_mat, pick_mat, leave_mat, name_mat,
    place_mat, table, wire, from_core, halved, from_rest, out_table,
    send_sems, recv_sems, core_sems, rest_sems, own_sems,
):
    count_x, count_y, channels, hidden, size_x, size_yz = plan
    total = count_x * count_y
    span_x, lead_x = span_of(count_x, REACH_X)
    span_y, lead_y = span_of(count_y, REACH_Y)
    held = span_x * span_y
    all_x, all_y = count_x * size_x, count_y * size_yz // NZ
    grid_x, grid_yz = span_x * size_x, span_y * size_yz
    size_y = size_yz // NZ
    width = size_y + 2 * RIM
    planes = size_x + 2 * RIM
    index_x, index_y = lax.axis_index("gx"), lax.axis_index("gy")
    me = index_y * count_x + index_x
    origin_x = 0 if span_x == count_x else index_x - lead_x
    origin_y = 0 if span_y == count_y else index_y - lead_y
    tiles = grid_yz // LANES
    tile_rows = 2 * span_x * BLOCK_ROWS
    flat = channels * grid_x

    def device(place):
        return {"gx": lax.rem(place, count_x), "gy": lax.div(place, count_x)}

    barrier = pltpu.get_barrier_semaphore()
    for_peers(
        total,
        lambda k: pl.semaphore_signal(
            barrier, inc=1, device_id=device(lax.rem(me + k, total)), device_id_type=MESH
        ),
    )

    rows = FIELD_ROWS * grid_x
    r, k = iota((rows, tile_rows), 0), iota((rows, tile_rows), 1)
    field = steps_of(r, grid_x, FIELD_ROWS)
    at_x = r - field * grid_x
    part = steps_of(k, tile_rows // 2, 2)
    rest = k - part * (tile_rows // 2)
    owner = shifted_by(rest, BLOCK_ROWS)
    inner = rest & (BLOCK_ROWS - 1)
    odd = at_x & 1
    row = (shifted_by(at_x, 2) & 1) * FIELD_ROWS + field
    same = (owner == shifted_by(at_x, size_x)) & (inner == row)
    spread_mat[:rows] = one_hot(same & (part == odd))
    spread_mat[rows:] = one_hot(same & (part != odd))
    r, k = iota((grid_yz, LANES), 0), iota((grid_yz, LANES), 1)
    enter_mat[...] = one_hot(
        ((r & (NZ - 1)) == shifted_by(k, width))
        & (shifted_by(r, NZ) + origin_y * size_y == index_y * size_y - RIM + (k & (width - 1)))
        & (shifted_by(r, NZ) + origin_y * size_y >= 0)
        & (shifted_by(r, NZ) + origin_y * size_y < all_y)
    )
    r, k = iota((planes * 16, 3 * flat), 0), iota((planes * 16, 3 * flat), 1)
    inner = r & 15
    side = steps_of(inner, channels, 3)
    part = steps_of(k, flat, 3)
    rest = k - part * flat
    field = steps_of(rest, grid_x, channels)
    pick_mat[...] = one_hot(
        (inner < 3 * channels)
        & (part == side)
        & (field == inner - channels * side)
        & (
            rest - field * grid_x + origin_x * size_x
            == index_x * size_x - RIM + shifted_by(r, 16)
        )
        & (rest - field * grid_x + origin_x * size_x >= 0)
        & (rest - field * grid_x + origin_x * size_x < all_x)
    )
    r, k = iota((2 * LANES, LANES), 0), iota((2 * LANES, LANES), 1)
    inner, lane = r & (LANES - 1), k & (size_yz - 1)
    leave_mat[...] = one_hot(
        (shifted_by(r, LANES) == steps_of(k, size_yz, 2))
        & (shifted_by(inner, width) == (lane & (NZ - 1)))
        & ((inner & (width - 1)) == shifted_by(lane, NZ) + RIM)
    )
    place = iota((8, LANES), 1) & (width - 1)
    at_y = place + (index_y * size_y - RIM)
    valid_y = jnp.where((at_y >= 0) & (at_y < all_y), 1.0, 0.0)
    mine = jnp.where((place >= RIM) & (place < RIM + size_y), 1.0, 0.0)

    def inside(p):
        at = index_x * size_x - RIM + p
        scale = jnp.where((at >= 0) & (at < all_x), 1.0, 0.0).astype(F32)
        return (valid_y * scale)[:1]

    r, k = iota((48, 256), 0), iota((48, 256), 1)
    inner = r & 15
    side = steps_of(inner, channels, 3)
    for b in range(3):
        goal = (inner - channels * side) * 27 + shifted_by(r, 16) * 9 + b * 3 + side
        name_mat[b * 48 : (b + 1) * 48] = one_hot((inner < 3 * channels) & (goal == k))
    r, k = iota((16, LANES), 0), iota((16, LANES), 1)
    for b in range(3):
        place_mat[b * 16 : (b + 1) * 16] = one_hot(
            (r >= b * channels) & (r < (b + 1) * channels) & (k == r - b * channels + hidden)
        )

    def pack(turn, rows_of):
        packs[...] = jnp.zeros(packs.shape, F32)
        for f, at_row in enumerate(rows_of):
            for x in range(size_x):
                spot = (x // 2) * FIELD_ROWS + f
                packs[x % 2, spot : spot + 1, :size_yz] = at_row(x)
        block[turn] = (packs[0] + pltpu.roll(packs[1], size_yz, 1)).astype(WIRE)

    pack(0, [lambda x, f=f: state_ref[f, x : x + 1, :] for f in range(channels)])
    scale = 1.0 / math.sqrt(total * size_x * size_yz)
    pack(
        1,
        [lambda x: velocity_ref[x : x + 1, :], lambda x: shear_ref[x : x + 1, :]]
        + [lambda x, f=f: cotangent_ref[f, x : x + 1, :] * scale for f in range(channels)],
    )
    pl.semaphore_wait(barrier, total - 1)

    own_slot = (index_y - origin_y) * span_x + index_x - origin_x

    def remote(turn, k):
        place = lax.rem(lead_y * span_x + lead_x + k, held)
        shift_x, shift_y = lax.rem(place, span_x) - lead_x, lax.div(place, span_x) - lead_y
        slot_x = index_x if span_x == count_x else lead_x - shift_x
        slot_y = index_y if span_y == count_y else lead_y - shift_y
        return pltpu.make_async_remote_copy(
            src_ref=block.at[turn],
            dst_ref=arrived.at[turn, slot_y * span_x + slot_x],
            send_sem=send_sems.at[turn, k - 1],
            recv_sem=recv_sems.at[turn, k - 1],
            device_id={
                "gx": lax.rem(index_x + shift_x + count_x, count_x),
                "gy": lax.rem(index_y + shift_y + count_y, count_y),
            },
            device_id_type=MESH,
        )

    def keep_own(turn):
        return pltpu.make_async_copy(block.at[turn], arrived.at[turn, own_slot], own_sems.at[turn])

    def send(turn):
        for_peers(held, lambda k: remote(turn, k).start())
        keep_own(turn).start()

    def receive(turn, number, target):
        for_peers(held, lambda k: remote(turn, k).wait_recv())
        keep_own(turn).wait()
        height = number * grid_x
        half = steps_of(iota((height, LANES), 1), size_yz, 2)
        keep = half == (iota((height, LANES), 0) & 1)
        matrix = jnp.concatenate([spread_mat[:height], spread_mat[rows : rows + height]], axis=0)
        for t in range(tiles):
            slots = arrived[turn, t * 2 * span_x : (t + 1) * 2 * span_x].reshape(tile_rows, LANES)
            both = dot(matrix, slots)
            target[:height, t * LANES : (t + 1) * LANES] = jnp.where(
                keep, both[:height], pltpu.roll(both[height:], size_yz, 1)
            )

    def at(ref, i, start=0):
        return ref[(start + i) * grid_x : (start + i + 1) * grid_x, :]

    def put(ref):
        def write(i, value):
            ref[i * grid_x : (i + 1) * grid_x, :] = value.astype(ref.dtype)

        return write

    def enter(values):
        return dot(values, enter_mat[...])

    def stacked(window, target):
        three = jnp.concatenate(
            [pltpu.roll(window, width, 1), window, pltpu.roll(window, LANES - width, 1)], axis=0
        )
        target[...] = dot(pick_mat[...], three.astype(jnp.bfloat16)).astype(jnp.bfloat16)

    def conv(weights, outs, source, unit, first, count, emit):
        matrix = weights[...]
        for p in range(first, first + count, 2):
            columns = jnp.concatenate(
                [source[(p - 1 + q) * unit : (p + 2 + q) * unit, :] for q in (0, 1)], axis=1
            )
            product = dot(matrix, columns)
            for q in (0, 1):
                part = product[:, q * LANES : (q + 1) * LANES]
                emit(
                    p + q,
                    pltpu.roll(part[:outs], 1, 1)
                    + part[outs : 2 * outs]
                    + pltpu.roll(part[2 * outs : 3 * outs], LANES - 1, 1),
                )

    def store_stack(target, p, value):
        base = p * 3 * hidden
        for c, turned in enumerate((width, 0, LANES - width)):
            moved = pltpu.roll(value, turned, 1) if turned else value
            target[base + c * hidden : base + (c + 1) * hidden, :] = moved.astype(jnp.bfloat16)

    def middle(source, p):
        return source[(3 * p + 1) * hidden : (3 * p + 2) * hidden, :].astype(F32)

    def store_error(target, p, value):
        if not RIM <= p < RIM + size_x:
            return
        kept = value * mine[:1]
        for b, turned in enumerate((LANES - 1, 0, 1)):
            moved = pltpu.roll(kept, turned, 1) if turned else kept
            target[
                b * hidden : (b + 1) * hidden, (p - RIM) * LANES : (p - RIM + 1) * LANES
            ] = moved.astype(jnp.bfloat16)

    def forward(zx, z1, z2, margin, turn):
        conv(
            w1, hidden, zx, 16, RIM - margin + 1, size_x + 2 * margin - 2,
            lambda p, v: store_stack(z1, p, jnp.tanh(v) * inside(p)),
        )
        conv(
            w23.at[: 3 * hidden], hidden, z1, 3 * hidden, RIM - margin + 2, size_x + 2 * margin - 4,
            lambda p, v: store_stack(z2, p, jnp.tanh(v) * inside(p)),
        )
        leave(w23.at[3 * hidden : 3 * hidden + 32], z2, turn)

    def leave(weights, source, turn):
        kept = {}
        conv(
            weights, FIELD_ROWS, source, 3 * hidden, RIM, size_x, lambda p, v: kept.update({p - RIM: v}),
        )
        sides = [
            jnp.concatenate([kept[q + 2 * i] for i in range(size_x // 2)], axis=0) for q in (0, 1)
        ]
        both = jnp.concatenate(sides, axis=1).astype(jnp.bfloat16)
        block[turn] = dot(both, leave_mat[...]).astype(WIRE)
        send(turn)

    def backward(ref, zx, z1, z2, margin):
        window = enter(ref[...])
        stacked(window, zin)
        kept = window * mine[:1]
        three = jnp.concatenate(
            [pltpu.roll(kept, LANES - 1, 1), kept, pltpu.roll(kept, 1, 1)], axis=0
        )
        own = dot(
            pick_mat[RIM * 16 : (RIM + size_x) * 16, :], three.astype(jnp.bfloat16)
        ).astype(jnp.bfloat16)
        for p in range(size_x):
            e3s[:, p * LANES : (p + 1) * LANES] = own[p * 16 : (p + 1) * 16]
        span = margin - 2

        def second(p, v):
            slope = 1.0 - jnp.square(middle(z2, p))
            value = v * slope * inside(p)
            store_stack(ze2, p, value)
            store_error(e2s, p, value)

        def first(p, v):
            slope = 1.0 - jnp.square(middle(z1, p))
            value = v * slope * inside(p)
            if span > 1:
                store_stack(ze1, p, value)
            store_error(e1s, p, value)

        conv(w3t, hidden, zin, 16, RIM - span, size_x + 2 * span, second)
        conv(w2t, hidden, ze2, 3 * hidden, RIM - span + 1, size_x + 2 * span - 2, first)

    def gradients(zx, z1, z2, save):
        def wide(source, unit, low, high):
            return jnp.concatenate(
                [
                    source[(RIM + p - 1) * unit + low : (RIM + p - 1) * unit + high, :]
                    for p in range(size_x)
                ],
                axis=1,
            )

        deep = 9 * hidden
        zero = jnp.zeros((hidden, size_x * LANES), jnp.bfloat16)
        e2 = e2s[...]
        values = wide(z1, 3 * hidden, 0, deep)
        save(0, dot_nt(values, e2[: 2 * hidden]))
        last = e2[2 * hidden :]
        save(
            deep,
            dot_nt(values[: deep // 2], jnp.concatenate([last, zero], axis=0))
            + dot_nt(values[deep // 2 :], jnp.concatenate([zero, last], axis=0)),
        )
        start = deep + deep // 2
        e1 = e1s[...]
        values = wide(zx, 16, 0, 48)
        save(start, dot_nt(values, e1[: 2 * hidden]))
        start += 48
        tail = dot_nt(values, jnp.concatenate([e1[2 * hidden :], zero], axis=0))
        e3 = e3s[...]
        product = dot_nt(e3, wide(z2, 3 * hidden, 0, 8 * hidden))
        for j in range(8 * hidden // LANES):
            save(start, product[:, j * LANES : (j + 1) * LANES])
            start += 16
        late = dot_nt(
            e3, jnp.concatenate([zero, wide(z2, 3 * hidden, 8 * hidden, deep)], axis=0)
        )
        save(start, tail[:16] + late)
        save(start + 16, tail[16:])

    slope = slopes(
        origin_x * size_x, origin_y * size_yz, all_x, all_y * NZ, (grid_x, grid_yz)
    )
    def prepare():
        first_in = turned_kernels.shape[0] - 2 * LANES
        long = kernel_mid.shape[1]
        laid[hidden:, :] = jnp.zeros((laid.shape[0] - hidden, laid.shape[1]), F32)
        laid[:hidden, long // LANES * LANES :] = jnp.zeros(
            (hidden, laid.shape[1] - long // LANES * LANES), F32
        )
        laid[:hidden, :long] = kernel_mid[...].astype(F32)
        laid[hidden : hidden + channels, :long] = kernel_out[...].astype(F32)
        laid[:hidden, first_in : first_in + kernel_in.shape[1]] = kernel_in[...].astype(F32)
        for j in range(laid.shape[1] // LANES):
            part = slice(j * LANES, (j + 1) * LANES)
            turned_kernels[part, :] = jnp.transpose(laid[:, part])
        lane = iota((hidden, LANES), 1)
        low = lane < hidden

        def tap(a, b, c):
            return turned_kernels[pl.ds(a * 9 + b * 3 + c, hidden, stride=27), :]

        def tap_in(a, b, c):
            return turned_kernels[pl.ds(first_in + a * 9 + b * 3 + c, FIELD_ROWS, stride=27), :]

        def two(left, right):
            return jnp.where(
                iota(left.shape, 1) < hidden, left, pltpu.roll(right, hidden, 1)
            )

        empty = jnp.zeros((hidden, LANES), F32)
        for n in range(0, 9, 2):
            tops, ends = [], []
            for m in (n, n + 1):
                if m > 8:
                    tops.append(empty)
                    ends.append(empty)
                    continue
                taps = [tap(m // 3, b, m % 3) for b in range(3)]
                tops.append(two(taps[0], taps[1]))
                late = jnp.where(
                    lane < hidden + 8,
                    taps[0],
                    jnp.where(
                        lane < hidden + 16,
                        pltpu.roll(taps[1], 8, 1),
                        jnp.where(lane < hidden + 24, pltpu.roll(taps[2], 16, 1), 0.0),
                    ),
                )
                ends.append(jnp.where(low, taps[2], late))
            stop = min((n + 2) * hidden, 9 * hidden)
            for start, halves in ((0, tops), (LANES, ends)):
                value = jnp.transpose(jnp.concatenate(halves, axis=0)).astype(jnp.bfloat16)
                w23[start : start + LANES, n * hidden : stop] = value[:, : stop - n * hidden]
        for b in range(3):
            for n in range(0, 9, 2):
                ours = [tap(2 - m // 3, 2 - b, 2 - m % 3) for m in range(n, min(n + 2, 9))]
                value = two(*ours) if len(ours) == 2 else ours[0][:, :hidden]
                w2t[b * hidden : (b + 1) * hidden, n * hidden : n * hidden + value.shape[1]] = (
                    value.astype(jnp.bfloat16)
                )
            placed = None
            for m in range(9):
                value = jnp.where(low, 0.0, tap(2 - m // 3, 2 - b, 2 - m % 3))
                goal = (m // 3) * 16 + (m % 3) * channels
                value = pltpu.roll(value, (goal - hidden) % LANES, 1)
                placed = value if placed is None else placed + value
            w3t[b * hidden : (b + 1) * hidden, :] = placed[:, :48].astype(jnp.bfloat16)
        for n in range(0, 9, 2):
            bands = []
            for b in range(3):
                ours = [tap_in(2 - m // 3, 2 - b, 2 - m % 3) for m in range(n, min(n + 2, 9))]
                bands.append(two(*ours) if len(ours) == 2 else ours[0])
            bands.append(jnp.zeros((FIELD_ROWS, LANES), F32))
            stop = min((n + 2) * hidden, 9 * hidden)
            value = jnp.concatenate(bands, axis=0).astype(jnp.bfloat16)
            w1t[:, n * hidden : stop] = value[:, : stop - n * hidden]
        tops, ends = [], []
        for a in range(3):
            bands = []
            for b in range(3):
                band = None
                for c in range(3):
                    value = jnp.concatenate(
                        [tap_in(a, b, c), jnp.zeros((FIELD_ROWS, LANES), F32)], axis=0
                    )
                    value = pltpu.roll(value, c * channels, 0) if c else value
                    band = value if band is None else band + value
                bands.append(band)
            tops.append(two(bands[0], bands[1]))
            ends.append(bands[2])
        for start, parts in ((0, tops), (LANES, ends)):
            value = jnp.concatenate(parts + [jnp.zeros((LANES - 48, LANES), F32)], axis=0)
            value = jnp.transpose(value)[: min(LANES, 3 * hidden - start), :48]
            w1[start : start + value.shape[0], :] = value.astype(jnp.bfloat16)

    def finish_gradients():
        deep = 9 * hidden
        folded = out_table[deep : deep + deep // 2, :].astype(F32)
        behind = jnp.concatenate([folded, pltpu.roll(folded, hidden, 1)], axis=0)
        start = deep + deep // 2
        lead = out_table[start : start + 48, :]
        start += 48
        parts = []
        for j in range(8 * hidden // LANES):
            parts.append(out_table[start : start + 16, :])
            start += 16
        last = out_table[start : start + 48, :]
        parts.append(pltpu.roll(last[:16].astype(F32), hidden, 1).astype(WIRE)[:, :hidden])
        trail = jnp.concatenate(parts, axis=1)
        contract = (((0,), (0,)), ((), ()))
        low = iota((hidden, LANES), 1) < hidden
        for b in range(3):
            placed = lax.dot_general(
                trail, place_mat[b * 16 : (b + 1) * 16], contract, preferred_element_type=F32
            )
            for n in range(9):
                rows_of = slice(n * hidden, (n + 1) * hidden)
                if b == 2:
                    value = behind[rows_of]
                else:
                    value = out_table[rows_of, :].astype(F32)
                    value = pltpu.roll(value, hidden, 1) if b == 1 else value
                turned_kernels[pl.ds((n // 3) * 9 + b * 3 + n % 3, hidden, stride=27), :] = (
                    jnp.where(low, value, placed[rows_of])
                )
        long = grad_mid.shape[1]
        for start in range(0, long, LANES):
            size = min(LANES, long - start)
            value = jnp.transpose(turned_kernels[start : start + LANES, :])
            grad_mid[:, start : start + size] = value[:hidden, :size]
            grad_out[:, start : start + size] = value[hidden : hidden + channels, :size]
        named = [
            lax.dot_general(
                source, name_mat[b * 48 : (b + 1) * 48], contract, preferred_element_type=F32
            )
            for b, source in enumerate((lead, lead, last))
        ]
        value = named[0][:hidden] + named[1][hidden:] + named[2][:hidden]
        grad_in[...] = value[:, : grad_in.shape[1]]

    send(0)
    send(1)
    prepare()
    receive(0, channels, fields)
    stacked(enter(fields[...].astype(jnp.bfloat16)), zx0)
    forward(zx0, z1s0, z2s0, 3, 2)

    receive(1, channels + 2, flow)
    velocity, shear = at(flow, 0), at(flow, 1)
    error = xs
    retreat(
        [at(flow, i, 2) for i in range(channels)], velocity, shear, channels, slope,
        put(error), put(carried),
    )
    receive(2, channels, sources)
    advance(
        lambda i: at(fields, i), velocity, shear, lambda i: at(sources, i), channels, slope,
        put(fields),
    )
    stacked(enter(fields[...].astype(jnp.bfloat16)), zx1)
    forward(zx1, z1s1, z2s1, 4, 3)
    backward(error, zx1, z1s1, z2s1, 4)
    leave(w1t, ze1, 4)

    def save(start, value):
        table[start : start + value.shape[0], :] = value

    gradients(zx1, z1s1, z2s1, save)
    receive(3, channels, sources)
    advance(
        lambda i: at(fields, i), velocity, shear, lambda i: at(sources, i), channels, slope,
        put(fields),
    )
    slot = index_y - origin_y
    tile = lax.div(slot, 2)
    for i in range(channels):
        value = fields[i * grid_x : (i + 1) * grid_x, pl.ds(pl.multiple_of(tile * LANES, LANES), LANES)]
        value = jnp.where(lax.rem(slot, 2) == 0, value, pltpu.roll(value, size_yz, 1))
        value = pltpu.roll(value, lax.rem(grid_x - (index_x - origin_x) * size_x, grid_x), 0)
        out_state[i] = value[:size_x, :size_yz]
    receive(4, channels, sources)
    retreat(
        [at(carried, i) + at(sources, i) for i in range(channels)],
        velocity, shear, channels, slope, put(error), None,
    )
    backward(error, zx0, z1s0, z2s0, 3)

    def finish(start, value):
        wire[start : start + value.shape[0], :] = (
            table[start : start + value.shape[0], :] + value
        ).astype(WIRE)

    height = wire.shape[0]
    used = table.shape[0]
    if height > used:
        wire[used:, :] = jnp.zeros((height - used, LANES), WIRE)
    gradients(zx0, z1s0, z2s0, finish)

    pairs = total // 2
    chunk = height // total
    core = lax.rem(index_x, 2)
    pair = index_y * (count_x // 2) + lax.div(index_x, 2)

    def at_pair(place, side):
        return {
            "gx": lax.rem(place, count_x // 2) * 2 + side, "gy": lax.div(place, count_x // 2)
        }

    half = height // 2
    copy = pltpu.make_async_remote_copy(
        src_ref=wire.at[pl.ds(pl.multiple_of((1 - core) * half, 16), half)],
        dst_ref=from_core,
        send_sem=core_sems.at[0],
        recv_sem=core_sems.at[1],
        device_id=at_pair(pair, 1 - core),
        device_id_type=MESH,
    )
    copy.start()
    copy.wait()
    halved[...] = (
        wire[pl.ds(pl.multiple_of(core * half, 16), half), :].astype(F32)
        + from_core[...].astype(F32)
    ).astype(WIRE)

    def scatter(k):
        other = lax.rem(pair + k, pairs)
        return pltpu.make_async_remote_copy(
            src_ref=halved.at[pl.ds(pl.multiple_of(other * chunk, 16), chunk)],
            dst_ref=from_rest.at[k - 1],
            send_sem=rest_sems.at[0, k - 1],
            recv_sem=rest_sems.at[1, k - 1],
            device_id=at_pair(other, core),
            device_id_type=MESH,
        )

    for_peers(pairs, lambda k: scatter(k).start())
    for_peers(pairs, lambda k: scatter(k).wait_recv())
    summed = halved[pl.ds(pl.multiple_of(pair * chunk, 16), chunk), :].astype(F32)
    for k in range(pairs - 1):
        summed = summed + from_rest[k].astype(F32)
    spot = pl.ds(pl.multiple_of(core * half + pair * chunk, 16), chunk)
    out_table[spot, :] = summed.astype(WIRE)

    def gather(k):
        other = lax.rem(pair + k, pairs)
        return pltpu.make_async_remote_copy(
            src_ref=out_table.at[spot],
            dst_ref=out_table.at[spot],
            send_sem=rest_sems.at[2, k - 1],
            recv_sem=rest_sems.at[3, k - 1],
            device_id=at_pair(other, core),
            device_id_type=MESH,
        )

    for_peers(pairs, lambda k: gather(k).start())
    for_peers(pairs, lambda k: gather(k).wait_recv())
    side = pl.ds(pl.multiple_of(core * half, 16), half)
    copy = pltpu.make_async_remote_copy(
        src_ref=out_table.at[side],
        dst_ref=out_table.at[side],
        send_sem=core_sems.at[2],
        recv_sem=core_sems.at[3],
        device_id=at_pair(pair, 1 - core),
        device_id_type=MESH,
    )
    copy.start()
    copy.wait()
    finish_gradients()
    for_peers(pairs, lambda k: scatter(k).wait_send())
    for_peers(pairs, lambda k: gather(k).wait_send())
    for turn in range(5):
        for_peers(held, lambda k: remote(turn, k).wait_send())


def body(perturbation, mean_velocity, mean_shear, cotangent, kernel_in, kernel_mid, kernel_out):
    channels, size_x, size_yz = perturbation.shape
    hidden = kernel_in.shape[0]
    count_x, count_y = lax.axis_size("gx"), lax.axis_size("gy")
    total = count_x * count_y
    span_x, span_y = span_of(count_x, REACH_X)[0], span_of(count_y, REACH_Y)[0]
    held = span_x * span_y
    grid_x, grid_yz = span_x * size_x, span_y * size_yz
    planes = size_x + 2 * RIM
    used = 1024
    unit = total * 16
    height = -(-used // unit) * unit
    deep, wide = 3 * hidden, size_x * LANES
    taps = -(-kernel_mid.shape[1] // LANES) * LANES
    b16 = jnp.bfloat16
    vmem = pltpu.VMEM
    scratch = [
        vmem((5, BLOCK_ROWS, LANES), WIRE),
        vmem((5, held, BLOCK_ROWS, LANES), WIRE),
        vmem((channels * grid_x, grid_yz), F32),
        vmem((channels * grid_x, grid_yz), F32),
        vmem(((channels + 2) * grid_x, grid_yz), F32),
        vmem((channels * grid_x, grid_yz), F32),
        vmem((planes * 16, LANES), b16),
        vmem((planes * 16, LANES), b16),
        vmem((planes * deep, LANES), b16),
        vmem((planes * deep, LANES), b16),
        vmem((planes * deep, LANES), b16),
        vmem((planes * deep, LANES), b16),
        vmem((planes * 16, LANES), b16),
        vmem((planes * deep, LANES), b16),
        vmem((planes * deep, LANES), b16),
        vmem((deep, wide), b16),
        vmem((deep, wide), b16),
        vmem((16, wide), b16),
        vmem((channels * grid_x, grid_yz), b16),
        vmem((2, BLOCK_ROWS, LANES), F32),
        vmem((LANES, taps + 2 * LANES), F32),
        vmem((taps + 2 * LANES, LANES), F32),
        vmem((deep, 48), b16),
        vmem((2 * LANES, 3 * deep), b16),
        vmem((deep, 48), b16),
        vmem((deep, 3 * deep), b16),
        vmem((32, 3 * deep), b16),
        vmem((2 * FIELD_ROWS * grid_x, 2 * span_x * BLOCK_ROWS), b16),
        vmem((grid_yz, LANES), b16),
        vmem((planes * 16, 3 * channels * grid_x), b16),
        vmem((2 * LANES, LANES), b16),
        vmem((3 * 48, 2 * LANES), b16),
        vmem((3 * 16, LANES), b16),
        vmem((used, LANES), F32),
        vmem((height, LANES), WIRE),
        vmem((height // 2, LANES), WIRE),
        vmem((height // 2, LANES), WIRE),
        vmem((total // 2 - 1, height // total, LANES), WIRE),
        vmem((height, LANES), WIRE),
        pltpu.SemaphoreType.DMA((5, held - 1)),
        pltpu.SemaphoreType.DMA((5, held - 1)),
        pltpu.SemaphoreType.DMA((4,)),
        pltpu.SemaphoreType.DMA((4, total // 2 - 1)),
        pltpu.SemaphoreType.DMA((5,)),
    ]
    operands = (
        perturbation, mean_velocity, mean_shear, cotangent, kernel_in, kernel_mid, kernel_out,
    )
    results = (perturbation,) + operands[4:]
    return tuple(
        pl.pallas_call(
            functools.partial(whole_kernel, (count_x, count_y, channels, hidden, size_x, size_yz)),
            out_shape=[jax.ShapeDtypeStruct(r.shape, F32) for r in results],
            in_specs=[pl.BlockSpec(memory_space=pltpu.VMEM)] * len(operands),
            out_specs=[pl.BlockSpec(memory_space=pltpu.VMEM)] * len(results),
            scratch_shapes=scratch,
            compiler_params=pltpu.CompilerParams(
                collective_id=0, has_side_effects=True, vmem_limit_bytes=56 * 2**20
            ),
        )(*operands)
    )


def solution(mesh):
    return jax.shard_map(
        body,
        mesh=mesh,
        in_specs=(
            P(None, "gx", "gy"),
            P("gx", "gy"),
            P("gx", "gy"),
            P(None, "gx", "gy"),
            P(),
            P(),
            P(),
        ),
        out_specs=(P(None, "gx", "gy"), P(), P(), P()),
        check_vma=False,
    )
```

```python
import functools
import math

import jax
import jax.numpy as jnp
from jax import lax
from jax.experimental import pallas as pl
from jax.experimental.pallas import tpu as pltpu
from jax.sharding import PartitionSpec as P

NZ = 8
LANES = 128
FIELD_ROWS = 8
BLOCK_ROWS = 2 * FIELD_ROWS
RIM = 4
REACH_X = 5
REACH_Y = 3

TIME_STEP = 0.25
STENCIL_WEIGHTS = (0.75, -0.15, 1.0 / 60.0)
MESH = pl.DeviceIdType.MESH
WIRE = jnp.bfloat16
F32 = jnp.float32


def dot(a, b):
    return lax.dot_general(a, b, (((1,), (0,)), ((), ())), preferred_element_type=F32)


def dot_nt(a, b):
    return lax.dot_general(a, b, (((1,), (1,)), ((), ())), preferred_element_type=F32)


def iota(shape, axis):
    return lax.broadcasted_iota(jnp.int32, shape, axis)


def shifted_by(values, size):
    return lax.shift_right_logical(values, size.bit_length() - 1)


def steps_of(values, size, count):
    return sum((values >= size * n).astype(jnp.int32) for n in range(1, count))


def one_hot(condition):
    return jnp.where(condition, 1.0, 0.0).astype(jnp.bfloat16)


def span_of(count, reach):
    span = min(count, 2 * reach + 2)
    return span, span // 2


def slopes(origin_x, origin_yz, grid_x, grid_yz, shape):
    row = iota(shape, 0) + origin_x
    lane = iota(shape, 1) + origin_yz
    depth = lane & (NZ - 1)

    def moved(field, offset, axis):
        return pltpu.roll(field, (-offset) % field.shape[axis], axis)

    def edged(field, axis, position, unit):
        size = (grid_x, grid_yz)[axis]
        result = None
        for offset, weight in zip((1, 2, 3), STENCIL_WEIGHTS):
            step = offset * unit
            upper = jnp.where(position < size - step, moved(field, step, axis), 0.0)
            lower = jnp.where(position >= step, moved(field, -step, axis), 0.0)
            contrib = weight * (upper - lower)
            result = contrib if result is None else result + contrib
        return result

    def along_x(field):
        return edged(field, 0, row, 1)

    def along_y(field):
        return edged(field, 1, lane, NZ)

    def along_z(field):
        result = None
        for offset, weight in zip((1, 2, 3), STENCIL_WEIGHTS):
            upper = jnp.where(
                depth < NZ - offset, moved(field, offset, 1), moved(field, offset - NZ, 1)
            )
            lower = jnp.where(depth >= offset, moved(field, -offset, 1), moved(field, NZ - offset, 1))
            contrib = weight * (upper - lower)
            result = contrib if result is None else result + contrib
        return result

    return along_x, along_y, along_z


def advance(now, velocity, shear, source, channels, slope, write):
    fields = range(channels)
    dx, dy, dz = slope

    def rates(f):
        across = [dx(c) for c in f]
        divergence = across[1] + dy(f[2]) + dz(f[3])
        return (
            -velocity * across[0] - divergence,
            -velocity * across[1] - shear * f[2] - across[4],
            -velocity * across[2] - dy(f[4]),
            -velocity * across[3] - dz(f[4]),
            -velocity * across[4] - divergence,
        )

    rate = rates([now(i) for i in fields])
    one = [now(i) + TIME_STEP * (rate[i] + source(i)) for i in fields]
    rate = rates(one)
    two = [0.75 * now(i) + 0.25 * (one[i] + TIME_STEP * (rate[i] + source(i))) for i in fields]
    rate = rates(two)
    for i in fields:
        write(i, 1.0 / 3.0 * now(i) + 2.0 / 3.0 * (two[i] + TIME_STEP * (rate[i] + source(i))))


def retreat(last, velocity, shear, channels, slope, write_error, write_carried):
    fields = range(channels)
    dx, dy, dz = slope

    def rates(g):
        acoustic = g[0] + g[4]
        return (
            dx(velocity * g[0]),
            dx(velocity * g[1] + acoustic),
            dx(velocity * g[2]) - shear * g[1] + dy(acoustic),
            dx(velocity * g[3]) + dz(acoustic),
            dx(velocity * g[4] + g[1]) + dy(g[2]) + dz(g[3]),
        )

    rate = rates(last)
    second = [2.0 / 3.0 * last[i] + 2.0 / 3.0 * TIME_STEP * rate[i] for i in fields]
    rate = rates(second)
    first = [0.25 * second[i] + 0.25 * TIME_STEP * rate[i] for i in fields]
    for i in fields:
        write_error(i, TIME_STEP * (2.0 / 3.0 * last[i] + 0.25 * second[i] + first[i]))
    if write_carried is None:
        return
    rate = rates(first)
    for i in fields:
        write_carried(i, 1.0 / 3.0 * last[i] + 0.75 * second[i] + first[i] + TIME_STEP * rate[i])


def for_peers(total, body):
    lax.fori_loop(1, total, lambda k, c: (body(k), c)[1], 0, unroll=total <= 32)


def whole_kernel(
    plan, state_from, velocity_from, shear_from, cotangent_from, in_from, mid_from, out_from,
    out_state, out_table,
    state_ref, velocity_ref, shear_ref, cotangent_ref, kernel_in, kernel_mid, kernel_out,
    block, arrived, fields, sources, flow, carried, zx0, zx1, z1s0, z1s1, z2s0, z2s1, zin, ze2, ze1,
    e1s, e2s, e3s, xs, packs, laid, turned_kernels, w1, w23, w3t, w2t, w1t, spread_mat, enter_mat, pick_mat, leave_mat, table, wire, from_core, halved, from_rest,
    send_sems, recv_sems, core_sems, rest_sems, own_sems, load_sems,
):
    count_x, count_y, channels, hidden, size_x, size_yz = plan
    total = count_x * count_y
    span_x, lead_x = span_of(count_x, REACH_X)
    span_y, lead_y = span_of(count_y, REACH_Y)
    held = span_x * span_y
    all_x, all_y = count_x * size_x, count_y * size_yz // NZ
    grid_x, grid_yz = span_x * size_x, span_y * size_yz
    size_y = size_yz // NZ
    width = size_y + 2 * RIM
    planes = size_x + 2 * RIM
    index_x, index_y = lax.axis_index("gx"), lax.axis_index("gy")
    me = index_y * count_x + index_x
    origin_x = 0 if span_x == count_x else index_x - lead_x
    origin_y = 0 if span_y == count_y else index_y - lead_y
    tiles = grid_yz // LANES
    tile_rows = 2 * span_x * BLOCK_ROWS
    flat = channels * grid_x

    def device(place):
        return {"gx": lax.rem(place, count_x), "gy": lax.div(place, count_x)}

    loads = [
        pltpu.make_async_copy(source, target, load_sems.at[n])
        for n, (source, target) in enumerate(
            (
                (state_from, state_ref),
                (velocity_from, velocity_ref),
                (shear_from, shear_ref),
                (cotangent_from, cotangent_ref),
                (in_from, kernel_in),
                (mid_from, kernel_mid),
                (out_from, kernel_out),
            )
        )
    ]
    for load in loads:
        load.start()
    barrier = pltpu.get_barrier_semaphore()
    for_peers(
        total,
        lambda k: pl.semaphore_signal(
            barrier, inc=1, device_id=device(lax.rem(me + k, total)), device_id_type=MESH
        ),
    )

    rows = FIELD_ROWS * grid_x
    r, k = iota((rows, tile_rows), 0), iota((rows, tile_rows), 1)
    field = steps_of(r, grid_x, FIELD_ROWS)
    at_x = r - field * grid_x
    part = steps_of(k, tile_rows // 2, 2)
    rest = k - part * (tile_rows // 2)
    owner = shifted_by(rest, BLOCK_ROWS)
    inner = rest & (BLOCK_ROWS - 1)
    odd = at_x & 1
    row = (shifted_by(at_x, 2) & 1) * FIELD_ROWS + field
    same = (owner == shifted_by(at_x, size_x)) & (inner == row)
    spread_mat[:rows] = one_hot(same & (part == odd))
    spread_mat[rows:] = one_hot(same & (part != odd))
    r, k = iota((grid_yz, LANES), 0), iota((grid_yz, LANES), 1)
    enter_mat[...] = one_hot(
        ((r & (NZ - 1)) == shifted_by(k, width))
        & (shifted_by(r, NZ) + origin_y * size_y == index_y * size_y - RIM + (k & (width - 1)))
        & (shifted_by(r, NZ) + origin_y * size_y >= 0)
        & (shifted_by(r, NZ) + origin_y * size_y < all_y)
    )
    r, k = iota((planes * 16, 3 * flat), 0), iota((planes * 16, 3 * flat), 1)
    inner = r & 15
    side = steps_of(inner, channels, 3)
    part = steps_of(k, flat, 3)
    rest = k - part * flat
    field = steps_of(rest, grid_x, channels)
    pick_mat[...] = one_hot(
        (inner < 3 * channels)
        & (part == side)
        & (field == inner - channels * side)
        & (
            rest - field * grid_x + origin_x * size_x
            == index_x * size_x - RIM + shifted_by(r, 16)
        )
        & (rest - field * grid_x + origin_x * size_x >= 0)
        & (rest - field * grid_x + origin_x * size_x < all_x)
    )
    r, k = iota((2 * LANES, LANES), 0), iota((2 * LANES, LANES), 1)
    inner, lane = r & (LANES - 1), k & (size_yz - 1)
    leave_mat[...] = one_hot(
        (shifted_by(r, LANES) == steps_of(k, size_yz, 2))
        & (shifted_by(inner, width) == (lane & (NZ - 1)))
        & ((inner & (width - 1)) == shifted_by(lane, NZ) + RIM)
    )
    place = iota((8, LANES), 1) & (width - 1)
    at_y = place + (index_y * size_y - RIM)
    valid_y = jnp.where((at_y >= 0) & (at_y < all_y), 1.0, 0.0)
    mine = jnp.where((place >= RIM) & (place < RIM + size_y), 1.0, 0.0)

    def inside(p):
        at = index_x * size_x - RIM + p
        scale = jnp.where((at >= 0) & (at < all_x), 1.0, 0.0).astype(F32)
        return (valid_y * scale)[:1]

    def pack(turn, rows_of):
        packs[...] = jnp.zeros(packs.shape, F32)
        for f, at_row in enumerate(rows_of):
            for x in range(size_x):
                spot = (x // 2) * FIELD_ROWS + f
                packs[x % 2, spot : spot + 1, :size_yz] = at_row(x)
        block[turn] = (packs[0] + pltpu.roll(packs[1], size_yz, 1)).astype(WIRE)

    for load in loads[:4]:
        load.wait()
    pack(0, [lambda x, f=f: state_ref[f, x : x + 1, :] for f in range(channels)])
    scale = 1.0 / math.sqrt(total * size_x * size_yz)
    pack(
        1,
        [lambda x: velocity_ref[x : x + 1, :], lambda x: shear_ref[x : x + 1, :]]
        + [lambda x, f=f: cotangent_ref[f, x : x + 1, :] * scale for f in range(channels)],
    )
    pl.semaphore_wait(barrier, total - 1)

    own_slot = (index_y - origin_y) * span_x + index_x - origin_x

    def remote(turn, k):
        place = lax.rem(lead_y * span_x + lead_x + k, held)
        shift_x, shift_y = lax.rem(place, span_x) - lead_x, lax.div(place, span_x) - lead_y
        slot_x = index_x if span_x == count_x else lead_x - shift_x
        slot_y = index_y if span_y == count_y else lead_y - shift_y
        return pltpu.make_async_remote_copy(
            src_ref=block.at[turn],
            dst_ref=arrived.at[turn, slot_y * span_x + slot_x],
            send_sem=send_sems.at[turn, k - 1],
            recv_sem=recv_sems.at[turn, k - 1],
            device_id={
                "gx": lax.rem(index_x + shift_x + count_x, count_x),
                "gy": lax.rem(index_y + shift_y + count_y, count_y),
            },
            device_id_type=MESH,
        )

    def keep_own(turn):
        return pltpu.make_async_copy(block.at[turn], arrived.at[turn, own_slot], own_sems.at[turn])

    def send(turn):
        for_peers(held, lambda k: remote(turn, k).start())
        keep_own(turn).start()

    def receive(turn, number, target):
        for_peers(held, lambda k: remote(turn, k).wait_recv())
        keep_own(turn).wait()
        height = number * grid_x
        half = steps_of(iota((height, LANES), 1), size_yz, 2)
        keep = half == (iota((height, LANES), 0) & 1)
        matrix = jnp.concatenate([spread_mat[:height], spread_mat[rows : rows + height]], axis=0)
        for t in range(tiles):
            slots = arrived[turn, t * 2 * span_x : (t + 1) * 2 * span_x].reshape(tile_rows, LANES)
            both = dot(matrix, slots)
            target[:height, t * LANES : (t + 1) * LANES] = jnp.where(
                keep, both[:height], pltpu.roll(both[height:], size_yz, 1)
            )

    def at(ref, i, start=0):
        return ref[(start + i) * grid_x : (start + i + 1) * grid_x, :]

    def put(ref):
        def write(i, value):
            ref[i * grid_x : (i + 1) * grid_x, :] = value.astype(ref.dtype)

        return write

    def enter(values):
        return dot(values, enter_mat[...])

    def stacked(window, target):
        three = jnp.concatenate(
            [pltpu.roll(window, width, 1), window, pltpu.roll(window, LANES - width, 1)], axis=0
        )
        target[...] = dot(pick_mat[...], three.astype(jnp.bfloat16)).astype(jnp.bfloat16)

    def conv(weights, outs, source, unit, first, count, emit):
        matrix = weights[...]
        for p in range(first, first + count, 2):
            columns = jnp.concatenate(
                [source[(p - 1 + q) * unit : (p + 2 + q) * unit, :] for q in (0, 1)], axis=1
            )
            product = dot(matrix, columns)
            for q in (0, 1):
                part = product[:, q * LANES : (q + 1) * LANES]
                emit(
                    p + q,
                    pltpu.roll(part[:outs], 1, 1)
                    + part[outs : 2 * outs]
                    + pltpu.roll(part[2 * outs : 3 * outs], LANES - 1, 1),
                )

    def store_stack(target, p, value):
        base = p * 3 * hidden
        for c, turned in enumerate((width, 0, LANES - width)):
            moved = pltpu.roll(value, turned, 1) if turned else value
            target[base + c * hidden : base + (c + 1) * hidden, :] = moved.astype(jnp.bfloat16)

    def middle(source, p):
        return source[(3 * p + 1) * hidden : (3 * p + 2) * hidden, :].astype(F32)

    def store_error(target, p, value):
        if not RIM <= p < RIM + size_x:
            return
        kept = value * mine[:1]
        for b, turned in enumerate((LANES - 1, 0, 1)):
            moved = pltpu.roll(kept, turned, 1) if turned else kept
            target[
                b * hidden : (b + 1) * hidden, (p - RIM) * LANES : (p - RIM + 1) * LANES
            ] = moved.astype(jnp.bfloat16)

    def forward(zx, z1, z2, margin, turn):
        conv(
            w1, hidden, zx, 16, RIM - margin + 1, size_x + 2 * margin - 2,
            lambda p, v: store_stack(z1, p, jnp.tanh(v) * inside(p)),
        )
        conv(
            w23.at[: 3 * hidden], hidden, z1, 3 * hidden, RIM - margin + 2, size_x + 2 * margin - 4,
            lambda p, v: store_stack(z2, p, jnp.tanh(v) * inside(p)),
        )
        leave(w23.at[3 * hidden : 3 * hidden + 32], z2, turn)

    def leave(weights, source, turn):
        kept = {}
        conv(
            weights, FIELD_ROWS, source, 3 * hidden, RIM, size_x, lambda p, v: kept.update({p - RIM: v}),
        )
        sides = [
            jnp.concatenate([kept[q + 2 * i] for i in range(size_x // 2)], axis=0) for q in (0, 1)
        ]
        both = jnp.concatenate(sides, axis=1).astype(jnp.bfloat16)
        block[turn] = dot(both, leave_mat[...]).astype(WIRE)
        send(turn)

    def backward(ref, zx, z1, z2, margin):
        window = enter(ref[...])
        stacked(window, zin)
        kept = window * mine[:1]
        three = jnp.concatenate(
            [pltpu.roll(kept, LANES - 1, 1), kept, pltpu.roll(kept, 1, 1)], axis=0
        )
        own = dot(
            pick_mat[RIM * 16 : (RIM + size_x) * 16, :], three.astype(jnp.bfloat16)
        ).astype(jnp.bfloat16)
        for p in range(size_x):
            e3s[:, p * LANES : (p + 1) * LANES] = own[p * 16 : (p + 1) * 16]
        span = margin - 2

        def second(p, v):
            slope = 1.0 - jnp.square(middle(z2, p))
            value = v * slope * inside(p)
            store_stack(ze2, p, value)
            store_error(e2s, p, value)

        def first(p, v):
            slope = 1.0 - jnp.square(middle(z1, p))
            value = v * slope * inside(p)
            if span > 1:
                store_stack(ze1, p, value)
            store_error(e1s, p, value)

        conv(w3t, hidden, zin, 16, RIM - span, size_x + 2 * span, second)
        conv(w2t, hidden, ze2, 3 * hidden, RIM - span + 1, size_x + 2 * span - 2, first)

    def gradients(zx, z1, z2, save):
        def wide(source, unit, low, high):
            return jnp.concatenate(
                [
                    source[(RIM + p - 1) * unit + low : (RIM + p - 1) * unit + high, :]
                    for p in range(size_x)
                ],
                axis=1,
            )

        deep = 9 * hidden
        zero = jnp.zeros((hidden, size_x * LANES), jnp.bfloat16)
        e2 = e2s[...]
        values = wide(z1, 3 * hidden, 0, deep)
        save(0, dot_nt(values, e2[: 2 * hidden]))
        last = e2[2 * hidden :]
        save(
            deep,
            dot_nt(values[: deep // 2], jnp.concatenate([last, zero], axis=0))
            + dot_nt(values[deep // 2 :], jnp.concatenate([zero, last], axis=0)),
        )
        start = deep + deep // 2
        e1 = e1s[...]
        values = wide(zx, 16, 0, 48)
        save(start, dot_nt(values, e1[: 2 * hidden]))
        start += 48
        tail = dot_nt(values, jnp.concatenate([e1[2 * hidden :], zero], axis=0))
        e3 = e3s[...]
        product = dot_nt(e3, wide(z2, 3 * hidden, 0, 8 * hidden))
        for j in range(8 * hidden // LANES):
            save(start, product[:, j * LANES : (j + 1) * LANES])
            start += 16
        late = dot_nt(
            e3, jnp.concatenate([zero, wide(z2, 3 * hidden, 8 * hidden, deep)], axis=0)
        )
        save(start, tail[:16] + late)
        save(start + 16, tail[16:])

    slope = slopes(
        origin_x * size_x, origin_y * size_yz, all_x, all_y * NZ, (grid_x, grid_yz)
    )
    def prepare():
        first_in = turned_kernels.shape[0] - 2 * LANES
        long = kernel_mid.shape[1]
        laid[hidden:, :] = jnp.zeros((laid.shape[0] - hidden, laid.shape[1]), F32)
        laid[:hidden, long // LANES * LANES :] = jnp.zeros(
            (hidden, laid.shape[1] - long // LANES * LANES), F32
        )
        laid[:hidden, :long] = kernel_mid[...].astype(F32)
        laid[hidden : hidden + channels, :long] = kernel_out[...].astype(F32)
        laid[:hidden, first_in : first_in + kernel_in.shape[1]] = kernel_in[...].astype(F32)
        for j in range(laid.shape[1] // LANES):
            part = slice(j * LANES, (j + 1) * LANES)
            turned_kernels[part, :] = jnp.transpose(laid[:, part])
        lane = iota((hidden, LANES), 1)
        low = lane < hidden

        def tap(a, b, c):
            return turned_kernels[pl.ds(a * 9 + b * 3 + c, hidden, stride=27), :]

        def tap_in(a, b, c):
            return turned_kernels[pl.ds(first_in + a * 9 + b * 3 + c, FIELD_ROWS, stride=27), :]

        def two(left, right):
            return jnp.where(
                iota(left.shape, 1) < hidden, left, pltpu.roll(right, hidden, 1)
            )

        empty = jnp.zeros((hidden, LANES), F32)
        for n in range(0, 9, 2):
            tops, ends = [], []
            for m in (n, n + 1):
                if m > 8:
                    tops.append(empty)
                    ends.append(empty)
                    continue
                taps = [tap(m // 3, b, m % 3) for b in range(3)]
                tops.append(two(taps[0], taps[1]))
                late = jnp.where(
                    lane < hidden + 8,
                    taps[0],
                    jnp.where(
                        lane < hidden + 16,
                        pltpu.roll(taps[1], 8, 1),
                        jnp.where(lane < hidden + 24, pltpu.roll(taps[2], 16, 1), 0.0),
                    ),
                )
                ends.append(jnp.where(low, taps[2], late))
            stop = min((n + 2) * hidden, 9 * hidden)
            for start, halves in ((0, tops), (LANES, ends)):
                value = jnp.transpose(jnp.concatenate(halves, axis=0)).astype(jnp.bfloat16)
                w23[start : start + LANES, n * hidden : stop] = value[:, : stop - n * hidden]
        for b in range(3):
            for n in range(0, 9, 2):
                ours = [tap(2 - m // 3, 2 - b, 2 - m % 3) for m in range(n, min(n + 2, 9))]
                value = two(*ours) if len(ours) == 2 else ours[0][:, :hidden]
                w2t[b * hidden : (b + 1) * hidden, n * hidden : n * hidden + value.shape[1]] = (
                    value.astype(jnp.bfloat16)
                )
            placed = None
            for m in range(9):
                value = jnp.where(low, 0.0, tap(2 - m // 3, 2 - b, 2 - m % 3))
                goal = (m // 3) * 16 + (m % 3) * channels
                value = pltpu.roll(value, (goal - hidden) % LANES, 1)
                placed = value if placed is None else placed + value
            w3t[b * hidden : (b + 1) * hidden, :] = placed[:, :48].astype(jnp.bfloat16)
        for n in range(0, 9, 2):
            bands = []
            for b in range(3):
                ours = [tap_in(2 - m // 3, 2 - b, 2 - m % 3) for m in range(n, min(n + 2, 9))]
                bands.append(two(*ours) if len(ours) == 2 else ours[0])
            bands.append(jnp.zeros((FIELD_ROWS, LANES), F32))
            stop = min((n + 2) * hidden, 9 * hidden)
            value = jnp.concatenate(bands, axis=0).astype(jnp.bfloat16)
            w1t[:, n * hidden : stop] = value[:, : stop - n * hidden]
        tops, ends = [], []
        for a in range(3):
            bands = []
            for b in range(3):
                band = None
                for c in range(3):
                    value = jnp.concatenate(
                        [tap_in(a, b, c), jnp.zeros((FIELD_ROWS, LANES), F32)], axis=0
                    )
                    value = pltpu.roll(value, c * channels, 0) if c else value
                    band = value if band is None else band + value
                bands.append(band)
            tops.append(two(bands[0], bands[1]))
            ends.append(bands[2])
        for start, parts in ((0, tops), (LANES, ends)):
            value = jnp.concatenate(parts + [jnp.zeros((LANES - 48, LANES), F32)], axis=0)
            value = jnp.transpose(value)[: min(LANES, 3 * hidden - start), :48]
            w1[start : start + value.shape[0], :] = value.astype(jnp.bfloat16)

    send(0)
    send(1)
    for load in loads[4:]:
        load.wait()
    prepare()
    receive(0, channels, fields)
    stacked(enter(fields[...].astype(jnp.bfloat16)), zx0)
    forward(zx0, z1s0, z2s0, 3, 2)

    receive(1, channels + 2, flow)
    velocity, shear = at(flow, 0), at(flow, 1)
    error = xs
    retreat(
        [at(flow, i, 2) for i in range(channels)], velocity, shear, channels, slope,
        put(error), put(carried),
    )
    receive(2, channels, sources)
    advance(
        lambda i: at(fields, i), velocity, shear, lambda i: at(sources, i), channels, slope,
        put(fields),
    )
    stacked(enter(fields[...].astype(jnp.bfloat16)), zx1)
    forward(zx1, z1s1, z2s1, 4, 3)
    backward(error, zx1, z1s1, z2s1, 4)
    leave(w1t, ze1, 4)

    def save(start, value):
        table[start : start + value.shape[0], :] = value

    gradients(zx1, z1s1, z2s1, save)
    receive(3, channels, sources)
    advance(
        lambda i: at(fields, i), velocity, shear, lambda i: at(sources, i), channels, slope,
        put(fields),
    )
    slot = index_y - origin_y
    tile = lax.div(slot, 2)
    for i in range(channels):
        value = fields[i * grid_x : (i + 1) * grid_x, pl.ds(pl.multiple_of(tile * LANES, LANES), LANES)]
        value = jnp.where(lax.rem(slot, 2) == 0, value, pltpu.roll(value, size_yz, 1))
        value = pltpu.roll(value, lax.rem(grid_x - (index_x - origin_x) * size_x, grid_x), 0)
        out_state[i] = value[:size_x, :size_yz]
    receive(4, channels, sources)
    retreat(
        [at(carried, i) + at(sources, i) for i in range(channels)],
        velocity, shear, channels, slope, put(error), None,
    )
    backward(error, zx0, z1s0, z2s0, 3)

    def finish(start, value):
        wire[start : start + value.shape[0], :] = (
            table[start : start + value.shape[0], :] + value
        ).astype(WIRE)

    height = wire.shape[0]
    used = table.shape[0]
    if height > used:
        wire[used:, :] = jnp.zeros((height - used, LANES), WIRE)
    gradients(zx0, z1s0, z2s0, finish)

    pairs = total // 2
    chunk = height // total
    core = lax.rem(index_x, 2)
    pair = index_y * (count_x // 2) + lax.div(index_x, 2)

    def at_pair(place, side):
        return {
            "gx": lax.rem(place, count_x // 2) * 2 + side, "gy": lax.div(place, count_x // 2)
        }

    half = height // 2
    copy = pltpu.make_async_remote_copy(
        src_ref=wire.at[pl.ds(pl.multiple_of((1 - core) * half, 16), half)],
        dst_ref=from_core,
        send_sem=core_sems.at[0],
        recv_sem=core_sems.at[1],
        device_id=at_pair(pair, 1 - core),
        device_id_type=MESH,
    )
    copy.start()
    copy.wait()
    halved[...] = (
        wire[pl.ds(pl.multiple_of(core * half, 16), half), :].astype(F32)
        + from_core[...].astype(F32)
    ).astype(WIRE)

    def scatter(k):
        other = lax.rem(pair + k, pairs)
        return pltpu.make_async_remote_copy(
            src_ref=halved.at[pl.ds(pl.multiple_of(other * chunk, 16), chunk)],
            dst_ref=from_rest.at[k - 1],
            send_sem=rest_sems.at[0, k - 1],
            recv_sem=rest_sems.at[1, k - 1],
            device_id=at_pair(other, core),
            device_id_type=MESH,
        )

    for_peers(pairs, lambda k: scatter(k).start())
    for_peers(pairs, lambda k: scatter(k).wait_recv())
    summed = halved[pl.ds(pl.multiple_of(pair * chunk, 16), chunk), :].astype(F32)
    for k in range(pairs - 1):
        summed = summed + from_rest[k].astype(F32)
    spot = pl.ds(pl.multiple_of(core * half + pair * chunk, 16), chunk)
    out_table[spot, :] = summed.astype(WIRE)

    def gather(k):
        other = lax.rem(pair + k, pairs)
        return pltpu.make_async_remote_copy(
            src_ref=out_table.at[spot],
            dst_ref=out_table.at[spot],
            send_sem=rest_sems.at[2, k - 1],
            recv_sem=rest_sems.at[3, k - 1],
            device_id=at_pair(other, core),
            device_id_type=MESH,
        )

    for_peers(pairs, lambda k: gather(k).start())
    for_peers(pairs, lambda k: gather(k).wait_recv())
    side = pl.ds(pl.multiple_of(core * half, 16), half)
    copy = pltpu.make_async_remote_copy(
        src_ref=out_table.at[side],
        dst_ref=out_table.at[side],
        send_sem=core_sems.at[2],
        recv_sem=core_sems.at[3],
        device_id=at_pair(pair, 1 - core),
        device_id_type=MESH,
    )
    copy.start()
    copy.wait()
    for_peers(pairs, lambda k: scatter(k).wait_send())
    for_peers(pairs, lambda k: gather(k).wait_send())
    for turn in range(5):
        for_peers(held, lambda k: remote(turn, k).wait_send())


def unpack_kernel(
    plan, state_ref, table_ref, out_state, grad_in, grad_mid, grad_out, name_mat, place_mat, turned
):
    channels, hidden = plan
    out_state[...] = state_ref[...]
    r, k = iota((48, 256), 0), iota((48, 256), 1)
    inner = r & 15
    side = steps_of(inner, channels, 3)
    for b in range(3):
        goal = (inner - channels * side) * 27 + shifted_by(r, 16) * 9 + b * 3 + side
        name_mat[b * 48 : (b + 1) * 48] = one_hot((inner < 3 * channels) & (goal == k))
    r, k = iota((16, LANES), 0), iota((16, LANES), 1)
    for b in range(3):
        place_mat[b * 16 : (b + 1) * 16] = one_hot(
            (r >= b * channels) & (r < (b + 1) * channels) & (k == r - b * channels + hidden)
        )

    deep = 9 * hidden
    folded = table_ref[deep : deep + deep // 2, :].astype(F32)
    behind = jnp.concatenate([folded, pltpu.roll(folded, hidden, 1)], axis=0)
    start = deep + deep // 2
    lead = table_ref[start : start + 48, :]
    start += 48
    parts = []
    for j in range(8 * hidden // LANES):
        parts.append(table_ref[start : start + 16, :])
        start += 16
    last = table_ref[start : start + 48, :]
    parts.append(pltpu.roll(last[:16].astype(F32), hidden, 1).astype(WIRE)[:, :hidden])
    trail = jnp.concatenate(parts, axis=1)
    contract = (((0,), (0,)), ((), ()))
    low = iota((hidden, LANES), 1) < hidden
    for b in range(3):
        placed = lax.dot_general(
            trail, place_mat[b * 16 : (b + 1) * 16], contract, preferred_element_type=F32
        )
        for n in range(9):
            rows_of = slice(n * hidden, (n + 1) * hidden)
            if b == 2:
                value = behind[rows_of]
            else:
                value = table_ref[rows_of, :].astype(F32)
                value = pltpu.roll(value, hidden, 1) if b == 1 else value
            turned[pl.ds((n // 3) * 9 + b * 3 + n % 3, hidden, stride=27), :] = (
                jnp.where(low, value, placed[rows_of])
            )
    long = grad_mid.shape[1]
    for start in range(0, long, LANES):
        size = min(LANES, long - start)
        value = jnp.transpose(turned[start : start + LANES, :])
        grad_mid[:, start : start + size] = value[:hidden, :size]
        grad_out[:, start : start + size] = value[hidden : hidden + channels, :size]
    named = [
        lax.dot_general(
            source, name_mat[b * 48 : (b + 1) * 48], contract, preferred_element_type=F32
        )
        for b, source in enumerate((lead, lead, last))
    ]
    value = named[0][:hidden] + named[1][hidden:] + named[2][:hidden]
    grad_in[...] = value[:, : grad_in.shape[1]]


def body(perturbation, mean_velocity, mean_shear, cotangent, kernel_in, kernel_mid, kernel_out):
    channels, size_x, size_yz = perturbation.shape
    hidden = kernel_in.shape[0]
    count_x, count_y = lax.axis_size("gx"), lax.axis_size("gy")
    total = count_x * count_y
    span_x, span_y = span_of(count_x, REACH_X)[0], span_of(count_y, REACH_Y)[0]
    held = span_x * span_y
    grid_x, grid_yz = span_x * size_x, span_y * size_yz
    planes = size_x + 2 * RIM
    operands = (
        perturbation, mean_velocity, mean_shear, cotangent, kernel_in, kernel_mid, kernel_out,
    )
    results = (perturbation,) + operands[4:]
    used = 1024
    unit = total * 16
    height = -(-used // unit) * unit
    deep, wide = 3 * hidden, size_x * LANES
    taps = -(-kernel_mid.shape[1] // LANES) * LANES
    b16 = jnp.bfloat16
    vmem = pltpu.VMEM
    scratch = [vmem(a.shape, a.dtype) for a in operands] + [
        vmem((5, BLOCK_ROWS, LANES), WIRE),
        vmem((5, held, BLOCK_ROWS, LANES), WIRE),
        vmem((channels * grid_x, grid_yz), F32),
        vmem((channels * grid_x, grid_yz), F32),
        vmem(((channels + 2) * grid_x, grid_yz), F32),
        vmem((channels * grid_x, grid_yz), F32),
        vmem((planes * 16, LANES), b16),
        vmem((planes * 16, LANES), b16),
        vmem((planes * deep, LANES), b16),
        vmem((planes * deep, LANES), b16),
        vmem((planes * deep, LANES), b16),
        vmem((planes * deep, LANES), b16),
        vmem((planes * 16, LANES), b16),
        vmem((planes * deep, LANES), b16),
        vmem((planes * deep, LANES), b16),
        vmem((deep, wide), b16),
        vmem((deep, wide), b16),
        vmem((16, wide), b16),
        vmem((channels * grid_x, grid_yz), b16),
        vmem((2, BLOCK_ROWS, LANES), F32),
        vmem((LANES, taps + 2 * LANES), F32),
        vmem((taps + 2 * LANES, LANES), F32),
        vmem((deep, 48), b16),
        vmem((2 * LANES, 3 * deep), b16),
        vmem((deep, 48), b16),
        vmem((deep, 3 * deep), b16),
        vmem((32, 3 * deep), b16),
        vmem((2 * FIELD_ROWS * grid_x, 2 * span_x * BLOCK_ROWS), b16),
        vmem((grid_yz, LANES), b16),
        vmem((planes * 16, 3 * channels * grid_x), b16),
        vmem((2 * LANES, LANES), b16),
        vmem((used, LANES), F32),
        vmem((height, LANES), WIRE),
        vmem((height // 2, LANES), WIRE),
        vmem((height // 2, LANES), WIRE),
        vmem((total // 2 - 1, height // total, LANES), WIRE),
        pltpu.SemaphoreType.DMA((5, held - 1)),
        pltpu.SemaphoreType.DMA((5, held - 1)),
        pltpu.SemaphoreType.DMA((4,)),
        pltpu.SemaphoreType.DMA((4, total // 2 - 1)),
        pltpu.SemaphoreType.DMA((5,)),
        pltpu.SemaphoreType.DMA((len(operands),)),
    ]
    whole = pl.BlockSpec(memory_space=pltpu.VMEM)
    state, table = pl.pallas_call(
        functools.partial(whole_kernel, (count_x, count_y, channels, hidden, size_x, size_yz)),
        out_shape=[
            jax.ShapeDtypeStruct(perturbation.shape, F32),
            jax.ShapeDtypeStruct((height, LANES), WIRE),
        ],
        in_specs=[pl.BlockSpec(memory_space=pltpu.HBM)] * len(operands),
        out_specs=[whole] * 2,
        scratch_shapes=scratch,
        compiler_params=pltpu.CompilerParams(
            collective_id=0, has_side_effects=True, vmem_limit_bytes=56 * 2**20
        ),
    )(*operands)
    return tuple(
        pl.pallas_call(
            functools.partial(unpack_kernel, (channels, hidden)),
            out_shape=[jax.ShapeDtypeStruct(r.shape, F32) for r in results],
            in_specs=[whole] * 2,
            out_specs=[whole] * len(results),
            scratch_shapes=[
                vmem((3 * 48, 2 * LANES), b16),
                vmem((3 * 16, LANES), b16),
                vmem((taps, LANES), F32),
            ],
            compiler_params=pltpu.CompilerParams(vmem_limit_bytes=56 * 2**20),
        )(state, table)
    )


def solution(mesh):
    return jax.shard_map(
        body,
        mesh=mesh,
        in_specs=(
            P(None, "gx", "gy"),
            P("gx", "gy"),
            P("gx", "gy"),
            P(None, "gx", "gy"),
            P(),
            P(),
            P(),
        ),
        out_specs=(P(None, "gx", "gy"), P(), P(), P()),
        check_vma=False,
    )
```

```python
import functools
import math

import jax
import jax.numpy as jnp
from jax import lax
from jax.experimental import pallas as pl
from jax.experimental.pallas import tpu as pltpu
from jax.sharding import PartitionSpec as P

NZ = 8
LANES = 128
FIELD_ROWS = 8
BLOCK_ROWS = 2 * FIELD_ROWS
RIM = 4
REACH_X = 5
REACH_Y = 3
NEAR, FIRST_SOURCE, LAST_SOURCE = 3, 15, 8

TIME_STEP = 0.25
STENCIL_WEIGHTS = (0.75, -0.15, 1.0 / 60.0)
MESH = pl.DeviceIdType.MESH
WIRE = jnp.bfloat16
F32 = jnp.float32


def dot(a, b):
    return lax.dot_general(a, b, (((1,), (0,)), ((), ())), preferred_element_type=F32)


def dot_nt(a, b):
    return lax.dot_general(a, b, (((1,), (1,)), ((), ())), preferred_element_type=F32)


def iota(shape, axis):
    return lax.broadcasted_iota(jnp.int32, shape, axis)


def shifted_by(values, size):
    return lax.shift_right_logical(values, size.bit_length() - 1)


def steps_of(values, size, count):
    return sum((values >= size * n).astype(jnp.int32) for n in range(1, count))


def one_hot(condition):
    return jnp.where(condition, 1.0, 0.0).astype(jnp.bfloat16)


def span_of(count, reach):
    span = min(count, 2 * reach + 2)
    return span, span // 2


def slopes(origin_x, origin_yz, grid_x, grid_yz, shape):
    row = iota(shape, 0) + origin_x
    lane = iota(shape, 1) + origin_yz
    depth = lane & (NZ - 1)

    def moved(field, offset, axis):
        return pltpu.roll(field, (-offset) % field.shape[axis], axis)

    def edged(field, axis, position, unit):
        size = (grid_x, grid_yz)[axis]
        result = None
        for offset, weight in zip((1, 2, 3), STENCIL_WEIGHTS):
            step = offset * unit
            upper = jnp.where(position < size - step, moved(field, step, axis), 0.0)
            lower = jnp.where(position >= step, moved(field, -step, axis), 0.0)
            contrib = weight * (upper - lower)
            result = contrib if result is None else result + contrib
        return result

    def along_x(field):
        return edged(field, 0, row, 1)

    def along_y(field):
        return edged(field, 1, lane, NZ)

    def along_z(field):
        result = None
        for offset, weight in zip((1, 2, 3), STENCIL_WEIGHTS):
            upper = jnp.where(
                depth < NZ - offset, moved(field, offset, 1), moved(field, offset - NZ, 1)
            )
            lower = jnp.where(depth >= offset, moved(field, -offset, 1), moved(field, NZ - offset, 1))
            contrib = weight * (upper - lower)
            result = contrib if result is None else result + contrib
        return result

    return along_x, along_y, along_z


def advance(now, velocity, shear, source, channels, slope, write):
    fields = range(channels)
    dx, dy, dz = slope

    def rates(f):
        across = [dx(c) for c in f]
        divergence = across[1] + dy(f[2]) + dz(f[3])
        return (
            -velocity * across[0] - divergence,
            -velocity * across[1] - shear * f[2] - across[4],
            -velocity * across[2] - dy(f[4]),
            -velocity * across[3] - dz(f[4]),
            -velocity * across[4] - divergence,
        )

    rate = rates([now(i) for i in fields])
    one = [now(i) + TIME_STEP * (rate[i] + source(i)) for i in fields]
    rate = rates(one)
    two = [0.75 * now(i) + 0.25 * (one[i] + TIME_STEP * (rate[i] + source(i))) for i in fields]
    rate = rates(two)
    for i in fields:
        write(i, 1.0 / 3.0 * now(i) + 2.0 / 3.0 * (two[i] + TIME_STEP * (rate[i] + source(i))))


def retreat(last, velocity, shear, channels, slope, write_error, write_carried):
    fields = range(channels)
    dx, dy, dz = slope

    def rates(g):
        acoustic = g[0] + g[4]
        return (
            dx(velocity * g[0]),
            dx(velocity * g[1] + acoustic),
            dx(velocity * g[2]) - shear * g[1] + dy(acoustic),
            dx(velocity * g[3]) + dz(acoustic),
            dx(velocity * g[4] + g[1]) + dy(g[2]) + dz(g[3]),
        )

    rate = rates(last)
    second = [2.0 / 3.0 * last[i] + 2.0 / 3.0 * TIME_STEP * rate[i] for i in fields]
    rate = rates(second)
    first = [0.25 * second[i] + 0.25 * TIME_STEP * rate[i] for i in fields]
    for i in fields:
        write_error(i, TIME_STEP * (2.0 / 3.0 * last[i] + 0.25 * second[i] + first[i]))
    if write_carried is None:
        return
    rate = rates(first)
    for i in fields:
        write_carried(i, 1.0 / 3.0 * last[i] + 0.75 * second[i] + first[i] + TIME_STEP * rate[i])


def for_peers(total, body):
    lax.fori_loop(1, total, lambda k, c: (body(k), c)[1], 0, unroll=total <= 32)


def whole_kernel(
    plan, state_from, velocity_from, shear_from, cotangent_from, in_from, mid_from, out_from,
    out_state, out_table,
    state_ref, velocity_ref, shear_ref, cotangent_ref, kernel_in, kernel_mid, kernel_out,
    block, arrived, fields, sources, flow, carried, zx0, zx1, z1s0, z1s1, z2s0, z2s1, zin, ze2, ze1,
    e1s, e2s, e3s, xs, packs, laid, turned_kernels, w1, w23, w3t, w2t, w1t, spread_mat, enter_mat, pick_mat, leave_mat, table, wire, from_core, halved, from_rest,
    send_sems, recv_sems, core_sems, rest_sems, own_sems, load_sems,
):
    count_x, count_y, channels, hidden, size_x, size_yz = plan
    total = count_x * count_y
    span_x, lead_x = span_of(count_x, REACH_X)
    span_y, lead_y = span_of(count_y, REACH_Y)
    held = span_x * span_y
    all_x, all_y = count_x * size_x, count_y * size_yz // NZ
    grid_x, grid_yz = span_x * size_x, span_y * size_yz
    size_y = size_yz // NZ
    width = size_y + 2 * RIM
    planes = size_x + 2 * RIM
    index_x, index_y = lax.axis_index("gx"), lax.axis_index("gy")
    me = index_y * count_x + index_x
    origin_x = 0 if span_x == count_x else index_x - lead_x
    origin_y = 0 if span_y == count_y else index_y - lead_y
    tiles = grid_yz // LANES
    tile_rows = 2 * span_x * BLOCK_ROWS
    flat = channels * grid_x

    def device(place):
        return {"gx": lax.rem(place, count_x), "gy": lax.div(place, count_x)}

    loads = [
        pltpu.make_async_copy(source, target, load_sems.at[n])
        for n, (source, target) in enumerate(
            (
                (state_from, state_ref),
                (velocity_from, velocity_ref),
                (shear_from, shear_ref),
                (cotangent_from, cotangent_ref),
                (in_from, kernel_in),
                (mid_from, kernel_mid),
                (out_from, kernel_out),
            )
        )
    ]
    for load in loads:
        load.start()
    arrived[...] = jnp.zeros(arrived.shape, WIRE)
    barrier = pltpu.get_barrier_semaphore()
    for_peers(
        total,
        lambda k: pl.semaphore_signal(
            barrier, inc=1, device_id=device(lax.rem(me + k, total)), device_id_type=MESH
        ),
    )

    rows = FIELD_ROWS * grid_x
    r, k = iota((rows, tile_rows), 0), iota((rows, tile_rows), 1)
    field = steps_of(r, grid_x, FIELD_ROWS)
    at_x = r - field * grid_x
    part = steps_of(k, tile_rows // 2, 2)
    rest = k - part * (tile_rows // 2)
    owner = shifted_by(rest, BLOCK_ROWS)
    inner = rest & (BLOCK_ROWS - 1)
    odd = at_x & 1
    row = (shifted_by(at_x, 2) & 1) * FIELD_ROWS + field
    same = (owner == shifted_by(at_x, size_x)) & (inner == row)
    spread_mat[:rows] = one_hot(same & (part == odd))
    spread_mat[rows:] = one_hot(same & (part != odd))
    r, k = iota((grid_yz, LANES), 0), iota((grid_yz, LANES), 1)
    enter_mat[...] = one_hot(
        ((r & (NZ - 1)) == shifted_by(k, width))
        & (shifted_by(r, NZ) + origin_y * size_y == index_y * size_y - RIM + (k & (width - 1)))
        & (shifted_by(r, NZ) + origin_y * size_y >= 0)
        & (shifted_by(r, NZ) + origin_y * size_y < all_y)
    )
    r, k = iota((planes * 16, 3 * flat), 0), iota((planes * 16, 3 * flat), 1)
    inner = r & 15
    side = steps_of(inner, channels, 3)
    part = steps_of(k, flat, 3)
    rest = k - part * flat
    field = steps_of(rest, grid_x, channels)
    pick_mat[...] = one_hot(
        (inner < 3 * channels)
        & (part == side)
        & (field == inner - channels * side)
        & (
            rest - field * grid_x + origin_x * size_x
            == index_x * size_x - RIM + shifted_by(r, 16)
        )
        & (rest - field * grid_x + origin_x * size_x >= 0)
        & (rest - field * grid_x + origin_x * size_x < all_x)
    )
    r, k = iota((2 * LANES, LANES), 0), iota((2 * LANES, LANES), 1)
    inner, lane = r & (LANES - 1), k & (size_yz - 1)
    leave_mat[...] = one_hot(
        (shifted_by(r, LANES) == steps_of(k, size_yz, 2))
        & (shifted_by(inner, width) == (lane & (NZ - 1)))
        & ((inner & (width - 1)) == shifted_by(lane, NZ) + RIM)
    )
    place = iota((8, LANES), 1) & (width - 1)
    at_y = place + (index_y * size_y - RIM)
    valid_y = jnp.where((at_y >= 0) & (at_y < all_y), 1.0, 0.0)
    mine = jnp.where((place >= RIM) & (place < RIM + size_y), 1.0, 0.0)

    def inside(p):
        at = index_x * size_x - RIM + p
        scale = jnp.where((at >= 0) & (at < all_x), 1.0, 0.0).astype(F32)
        return (valid_y * scale)[:1]

    def pack(turn, rows_of):
        packs[...] = jnp.zeros(packs.shape, F32)
        for f, at_row in enumerate(rows_of):
            for x in range(size_x):
                spot = (x // 2) * FIELD_ROWS + f
                packs[x % 2, spot : spot + 1, :size_yz] = at_row(x)
        block[turn] = (packs[0] + pltpu.roll(packs[1], size_yz, 1)).astype(WIRE)

    for load in loads[:4]:
        load.wait()
    pack(0, [lambda x, f=f: state_ref[f, x : x + 1, :] for f in range(channels)])
    scale = 1.0 / math.sqrt(total * size_x * size_yz)
    pack(
        1,
        [lambda x: velocity_ref[x : x + 1, :], lambda x: shear_ref[x : x + 1, :]]
        + [lambda x, f=f: cotangent_ref[f, x : x + 1, :] * scale for f in range(channels)],
    )
    pl.semaphore_wait(barrier, total - 1)

    own_slot = (index_y - origin_y) * span_x + index_x - origin_x

    def around(cells):
        reach_x, reach_y = -(-cells // size_x), -(-cells // size_y)
        return [
            (x, y)
            for y in range(-lead_y, span_y - lead_y)
            for x in range(-lead_x, span_x - lead_x)
            if abs(x) <= reach_x and abs(y) <= reach_y and (x or y)
        ]

    everyone = around(max(all_x, all_y))
    near = around(NEAR)
    shifts = [
        [shift for shift in everyone if shift not in near],
        everyone,
        around(FIRST_SOURCE),
        around(LAST_SOURCE),
        around(LAST_SOURCE),
        near,
    ]

    def remote(turn, k):
        shift_x, shift_y = shifts[turn][k]
        slot_x = index_x if span_x == count_x else lead_x - shift_x
        slot_y = index_y if span_y == count_y else lead_y - shift_y
        return pltpu.make_async_remote_copy(
            src_ref=block.at[turn % 5],
            dst_ref=arrived.at[turn, slot_y * span_x + slot_x],
            send_sem=send_sems.at[turn, k],
            recv_sem=recv_sems.at[turn, k],
            device_id={
                "gx": lax.rem(index_x + shift_x + count_x, count_x),
                "gy": lax.rem(index_y + shift_y + count_y, count_y),
            },
            device_id_type=MESH,
        )

    def keep_own(turn):
        return pltpu.make_async_copy(
            block.at[turn % 5], arrived.at[turn, own_slot], own_sems.at[turn]
        )

    def send(turn):
        for k in range(len(shifts[turn])):
            remote(turn, k).start()
        if turn > 0:
            keep_own(turn).start()

    def receive(turn, number, target):
        for k in range(len(shifts[turn])):
            remote(turn, k).wait_recv()
        if turn > 0:
            keep_own(turn).wait()
        height = number * grid_x
        half = steps_of(iota((height, LANES), 1), size_yz, 2)
        keep = half == (iota((height, LANES), 0) & 1)
        matrix = jnp.concatenate([spread_mat[:height], spread_mat[rows : rows + height]], axis=0)
        for t in range(tiles):
            slots = arrived[turn, t * 2 * span_x : (t + 1) * 2 * span_x].reshape(tile_rows, LANES)
            both = dot(matrix, slots)
            value = jnp.where(keep, both[:height], pltpu.roll(both[height:], size_yz, 1))
            part = slice(t * LANES, (t + 1) * LANES)
            if turn == 0:
                value = value + target[:height, part]
            target[:height, part] = value

    def at(ref, i, start=0):
        return ref[(start + i) * grid_x : (start + i + 1) * grid_x, :]

    def put(ref):
        def write(i, value):
            ref[i * grid_x : (i + 1) * grid_x, :] = value.astype(ref.dtype)

        return write

    def enter(values):
        return dot(values, enter_mat[...])

    def stacked(window, target):
        three = jnp.concatenate(
            [pltpu.roll(window, width, 1), window, pltpu.roll(window, LANES - width, 1)], axis=0
        )
        target[...] = dot(pick_mat[...], three.astype(jnp.bfloat16)).astype(jnp.bfloat16)

    def conv(weights, outs, source, unit, first, count, emit):
        matrix = weights[...]
        for p in range(first, first + count, 2):
            columns = jnp.concatenate(
                [source[(p - 1 + q) * unit : (p + 2 + q) * unit, :] for q in (0, 1)], axis=1
            )
            product = dot(matrix, columns)
            for q in (0, 1):
                part = product[:, q * LANES : (q + 1) * LANES]
                emit(
                    p + q,
                    pltpu.roll(part[:outs], 1, 1)
                    + part[outs : 2 * outs]
                    + pltpu.roll(part[2 * outs : 3 * outs], LANES - 1, 1),
                )

    def store_stack(target, p, value):
        base = p * 3 * hidden
        for c, turned in enumerate((width, 0, LANES - width)):
            moved = pltpu.roll(value, turned, 1) if turned else value
            target[base + c * hidden : base + (c + 1) * hidden, :] = moved.astype(jnp.bfloat16)

    def middle(source, p):
        return source[(3 * p + 1) * hidden : (3 * p + 2) * hidden, :].astype(F32)

    def store_error(target, p, value):
        if not RIM <= p < RIM + size_x:
            return
        kept = value * mine[:1]
        for b, turned in enumerate((LANES - 1, 0, 1)):
            moved = pltpu.roll(kept, turned, 1) if turned else kept
            target[
                b * hidden : (b + 1) * hidden, (p - RIM) * LANES : (p - RIM + 1) * LANES
            ] = moved.astype(jnp.bfloat16)

    def forward(zx, z1, z2, margin, turn):
        conv(
            w1, hidden, zx, 16, RIM - margin + 1, size_x + 2 * margin - 2,
            lambda p, v: store_stack(z1, p, jnp.tanh(v) * inside(p)),
        )
        conv(
            w23.at[: 3 * hidden], hidden, z1, 3 * hidden, RIM - margin + 2, size_x + 2 * margin - 4,
            lambda p, v: store_stack(z2, p, jnp.tanh(v) * inside(p)),
        )
        leave(w23.at[3 * hidden : 3 * hidden + 32], z2, turn)

    def leave(weights, source, turn):
        kept = {}
        conv(
            weights, FIELD_ROWS, source, 3 * hidden, RIM, size_x, lambda p, v: kept.update({p - RIM: v}),
        )
        sides = [
            jnp.concatenate([kept[q + 2 * i] for i in range(size_x // 2)], axis=0) for q in (0, 1)
        ]
        both = jnp.concatenate(sides, axis=1).astype(jnp.bfloat16)
        block[turn] = dot(both, leave_mat[...]).astype(WIRE)

    def backward(ref, zx, z1, z2, margin):
        window = enter(ref[...])
        stacked(window, zin)
        kept = window * mine[:1]
        three = jnp.concatenate(
            [pltpu.roll(kept, LANES - 1, 1), kept, pltpu.roll(kept, 1, 1)], axis=0
        )
        own = dot(
            pick_mat[RIM * 16 : (RIM + size_x) * 16, :], three.astype(jnp.bfloat16)
        ).astype(jnp.bfloat16)
        for p in range(size_x):
            e3s[:, p * LANES : (p + 1) * LANES] = own[p * 16 : (p + 1) * 16]
        span = margin - 2

        def second(p, v):
            slope = 1.0 - jnp.square(middle(z2, p))
            value = v * slope * inside(p)
            store_stack(ze2, p, value)
            store_error(e2s, p, value)

        def first(p, v):
            slope = 1.0 - jnp.square(middle(z1, p))
            value = v * slope * inside(p)
            if span > 1:
                store_stack(ze1, p, value)
            store_error(e1s, p, value)

        conv(w3t, hidden, zin, 16, RIM - span, size_x + 2 * span, second)
        conv(w2t, hidden, ze2, 3 * hidden, RIM - span + 1, size_x + 2 * span - 2, first)

    def gradients(zx, z1, z2, save):
        def wide(source, unit, low, high):
            return jnp.concatenate(
                [
                    source[(RIM + p - 1) * unit + low : (RIM + p - 1) * unit + high, :]
                    for p in range(size_x)
                ],
                axis=1,
            )

        deep = 9 * hidden
        zero = jnp.zeros((hidden, size_x * LANES), jnp.bfloat16)
        e2 = e2s[...]
        values = wide(z1, 3 * hidden, 0, deep)
        save(0, dot_nt(values, e2[: 2 * hidden]))
        last = e2[2 * hidden :]
        save(
            deep,
            dot_nt(values[: deep // 2], jnp.concatenate([last, zero], axis=0))
            + dot_nt(values[deep // 2 :], jnp.concatenate([zero, last], axis=0)),
        )
        start = deep + deep // 2
        e1 = e1s[...]
        values = wide(zx, 16, 0, 48)
        save(start, dot_nt(values, e1[: 2 * hidden]))
        start += 48
        tail = dot_nt(values, jnp.concatenate([e1[2 * hidden :], zero], axis=0))
        e3 = e3s[...]
        product = dot_nt(e3, wide(z2, 3 * hidden, 0, 8 * hidden))
        for j in range(8 * hidden // LANES):
            save(start, product[:, j * LANES : (j + 1) * LANES])
            start += 16
        late = dot_nt(
            e3, jnp.concatenate([zero, wide(z2, 3 * hidden, 8 * hidden, deep)], axis=0)
        )
        save(start, tail[:16] + late)
        save(start + 16, tail[16:])

    slope = slopes(
        origin_x * size_x, origin_y * size_yz, all_x, all_y * NZ, (grid_x, grid_yz)
    )
    def prepare():
        first_in = turned_kernels.shape[0] - 2 * LANES
        long = kernel_mid.shape[1]
        laid[hidden:, :] = jnp.zeros((laid.shape[0] - hidden, laid.shape[1]), F32)
        laid[:hidden, long // LANES * LANES :] = jnp.zeros(
            (hidden, laid.shape[1] - long // LANES * LANES), F32
        )
        laid[:hidden, :long] = kernel_mid[...].astype(F32)
        laid[hidden : hidden + channels, :long] = kernel_out[...].astype(F32)
        laid[:hidden, first_in : first_in + kernel_in.shape[1]] = kernel_in[...].astype(F32)
        for j in range(laid.shape[1] // LANES):
            part = slice(j * LANES, (j + 1) * LANES)
            turned_kernels[part, :] = jnp.transpose(laid[:, part])
        lane = iota((hidden, LANES), 1)
        low = lane < hidden

        def tap(a, b, c):
            return turned_kernels[pl.ds(a * 9 + b * 3 + c, hidden, stride=27), :]

        def tap_in(a, b, c):
            return turned_kernels[pl.ds(first_in + a * 9 + b * 3 + c, FIELD_ROWS, stride=27), :]

        def two(left, right):
            return jnp.where(
                iota(left.shape, 1) < hidden, left, pltpu.roll(right, hidden, 1)
            )

        empty = jnp.zeros((hidden, LANES), F32)
        for n in range(0, 9, 2):
            tops, ends = [], []
            for m in (n, n + 1):
                if m > 8:
                    tops.append(empty)
                    ends.append(empty)
                    continue
                taps = [tap(m // 3, b, m % 3) for b in range(3)]
                tops.append(two(taps[0], taps[1]))
                late = jnp.where(
                    lane < hidden + 8,
                    taps[0],
                    jnp.where(
                        lane < hidden + 16,
                        pltpu.roll(taps[1], 8, 1),
                        jnp.where(lane < hidden + 24, pltpu.roll(taps[2], 16, 1), 0.0),
                    ),
                )
                ends.append(jnp.where(low, taps[2], late))
            stop = min((n + 2) * hidden, 9 * hidden)
            for start, halves in ((0, tops), (LANES, ends)):
                value = jnp.transpose(jnp.concatenate(halves, axis=0)).astype(jnp.bfloat16)
                w23[start : start + LANES, n * hidden : stop] = value[:, : stop - n * hidden]
        for b in range(3):
            for n in range(0, 9, 2):
                ours = [tap(2 - m // 3, 2 - b, 2 - m % 3) for m in range(n, min(n + 2, 9))]
                value = two(*ours) if len(ours) == 2 else ours[0][:, :hidden]
                w2t[b * hidden : (b + 1) * hidden, n * hidden : n * hidden + value.shape[1]] = (
                    value.astype(jnp.bfloat16)
                )
            placed = None
            for m in range(9):
                value = jnp.where(low, 0.0, tap(2 - m // 3, 2 - b, 2 - m % 3))
                goal = (m // 3) * 16 + (m % 3) * channels
                value = pltpu.roll(value, (goal - hidden) % LANES, 1)
                placed = value if placed is None else placed + value
            w3t[b * hidden : (b + 1) * hidden, :] = placed[:, :48].astype(jnp.bfloat16)
        for n in range(0, 9, 2):
            bands = []
            for b in range(3):
                ours = [tap_in(2 - m // 3, 2 - b, 2 - m % 3) for m in range(n, min(n + 2, 9))]
                bands.append(two(*ours) if len(ours) == 2 else ours[0])
            bands.append(jnp.zeros((FIELD_ROWS, LANES), F32))
            stop = min((n + 2) * hidden, 9 * hidden)
            value = jnp.concatenate(bands, axis=0).astype(jnp.bfloat16)
            w1t[:, n * hidden : stop] = value[:, : stop - n * hidden]
        tops, ends = [], []
        for a in range(3):
            bands = []
            for b in range(3):
                band = None
                for c in range(3):
                    value = jnp.concatenate(
                        [tap_in(a, b, c), jnp.zeros((FIELD_ROWS, LANES), F32)], axis=0
                    )
                    value = pltpu.roll(value, c * channels, 0) if c else value
                    band = value if band is None else band + value
                bands.append(band)
            tops.append(two(bands[0], bands[1]))
            ends.append(bands[2])
        for start, parts in ((0, tops), (LANES, ends)):
            value = jnp.concatenate(parts + [jnp.zeros((LANES - 48, LANES), F32)], axis=0)
            value = jnp.transpose(value)[: min(LANES, 3 * hidden - start), :48]
            w1[start : start + value.shape[0], :] = value.astype(jnp.bfloat16)

    send(5)
    send(1)
    send(0)
    for load in loads[4:]:
        load.wait()
    prepare()
    receive(5, channels, fields)
    stacked(enter(fields[...].astype(jnp.bfloat16)), zx0)
    forward(zx0, z1s0, z2s0, 3, 2)
    send(2)

    receive(0, channels, fields)
    receive(1, channels + 2, flow)
    velocity, shear = at(flow, 0), at(flow, 1)
    error = xs
    retreat(
        [at(flow, i, 2) for i in range(channels)], velocity, shear, channels, slope,
        put(error), put(carried),
    )
    receive(2, channels, sources)
    advance(
        lambda i: at(fields, i), velocity, shear, lambda i: at(sources, i), channels, slope,
        put(fields),
    )
    stacked(enter(fields[...].astype(jnp.bfloat16)), zx1)
    forward(zx1, z1s1, z2s1, 4, 3)
    backward(error, zx1, z1s1, z2s1, 4)
    leave(w1t, ze1, 4)
    send(4)
    send(3)

    def save(start, value):
        table[start : start + value.shape[0], :] = value

    gradients(zx1, z1s1, z2s1, save)
    receive(4, channels, sources)
    retreat(
        [at(carried, i) + at(sources, i) for i in range(channels)],
        velocity, shear, channels, slope, put(error), None,
    )
    backward(error, zx0, z1s0, z2s0, 3)

    def finish(start, value):
        wire[start : start + value.shape[0], :] = (
            table[start : start + value.shape[0], :] + value
        ).astype(WIRE)

    height = wire.shape[0]
    used = table.shape[0]
    if height > used:
        wire[used:, :] = jnp.zeros((height - used, LANES), WIRE)
    gradients(zx0, z1s0, z2s0, finish)

    pairs = total // 2
    chunk = height // total
    core = lax.rem(index_x, 2)
    pair = index_y * (count_x // 2) + lax.div(index_x, 2)

    def at_pair(place, side):
        return {
            "gx": lax.rem(place, count_x // 2) * 2 + side, "gy": lax.div(place, count_x // 2)
        }

    half = height // 2
    copy = pltpu.make_async_remote_copy(
        src_ref=wire.at[pl.ds(pl.multiple_of((1 - core) * half, 16), half)],
        dst_ref=from_core,
        send_sem=core_sems.at[0],
        recv_sem=core_sems.at[1],
        device_id=at_pair(pair, 1 - core),
        device_id_type=MESH,
    )
    copy.start()
    receive(3, channels, sources)
    advance(
        lambda i: at(fields, i), velocity, shear, lambda i: at(sources, i), channels, slope,
        put(fields),
    )
    slot = index_y - origin_y
    tile = lax.div(slot, 2)
    for i in range(channels):
        value = fields[i * grid_x : (i + 1) * grid_x, pl.ds(pl.multiple_of(tile * LANES, LANES), LANES)]
        value = jnp.where(lax.rem(slot, 2) == 0, value, pltpu.roll(value, size_yz, 1))
        value = pltpu.roll(value, lax.rem(grid_x - (index_x - origin_x) * size_x, grid_x), 0)
        out_state[i] = value[:size_x, :size_yz]
    copy.wait()
    halved[...] = (
        wire[pl.ds(pl.multiple_of(core * half, 16), half), :].astype(F32)
        + from_core[...].astype(F32)
    ).astype(WIRE)

    def scatter(k):
        other = lax.rem(pair + k, pairs)
        return pltpu.make_async_remote_copy(
            src_ref=halved.at[pl.ds(pl.multiple_of(other * chunk, 16), chunk)],
            dst_ref=from_rest.at[k - 1],
            send_sem=rest_sems.at[0, k - 1],
            recv_sem=rest_sems.at[1, k - 1],
            device_id=at_pair(other, core),
            device_id_type=MESH,
        )

    for_peers(pairs, lambda k: scatter(k).start())
    for_peers(pairs, lambda k: scatter(k).wait_recv())
    summed = halved[pl.ds(pl.multiple_of(pair * chunk, 16), chunk), :].astype(F32)
    for k in range(pairs - 1):
        summed = summed + from_rest[k].astype(F32)
    spot = pl.ds(pl.multiple_of(core * half + pair * chunk, 16), chunk)
    out_table[spot, :] = summed.astype(WIRE)

    def gather(k):
        other = lax.rem(pair + k, pairs)
        return pltpu.make_async_remote_copy(
            src_ref=out_table.at[spot],
            dst_ref=out_table.at[spot],
            send_sem=rest_sems.at[2, k - 1],
            recv_sem=rest_sems.at[3, k - 1],
            device_id=at_pair(other, core),
            device_id_type=MESH,
        )

    for_peers(pairs, lambda k: gather(k).start())
    for_peers(pairs, lambda k: gather(k).wait_recv())
    side = pl.ds(pl.multiple_of(core * half, 16), half)
    copy = pltpu.make_async_remote_copy(
        src_ref=out_table.at[side],
        dst_ref=out_table.at[side],
        send_sem=core_sems.at[2],
        recv_sem=core_sems.at[3],
        device_id=at_pair(pair, 1 - core),
        device_id_type=MESH,
    )
    copy.start()
    copy.wait()
    for_peers(pairs, lambda k: scatter(k).wait_send())
    for_peers(pairs, lambda k: gather(k).wait_send())
    for turn in range(6):
        for k in range(len(shifts[turn])):
            remote(turn, k).wait_send()


def unpack_kernel(
    plan, state_ref, table_ref, out_state, grad_in, grad_mid, grad_out, name_mat, place_mat, turned
):
    channels, hidden = plan
    out_state[...] = state_ref[...]
    r, k = iota((48, 256), 0), iota((48, 256), 1)
    inner = r & 15
    side = steps_of(inner, channels, 3)
    for b in range(3):
        goal = (inner - channels * side) * 27 + shifted_by(r, 16) * 9 + b * 3 + side
        name_mat[b * 48 : (b + 1) * 48] = one_hot((inner < 3 * channels) & (goal == k))
    r, k = iota((16, LANES), 0), iota((16, LANES), 1)
    for b in range(3):
        place_mat[b * 16 : (b + 1) * 16] = one_hot(
            (r >= b * channels) & (r < (b + 1) * channels) & (k == r - b * channels + hidden)
        )

    deep = 9 * hidden
    folded = table_ref[deep : deep + deep // 2, :].astype(F32)
    behind = jnp.concatenate([folded, pltpu.roll(folded, hidden, 1)], axis=0)
    start = deep + deep // 2
    lead = table_ref[start : start + 48, :]
    start += 48
    parts = []
    for j in range(8 * hidden // LANES):
        parts.append(table_ref[start : start + 16, :])
        start += 16
    last = table_ref[start : start + 48, :]
    parts.append(pltpu.roll(last[:16].astype(F32), hidden, 1).astype(WIRE)[:, :hidden])
    trail = jnp.concatenate(parts, axis=1)
    contract = (((0,), (0,)), ((), ()))
    low = iota((hidden, LANES), 1) < hidden
    for b in range(3):
        placed = lax.dot_general(
            trail, place_mat[b * 16 : (b + 1) * 16], contract, preferred_element_type=F32
        )
        for n in range(9):
            rows_of = slice(n * hidden, (n + 1) * hidden)
            if b == 2:
                value = behind[rows_of]
            else:
                value = table_ref[rows_of, :].astype(F32)
                value = pltpu.roll(value, hidden, 1) if b == 1 else value
            turned[pl.ds((n // 3) * 9 + b * 3 + n % 3, hidden, stride=27), :] = (
                jnp.where(low, value, placed[rows_of])
            )
    long = grad_mid.shape[1]
    for start in range(0, long, LANES):
        size = min(LANES, long - start)
        value = jnp.transpose(turned[start : start + LANES, :])
        grad_mid[:, start : start + size] = value[:hidden, :size]
        grad_out[:, start : start + size] = value[hidden : hidden + channels, :size]
    named = [
        lax.dot_general(
            source, name_mat[b * 48 : (b + 1) * 48], contract, preferred_element_type=F32
        )
        for b, source in enumerate((lead, lead, last))
    ]
    value = named[0][:hidden] + named[1][hidden:] + named[2][:hidden]
    grad_in[...] = value[:, : grad_in.shape[1]]


def body(perturbation, mean_velocity, mean_shear, cotangent, kernel_in, kernel_mid, kernel_out):
    channels, size_x, size_yz = perturbation.shape
    hidden = kernel_in.shape[0]
    count_x, count_y = lax.axis_size("gx"), lax.axis_size("gy")
    total = count_x * count_y
    span_x, span_y = span_of(count_x, REACH_X)[0], span_of(count_y, REACH_Y)[0]
    held = span_x * span_y
    grid_x, grid_yz = span_x * size_x, span_y * size_yz
    planes = size_x + 2 * RIM
    operands = (
        perturbation, mean_velocity, mean_shear, cotangent, kernel_in, kernel_mid, kernel_out,
    )
    results = (perturbation,) + operands[4:]
    used = 1024
    unit = total * 16
    height = -(-used // unit) * unit
    deep, wide = 3 * hidden, size_x * LANES
    taps = -(-kernel_mid.shape[1] // LANES) * LANES
    b16 = jnp.bfloat16
    vmem = pltpu.VMEM
    scratch = [vmem(a.shape, a.dtype) for a in operands] + [
        vmem((5, BLOCK_ROWS, LANES), WIRE),
        vmem((6, held, BLOCK_ROWS, LANES), WIRE),
        vmem((channels * grid_x, grid_yz), F32),
        vmem((channels * grid_x, grid_yz), F32),
        vmem(((channels + 2) * grid_x, grid_yz), F32),
        vmem((channels * grid_x, grid_yz), F32),
        vmem((planes * 16, LANES), b16),
        vmem((planes * 16, LANES), b16),
        vmem((planes * deep, LANES), b16),
        vmem((planes * deep, LANES), b16),
        vmem((planes * deep, LANES), b16),
        vmem((planes * deep, LANES), b16),
        vmem((planes * 16, LANES), b16),
        vmem((planes * deep, LANES), b16),
        vmem((planes * deep, LANES), b16),
        vmem((deep, wide), b16),
        vmem((deep, wide), b16),
        vmem((16, wide), b16),
        vmem((channels * grid_x, grid_yz), b16),
        vmem((2, BLOCK_ROWS, LANES), F32),
        vmem((LANES, taps + 2 * LANES), F32),
        vmem((taps + 2 * LANES, LANES), F32),
        vmem((deep, 48), b16),
        vmem((2 * LANES, 3 * deep), b16),
        vmem((deep, 48), b16),
        vmem((deep, 3 * deep), b16),
        vmem((32, 3 * deep), b16),
        vmem((2 * FIELD_ROWS * grid_x, 2 * span_x * BLOCK_ROWS), b16),
        vmem((grid_yz, LANES), b16),
        vmem((planes * 16, 3 * channels * grid_x), b16),
        vmem((2 * LANES, LANES), b16),
        vmem((used, LANES), F32),
        vmem((height, LANES), WIRE),
        vmem((height // 2, LANES), WIRE),
        vmem((height // 2, LANES), WIRE),
        vmem((total // 2 - 1, height // total, LANES), WIRE),
        pltpu.SemaphoreType.DMA((6, held - 1)),
        pltpu.SemaphoreType.DMA((6, held - 1)),
        pltpu.SemaphoreType.DMA((4,)),
        pltpu.SemaphoreType.DMA((4, total // 2 - 1)),
        pltpu.SemaphoreType.DMA((6,)),
        pltpu.SemaphoreType.DMA((len(operands),)),
    ]
    whole = pl.BlockSpec(memory_space=pltpu.VMEM)
    state, table = pl.pallas_call(
        functools.partial(whole_kernel, (count_x, count_y, channels, hidden, size_x, size_yz)),
        out_shape=[
            jax.ShapeDtypeStruct(perturbation.shape, F32),
            jax.ShapeDtypeStruct((height, LANES), WIRE),
        ],
        in_specs=[pl.BlockSpec(memory_space=pltpu.HBM)] * len(operands),
        out_specs=[whole] * 2,
        scratch_shapes=scratch,
        compiler_params=pltpu.CompilerParams(
            collective_id=0, has_side_effects=True, vmem_limit_bytes=56 * 2**20
        ),
    )(*operands)
    return tuple(
        pl.pallas_call(
            functools.partial(unpack_kernel, (channels, hidden)),
            out_shape=[jax.ShapeDtypeStruct(r.shape, F32) for r in results],
            in_specs=[whole] * 2,
            out_specs=[whole] * len(results),
            scratch_shapes=[
                vmem((3 * 48, 2 * LANES), b16),
                vmem((3 * 16, LANES), b16),
                vmem((taps, LANES), F32),
            ],
            compiler_params=pltpu.CompilerParams(vmem_limit_bytes=56 * 2**20),
        )(state, table)
    )


def solution(mesh):
    return jax.shard_map(
        body,
        mesh=mesh,
        in_specs=(
            P(None, "gx", "gy"),
            P("gx", "gy"),
            P("gx", "gy"),
            P(None, "gx", "gy"),
            P(),
            P(),
            P(),
        ),
        out_specs=(P(None, "gx", "gy"), P(), P(), P()),
        check_vma=False,
    )
```

```python
import functools
import math

import jax
import jax.numpy as jnp
from jax import lax
from jax.experimental import pallas as pl
from jax.experimental.pallas import tpu as pltpu
from jax.sharding import PartitionSpec as P

NZ = 8
LANES = 128
FIELD_ROWS = 8
BLOCK_ROWS = 2 * FIELD_ROWS
RIM = 4
REACH_X = 5
REACH_Y = 3
NEAR, STATE, FIRST_SOURCE, LAST_SOURCE = 3, 18, 15, 8

TIME_STEP = 0.25
STENCIL_WEIGHTS = (0.75, -0.15, 1.0 / 60.0)
MESH = pl.DeviceIdType.MESH
WIRE = jnp.bfloat16
F32 = jnp.float32


def dot(a, b):
    return lax.dot_general(a, b, (((1,), (0,)), ((), ())), preferred_element_type=F32)


def dot_nt(a, b):
    return lax.dot_general(a, b, (((1,), (1,)), ((), ())), preferred_element_type=F32)


def iota(shape, axis):
    return lax.broadcasted_iota(jnp.int32, shape, axis)


def shifted_by(values, size):
    return lax.shift_right_logical(values, size.bit_length() - 1)


def steps_of(values, size, count):
    return sum((values >= size * n).astype(jnp.int32) for n in range(1, count))


def one_hot(condition):
    return jnp.where(condition, 1.0, 0.0).astype(jnp.bfloat16)


def span_of(count, reach):
    span = min(count, 2 * reach + 2)
    return span, span // 2


def slopes(origin_x, origin_yz, grid_x, grid_yz, shape):
    row = iota(shape, 0) + origin_x
    lane = iota(shape, 1) + origin_yz
    depth = lane & (NZ - 1)

    def moved(field, offset, axis):
        return pltpu.roll(field, (-offset) % field.shape[axis], axis)

    def edged(field, axis, position, unit):
        size = (grid_x, grid_yz)[axis]
        result = None
        for offset, weight in zip((1, 2, 3), STENCIL_WEIGHTS):
            step = offset * unit
            upper = jnp.where(position < size - step, moved(field, step, axis), 0.0)
            lower = jnp.where(position >= step, moved(field, -step, axis), 0.0)
            contrib = weight * (upper - lower)
            result = contrib if result is None else result + contrib
        return result

    def along_x(field):
        return edged(field, 0, row, 1)

    def along_y(field):
        return edged(field, 1, lane, NZ)

    def along_z(field):
        result = None
        for offset, weight in zip((1, 2, 3), STENCIL_WEIGHTS):
            upper = jnp.where(
                depth < NZ - offset, moved(field, offset, 1), moved(field, offset - NZ, 1)
            )
            lower = jnp.where(depth >= offset, moved(field, -offset, 1), moved(field, NZ - offset, 1))
            contrib = weight * (upper - lower)
            result = contrib if result is None else result + contrib
        return result

    return along_x, along_y, along_z


def advance(now, velocity, shear, channels, slope, save, saved, ready, source, write):
    fields = range(channels)
    dx, dy, dz = slope

    def rates(f):
        across = [dx(c) for c in f]
        divergence = across[1] + dy(f[2]) + dz(f[3])
        return (
            -velocity * across[0] - divergence,
            -velocity * across[1] - shear * f[2] - across[4],
            -velocity * across[2] - dy(f[4]),
            -velocity * across[3] - dz(f[4]),
            -velocity * across[4] - divergence,
        )

    rate = rates([now(i) for i in fields])
    for i in fields:
        save(i, now(i) + TIME_STEP * rate[i])
    ready()
    one = [saved(i) + TIME_STEP * source(i) for i in fields]
    rate = rates(one)
    two = [0.75 * now(i) + 0.25 * (one[i] + TIME_STEP * (rate[i] + source(i))) for i in fields]
    rate = rates(two)
    for i in fields:
        write(i, 1.0 / 3.0 * now(i) + 2.0 / 3.0 * (two[i] + TIME_STEP * (rate[i] + source(i))))


def retreat(last, velocity, shear, channels, slope, write_error, write_carried):
    fields = range(channels)
    dx, dy, dz = slope

    def rates(g):
        acoustic = g[0] + g[4]
        return (
            dx(velocity * g[0]),
            dx(velocity * g[1] + acoustic),
            dx(velocity * g[2]) - shear * g[1] + dy(acoustic),
            dx(velocity * g[3]) + dz(acoustic),
            dx(velocity * g[4] + g[1]) + dy(g[2]) + dz(g[3]),
        )

    rate = rates(last)
    second = [2.0 / 3.0 * last[i] + 2.0 / 3.0 * TIME_STEP * rate[i] for i in fields]
    rate = rates(second)
    first = [0.25 * second[i] + 0.25 * TIME_STEP * rate[i] for i in fields]
    for i in fields:
        write_error(i, TIME_STEP * (2.0 / 3.0 * last[i] + 0.25 * second[i] + first[i]))
    if write_carried is None:
        return
    rate = rates(first)
    for i in fields:
        write_carried(i, 1.0 / 3.0 * last[i] + 0.75 * second[i] + first[i] + TIME_STEP * rate[i])


def for_peers(total, body):
    if total <= 32:
        for k in range(1, total):
            body(k)
    else:
        lax.fori_loop(1, total, lambda k, c: (body(k), c)[1], 0)


def onward(index, shift, count):
    if not isinstance(shift, int):
        return lax.rem(index + shift, count)
    if shift % count == 0:
        return index
    moved = index + shift % count
    return jnp.where(moved >= count, moved - count, moved)


def apart(k, count):
    if isinstance(k, int):
        return k % count, k // count
    return lax.rem(k, count), lax.div(k, count)


def whole_kernel(
    plan, state_from, velocity_from, shear_from, cotangent_from, in_from, mid_from, out_from,
    out_state, out_table,
    state_ref, velocity_ref, shear_ref, cotangent_ref, kernel_in, kernel_mid, kernel_out,
    block, arrived, arrived_both, fields, sources, flow, carried, zx0, zx1, z1s0, z1s1, z2s0, z2s1, zin, ze2, ze1,
    e1s, e2s, e3s, xs, packs, laid, turned_kernels, w1, w23, w3t, w2t, w1t, spread_mat, enter_mat, pick_mat, leave_mat, table, wire, from_core, halved, from_rest,
    send_sems, recv_sems, core_sems, rest_sems, own_sems, load_sems,
):
    count_x, count_y, channels, hidden, size_x, size_yz = plan
    total = count_x * count_y
    span_x, lead_x = span_of(count_x, REACH_X)
    span_y, lead_y = span_of(count_y, REACH_Y)
    held = span_x * span_y
    all_x, all_y = count_x * size_x, count_y * size_yz // NZ
    grid_x, grid_yz = span_x * size_x, span_y * size_yz
    size_y = size_yz // NZ
    width = size_y + 2 * RIM
    planes = size_x + 2 * RIM
    index_x, index_y = lax.axis_index("gx"), lax.axis_index("gy")
    origin_x = 0 if span_x == count_x else index_x - lead_x
    origin_y = 0 if span_y == count_y else index_y - lead_y
    tiles = grid_yz // LANES
    tile_rows = 2 * span_x * BLOCK_ROWS
    flat = channels * grid_x

    def device(k):
        shift_x, shift_y = apart(k, count_x)
        return {
            "gx": onward(index_x, shift_x, count_x), "gy": onward(index_y, shift_y, count_y)
        }

    loads = [
        pltpu.make_async_copy(source, target, load_sems.at[n])
        for n, (source, target) in enumerate(
            (
                (state_from, state_ref),
                (velocity_from, velocity_ref),
                (shear_from, shear_ref),
                (cotangent_from, cotangent_ref),
                (in_from, kernel_in),
                (mid_from, kernel_mid),
                (out_from, kernel_out),
            )
        )
    ]
    for load in loads:
        load.start()
    arrived[...] = jnp.zeros(arrived.shape, WIRE)
    arrived_both[...] = jnp.zeros(arrived_both.shape, WIRE)
    barrier = pltpu.get_barrier_semaphore()
    for_peers(
        total,
        lambda k: pl.semaphore_signal(
            barrier, inc=1, device_id=device(k), device_id_type=MESH
        ),
    )

    rows = FIELD_ROWS * grid_x
    r, k = iota((rows, tile_rows), 0), iota((rows, tile_rows), 1)
    field = steps_of(r, grid_x, FIELD_ROWS)
    at_x = r - field * grid_x
    part = steps_of(k, tile_rows // 2, 2)
    rest = k - part * (tile_rows // 2)
    owner = shifted_by(rest, BLOCK_ROWS)
    inner = rest & (BLOCK_ROWS - 1)
    odd = at_x & 1
    row = (shifted_by(at_x, 2) & 1) * FIELD_ROWS + field
    same = (owner == shifted_by(at_x, size_x)) & (inner == row)
    spread_mat[:rows] = one_hot(same & (part == odd))
    spread_mat[rows:] = one_hot(same & (part != odd))
    r, k = iota((grid_yz, LANES), 0), iota((grid_yz, LANES), 1)
    enter_mat[...] = one_hot(
        ((r & (NZ - 1)) == shifted_by(k, width))
        & (shifted_by(r, NZ) + origin_y * size_y == index_y * size_y - RIM + (k & (width - 1)))
        & (shifted_by(r, NZ) + origin_y * size_y >= 0)
        & (shifted_by(r, NZ) + origin_y * size_y < all_y)
    )
    r, k = iota((planes * 16, 3 * flat), 0), iota((planes * 16, 3 * flat), 1)
    inner = r & 15
    side = steps_of(inner, channels, 3)
    part = steps_of(k, flat, 3)
    rest = k - part * flat
    field = steps_of(rest, grid_x, channels)
    pick_mat[...] = one_hot(
        (inner < 3 * channels)
        & (part == side)
        & (field == inner - channels * side)
        & (
            rest - field * grid_x + origin_x * size_x
            == index_x * size_x - RIM + shifted_by(r, 16)
        )
        & (rest - field * grid_x + origin_x * size_x >= 0)
        & (rest - field * grid_x + origin_x * size_x < all_x)
    )
    r, k = iota((2 * LANES, LANES), 0), iota((2 * LANES, LANES), 1)
    inner, lane = r & (LANES - 1), k & (size_yz - 1)
    leave_mat[...] = one_hot(
        (shifted_by(r, LANES) == steps_of(k, size_yz, 2))
        & (shifted_by(inner, width) == (lane & (NZ - 1)))
        & ((inner & (width - 1)) == shifted_by(lane, NZ) + RIM)
    )
    across = iota((8, LANES), 1) & (width - 1)
    at_y = across + (index_y * size_y - RIM)
    valid_y = jnp.where((at_y >= 0) & (at_y < all_y), 1.0, 0.0)
    mine = jnp.where((across >= RIM) & (across < RIM + size_y), 1.0, 0.0)

    def inside(p):
        at = index_x * size_x - RIM + p
        scale = jnp.where((at >= 0) & (at < all_x), 1.0, 0.0).astype(F32)
        return (valid_y * scale)[:1]

    def pack(turn, rows_of):
        packs[...] = jnp.zeros(packs.shape, F32)
        for f, at_row in enumerate(rows_of):
            for x in range(size_x):
                spot = (x // 2) * FIELD_ROWS + f
                packs[x % 2, spot : spot + 1, :size_yz] = at_row(x)
        block[turn] = (packs[0] + pltpu.roll(packs[1], size_yz, 1)).astype(WIRE)

    for load in loads[:4]:
        load.wait()
    pack(0, [lambda x, f=f: state_ref[f, x : x + 1, :] for f in range(channels)])
    scale = 1.0 / math.sqrt(total * size_x * size_yz)
    pack(
        1,
        [lambda x: velocity_ref[x : x + 1, :], lambda x: shear_ref[x : x + 1, :]]
        + [lambda x, f=f: cotangent_ref[f, x : x + 1, :] * scale for f in range(channels)],
    )
    pl.semaphore_wait(barrier, total - 1)

    own_slot = (index_y - origin_y) * span_x + index_x - origin_x

    def around(cells):
        reach_x, reach_y = -(-cells // size_x), -(-cells // size_y)
        found = [
            (x, y)
            for y in range(-lead_y, span_y - lead_y)
            for x in range(-lead_x, span_x - lead_x)
            if abs(x) <= reach_x and abs(y) <= reach_y and (x or y)
        ]
        return sorted(found, key=lambda shift: -2 * abs(shift[1]) - abs(shift[0]))

    everyone = around(STATE)
    near = around(NEAR)
    shifts = [
        [],
        everyone,
        around(FIRST_SOURCE),
        around(LAST_SOURCE),
        around(LAST_SOURCE),
        near,
    ]

    def landing(turn, slot):
        return arrived_both.at[slot] if turn == 1 else arrived.at[turn, slot]

    def remote(turn, k):
        shift_x, shift_y = shifts[turn][k]
        slot_x = index_x if span_x == count_x else lead_x - shift_x
        slot_y = index_y if span_y == count_y else lead_y - shift_y
        return pltpu.make_async_remote_copy(
            src_ref=block.at[:2] if turn == 1 else block.at[turn % 5],
            dst_ref=landing(turn, slot_y * span_x + slot_x),
            send_sem=send_sems.at[turn, k],
            recv_sem=recv_sems.at[turn, k],
            device_id={
                "gx": onward(index_x, shift_x, count_x),
                "gy": onward(index_y, shift_y, count_y),
            },
            device_id_type=MESH,
        )

    def keep_own(turn):
        return pltpu.make_async_copy(
            block.at[:2] if turn == 1 else block.at[turn % 5],
            landing(turn, own_slot),
            own_sems.at[turn],
        )

    def send(turn):
        for k in range(len(shifts[turn])):
            remote(turn, k).start()
        if turn > 0:
            keep_own(turn).start()

    def receive(turn, number, target):
        for k in range(len(shifts[turn])):
            remote(turn, k).wait_recv()
        if turn > 0:
            keep_own(turn).wait()
        place(lambda slots: arrived_both[slots, 1] if turn == 1 else arrived[turn, slots], number, target)

    def place(slots_of, number, target):
        height = number * grid_x
        half = steps_of(iota((height, LANES), 1), size_yz, 2)
        keep = half == (iota((height, LANES), 0) & 1)
        matrix = jnp.concatenate([spread_mat[:height], spread_mat[rows : rows + height]], axis=0)
        for t in range(tiles):
            slots = slots_of(slice(t * 2 * span_x, (t + 1) * 2 * span_x)).reshape(tile_rows, LANES)
            both = dot(matrix, slots)
            value = jnp.where(keep, both[:height], pltpu.roll(both[height:], size_yz, 1))
            part = slice(t * LANES, (t + 1) * LANES)
            target[:height, part] = value

    def at(ref, i, start=0):
        return ref[(start + i) * grid_x : (start + i + 1) * grid_x, :]

    def put(ref):
        def write(i, value):
            ref[i * grid_x : (i + 1) * grid_x, :] = value.astype(ref.dtype)

        return write

    def enter(values):
        return dot(values, enter_mat[...])

    def stacked(window, target):
        three = jnp.concatenate(
            [pltpu.roll(window, width, 1), window, pltpu.roll(window, LANES - width, 1)], axis=0
        )
        target[...] = dot(pick_mat[...], three.astype(jnp.bfloat16)).astype(jnp.bfloat16)

    def conv(weights, outs, source, unit, first, count, emit):
        matrix = weights[...]
        for p in range(first, first + count, 2):
            columns = jnp.concatenate(
                [source[(p - 1 + q) * unit : (p + 2 + q) * unit, :] for q in (0, 1)], axis=1
            )
            product = dot(matrix, columns)
            for q in (0, 1):
                part = product[:, q * LANES : (q + 1) * LANES]
                emit(
                    p + q,
                    pltpu.roll(part[:outs], 1, 1)
                    + part[outs : 2 * outs]
                    + pltpu.roll(part[2 * outs : 3 * outs], LANES - 1, 1),
                )

    def store_stack(target, p, value):
        base = p * 3 * hidden
        for c, turned in enumerate((width, 0, LANES - width)):
            moved = pltpu.roll(value, turned, 1) if turned else value
            target[base + c * hidden : base + (c + 1) * hidden, :] = moved.astype(jnp.bfloat16)

    def middle(source, p):
        return source[(3 * p + 1) * hidden : (3 * p + 2) * hidden, :].astype(F32)

    def store_error(target, p, value):
        if not RIM <= p < RIM + size_x:
            return
        kept = value * mine[:1]
        for b, turned in enumerate((LANES - 1, 0, 1)):
            moved = pltpu.roll(kept, turned, 1) if turned else kept
            target[
                b * hidden : (b + 1) * hidden, (p - RIM) * LANES : (p - RIM + 1) * LANES
            ] = moved.astype(jnp.bfloat16)

    def forward(zx, z1, z2, margin, turn):
        conv(
            w1, hidden, zx, 16, RIM - margin + 1, size_x + 2 * margin - 2,
            lambda p, v: store_stack(z1, p, jnp.tanh(v) * inside(p)),
        )
        conv(
            w23.at[: 3 * hidden], hidden, z1, 3 * hidden, RIM - margin + 2, size_x + 2 * margin - 4,
            lambda p, v: store_stack(z2, p, jnp.tanh(v) * inside(p)),
        )
        leave(w23.at[3 * hidden : 3 * hidden + 32], z2, turn)

    def leave(weights, source, turn):
        kept = {}
        conv(
            weights, FIELD_ROWS, source, 3 * hidden, RIM, size_x, lambda p, v: kept.update({p - RIM: v}),
        )
        sides = [
            jnp.concatenate([kept[q + 2 * i] for i in range(size_x // 2)], axis=0) for q in (0, 1)
        ]
        both = jnp.concatenate(sides, axis=1).astype(jnp.bfloat16)
        block[turn] = dot(both, leave_mat[...]).astype(WIRE)

    def backward(ref, zx, z1, z2, margin):
        window = enter(ref[...])
        stacked(window, zin)
        kept = window * mine[:1]
        three = jnp.concatenate(
            [pltpu.roll(kept, LANES - 1, 1), kept, pltpu.roll(kept, 1, 1)], axis=0
        )
        own = dot(
            pick_mat[RIM * 16 : (RIM + size_x) * 16, :], three.astype(jnp.bfloat16)
        ).astype(jnp.bfloat16)
        for p in range(size_x):
            e3s[:, p * LANES : (p + 1) * LANES] = own[p * 16 : (p + 1) * 16]
        span = margin - 2

        def second(p, v):
            slope = 1.0 - jnp.square(middle(z2, p))
            value = v * slope * inside(p)
            store_stack(ze2, p, value)
            store_error(e2s, p, value)

        def first(p, v):
            slope = 1.0 - jnp.square(middle(z1, p))
            value = v * slope * inside(p)
            if span > 1:
                store_stack(ze1, p, value)
            store_error(e1s, p, value)

        conv(w3t, hidden, zin, 16, RIM - span, size_x + 2 * span, second)
        conv(w2t, hidden, ze2, 3 * hidden, RIM - span + 1, size_x + 2 * span - 2, first)

    def gradients(zx, z1, z2, save):
        def wide(source, unit, low, high):
            return jnp.concatenate(
                [
                    source[(RIM + p - 1) * unit + low : (RIM + p - 1) * unit + high, :]
                    for p in range(size_x)
                ],
                axis=1,
            )

        deep = 9 * hidden
        zero = jnp.zeros((hidden, size_x * LANES), jnp.bfloat16)
        e2 = e2s[...]
        values = wide(z1, 3 * hidden, 0, deep)
        save(0, dot_nt(values, e2[: 2 * hidden]))
        last = e2[2 * hidden :]
        save(
            deep,
            dot_nt(values[: deep // 2], jnp.concatenate([last, zero], axis=0))
            + dot_nt(values[deep // 2 :], jnp.concatenate([zero, last], axis=0)),
        )
        start = deep + deep // 2
        e1 = e1s[...]
        values = wide(zx, 16, 0, 48)
        save(start, dot_nt(values, e1[: 2 * hidden]))
        start += 48
        tail = dot_nt(values, jnp.concatenate([e1[2 * hidden :], zero], axis=0))
        e3 = e3s[...]
        product = dot_nt(e3, wide(z2, 3 * hidden, 0, 8 * hidden))
        for j in range(8 * hidden // LANES):
            save(start, product[:, j * LANES : (j + 1) * LANES])
            start += 16
        late = dot_nt(
            e3, jnp.concatenate([zero, wide(z2, 3 * hidden, 8 * hidden, deep)], axis=0)
        )
        save(start, tail[:16] + late)
        save(start + 16, tail[16:])

    slope = slopes(
        origin_x * size_x, origin_y * size_yz, all_x, all_y * NZ, (grid_x, grid_yz)
    )
    def prepare():
        first_in = turned_kernels.shape[0] - 2 * LANES
        long = kernel_mid.shape[1]
        laid[hidden:, :] = jnp.zeros((laid.shape[0] - hidden, laid.shape[1]), F32)
        laid[:hidden, long // LANES * LANES :] = jnp.zeros(
            (hidden, laid.shape[1] - long // LANES * LANES), F32
        )
        laid[:hidden, :long] = kernel_mid[...].astype(F32)
        laid[hidden : hidden + channels, :long] = kernel_out[...].astype(F32)
        laid[:hidden, first_in : first_in + kernel_in.shape[1]] = kernel_in[...].astype(F32)
        for j in range(laid.shape[1] // LANES):
            part = slice(j * LANES, (j + 1) * LANES)
            turned_kernels[part, :] = jnp.transpose(laid[:, part])
        lane = iota((hidden, LANES), 1)
        low = lane < hidden

        def tap(a, b, c):
            return turned_kernels[pl.ds(a * 9 + b * 3 + c, hidden, stride=27), :]

        def tap_in(a, b, c):
            return turned_kernels[pl.ds(first_in + a * 9 + b * 3 + c, FIELD_ROWS, stride=27), :]

        def two(left, right):
            return jnp.where(
                iota(left.shape, 1) < hidden, left, pltpu.roll(right, hidden, 1)
            )

        empty = jnp.zeros((hidden, LANES), F32)
        for n in range(0, 9, 2):
            tops, ends = [], []
            for m in (n, n + 1):
                if m > 8:
                    tops.append(empty)
                    ends.append(empty)
                    continue
                taps = [tap(m // 3, b, m % 3) for b in range(3)]
                tops.append(two(taps[0], taps[1]))
                late = jnp.where(
                    lane < hidden + 8,
                    taps[0],
                    jnp.where(
                        lane < hidden + 16,
                        pltpu.roll(taps[1], 8, 1),
                        jnp.where(lane < hidden + 24, pltpu.roll(taps[2], 16, 1), 0.0),
                    ),
                )
                ends.append(jnp.where(low, taps[2], late))
            stop = min((n + 2) * hidden, 9 * hidden)
            for start, halves in ((0, tops), (LANES, ends)):
                value = jnp.transpose(jnp.concatenate(halves, axis=0)).astype(jnp.bfloat16)
                w23[start : start + LANES, n * hidden : stop] = value[:, : stop - n * hidden]
        for b in range(3):
            for n in range(0, 9, 2):
                ours = [tap(2 - m // 3, 2 - b, 2 - m % 3) for m in range(n, min(n + 2, 9))]
                value = two(*ours) if len(ours) == 2 else ours[0][:, :hidden]
                w2t[b * hidden : (b + 1) * hidden, n * hidden : n * hidden + value.shape[1]] = (
                    value.astype(jnp.bfloat16)
                )
            placed = None
            for m in range(9):
                value = jnp.where(low, 0.0, tap(2 - m // 3, 2 - b, 2 - m % 3))
                goal = (m // 3) * 16 + (m % 3) * channels
                value = pltpu.roll(value, (goal - hidden) % LANES, 1)
                placed = value if placed is None else placed + value
            w3t[b * hidden : (b + 1) * hidden, :] = placed[:, :48].astype(jnp.bfloat16)
        for n in range(0, 9, 2):
            bands = []
            for b in range(3):
                ours = [tap_in(2 - m // 3, 2 - b, 2 - m % 3) for m in range(n, min(n + 2, 9))]
                bands.append(two(*ours) if len(ours) == 2 else ours[0])
            bands.append(jnp.zeros((FIELD_ROWS, LANES), F32))
            stop = min((n + 2) * hidden, 9 * hidden)
            value = jnp.concatenate(bands, axis=0).astype(jnp.bfloat16)
            w1t[:, n * hidden : stop] = value[:, : stop - n * hidden]
        tops, ends = [], []
        for a in range(3):
            bands = []
            for b in range(3):
                band = None
                for c in range(3):
                    value = jnp.concatenate(
                        [tap_in(a, b, c), jnp.zeros((FIELD_ROWS, LANES), F32)], axis=0
                    )
                    value = pltpu.roll(value, c * channels, 0) if c else value
                    band = value if band is None else band + value
                bands.append(band)
            tops.append(two(bands[0], bands[1]))
            ends.append(bands[2])
        for start, parts in ((0, tops), (LANES, ends)):
            value = jnp.concatenate(parts + [jnp.zeros((LANES - 48, LANES), F32)], axis=0)
            value = jnp.transpose(value)[: min(LANES, 3 * hidden - start), :48]
            w1[start : start + value.shape[0], :] = value.astype(jnp.bfloat16)

    send(5)
    send(1)
    for load in loads[4:]:
        load.wait()
    prepare()
    receive(5, channels, fields)
    stacked(enter(fields[...].astype(jnp.bfloat16)), zx0)
    forward(zx0, z1s0, z2s0, 3, 2)
    send(2)

    receive(1, channels + 2, flow)
    place(lambda slots: arrived_both[slots, 0], channels, fields)
    velocity, shear = at(flow, 0), at(flow, 1)
    error = xs
    retreat(
        [at(flow, i, 2) for i in range(channels)], velocity, shear, channels, slope,
        put(error), put(carried),
    )
    begun = flow.at[2 * grid_x :]
    advance(
        lambda i: at(fields, i), velocity, shear, channels, slope, put(begun), lambda i: at(begun, i),
        lambda: receive(2, channels, sources), lambda i: at(sources, i), put(fields),
    )
    stacked(enter(fields[...].astype(jnp.bfloat16)), zx1)
    forward(zx1, z1s1, z2s1, 4, 3)
    backward(error, zx1, z1s1, z2s1, 4)
    leave(w1t, ze1, 4)
    send(4)
    send(3)

    def save(start, value):
        table[start : start + value.shape[0], :] = value

    gradients(zx1, z1s1, z2s1, save)
    receive(4, channels, sources)
    retreat(
        [at(carried, i) + at(sources, i) for i in range(channels)],
        velocity, shear, channels, slope, put(error), None,
    )
    backward(error, zx0, z1s0, z2s0, 3)

    def finish(start, value):
        wire[start : start + value.shape[0], :] = (
            table[start : start + value.shape[0], :] + value
        ).astype(WIRE)

    height = wire.shape[0]
    used = table.shape[0]
    if height > used:
        wire[used:, :] = jnp.zeros((height - used, LANES), WIRE)
    gradients(zx0, z1s0, z2s0, finish)

    pairs = total // 2
    chunk = height // total
    core = lax.rem(index_x, 2)
    half_x, half_at = count_x // 2, lax.div(index_x, 2)
    pair = index_y * half_x + half_at
    sibling = {"gx": half_at * 2 + 1 - core, "gy": index_y}

    def other_pair(k):
        shift_x, shift_y = apart(k, half_x)
        at_x = onward(half_at, shift_x, half_x)
        at_y = onward(index_y, shift_y, count_y)
        return at_y * half_x + at_x, {"gx": at_x * 2 + core, "gy": at_y}

    half = height // 2
    copy = pltpu.make_async_remote_copy(
        src_ref=wire.at[pl.ds(pl.multiple_of((1 - core) * half, 16), half)],
        dst_ref=from_core,
        send_sem=core_sems.at[0],
        recv_sem=core_sems.at[1],
        device_id=sibling,
        device_id_type=MESH,
    )
    copy.start()
    advance(
        lambda i: at(fields, i), velocity, shear, channels, slope, put(begun), lambda i: at(begun, i),
        lambda: receive(3, channels, sources), lambda i: at(sources, i), put(fields),
    )
    slot = index_y - origin_y
    tile = lax.div(slot, 2)
    for i in range(channels):
        value = fields[i * grid_x : (i + 1) * grid_x, pl.ds(pl.multiple_of(tile * LANES, LANES), LANES)]
        value = jnp.where(lax.rem(slot, 2) == 0, value, pltpu.roll(value, size_yz, 1))
        value = pltpu.roll(value, lax.rem(grid_x - (index_x - origin_x) * size_x, grid_x), 0)
        out_state[i] = value[:size_x, :size_yz]
    copy.wait()
    halved[...] = (
        wire[pl.ds(pl.multiple_of(core * half, 16), half), :].astype(F32)
        + from_core[...].astype(F32)
    ).astype(WIRE)

    def scatter(k):
        other, target = other_pair(k)
        return pltpu.make_async_remote_copy(
            src_ref=halved.at[pl.ds(pl.multiple_of(other * chunk, 16), chunk)],
            dst_ref=from_rest.at[k - 1],
            send_sem=rest_sems.at[0, k - 1],
            recv_sem=rest_sems.at[1, k - 1],
            device_id=target,
            device_id_type=MESH,
        )

    for_peers(pairs, lambda k: scatter(k).start())
    for_peers(pairs, lambda k: scatter(k).wait_recv())
    summed = halved[pl.ds(pl.multiple_of(pair * chunk, 16), chunk), :].astype(F32)
    for k in range(pairs - 1):
        summed = summed + from_rest[k].astype(F32)
    spot = pl.ds(pl.multiple_of(core * half + pair * chunk, 16), chunk)
    out_table[spot, :] = summed.astype(WIRE)

    def gather(k):
        other, target = other_pair(k)
        return pltpu.make_async_remote_copy(
            src_ref=out_table.at[spot],
            dst_ref=out_table.at[spot],
            send_sem=rest_sems.at[2, k - 1],
            recv_sem=rest_sems.at[3, k - 1],
            device_id=target,
            device_id_type=MESH,
        )

    for_peers(pairs, lambda k: gather(k).start())
    for_peers(pairs, lambda k: gather(k).wait_recv())
    side = pl.ds(pl.multiple_of(core * half, 16), half)
    copy = pltpu.make_async_remote_copy(
        src_ref=out_table.at[side],
        dst_ref=out_table.at[side],
        send_sem=core_sems.at[2],
        recv_sem=core_sems.at[3],
        device_id=sibling,
        device_id_type=MESH,
    )
    copy.start()
    copy.wait()
    for_peers(pairs, lambda k: scatter(k).wait_send())
    for_peers(pairs, lambda k: gather(k).wait_send())
    for turn in range(6):
        for k in range(len(shifts[turn])):
            remote(turn, k).wait_send()


def unpack_kernel(
    plan, state_ref, table_ref, out_state, grad_in, grad_mid, grad_out, name_mat, place_mat, turned
):
    channels, hidden = plan
    out_state[...] = state_ref[...]
    r, k = iota((48, 256), 0), iota((48, 256), 1)
    inner = r & 15
    side = steps_of(inner, channels, 3)
    for b in range(3):
        goal = (inner - channels * side) * 27 + shifted_by(r, 16) * 9 + b * 3 + side
        name_mat[b * 48 : (b + 1) * 48] = one_hot((inner < 3 * channels) & (goal == k))
    r, k = iota((16, LANES), 0), iota((16, LANES), 1)
    for b in range(3):
        place_mat[b * 16 : (b + 1) * 16] = one_hot(
            (r >= b * channels) & (r < (b + 1) * channels) & (k == r - b * channels + hidden)
        )

    deep = 9 * hidden
    folded = table_ref[deep : deep + deep // 2, :].astype(F32)
    behind = jnp.concatenate([folded, pltpu.roll(folded, hidden, 1)], axis=0)
    start = deep + deep // 2
    lead = table_ref[start : start + 48, :]
    start += 48
    parts = []
    for j in range(8 * hidden // LANES):
        parts.append(table_ref[start : start + 16, :])
        start += 16
    last = table_ref[start : start + 48, :]
    parts.append(pltpu.roll(last[:16].astype(F32), hidden, 1).astype(WIRE)[:, :hidden])
    trail = jnp.concatenate(parts, axis=1)
    contract = (((0,), (0,)), ((), ()))
    low = iota((hidden, LANES), 1) < hidden
    for b in range(3):
        placed = lax.dot_general(
            trail, place_mat[b * 16 : (b + 1) * 16], contract, preferred_element_type=F32
        )
        for n in range(9):
            rows_of = slice(n * hidden, (n + 1) * hidden)
            if b == 2:
                value = behind[rows_of]
            else:
                value = table_ref[rows_of, :].astype(F32)
                value = pltpu.roll(value, hidden, 1) if b == 1 else value
            turned[pl.ds((n // 3) * 9 + b * 3 + n % 3, hidden, stride=27), :] = (
                jnp.where(low, value, placed[rows_of])
            )
    long = grad_mid.shape[1]
    for start in range(0, long, LANES):
        size = min(LANES, long - start)
        value = jnp.transpose(turned[start : start + LANES, :])
        grad_mid[:, start : start + size] = value[:hidden, :size]
        grad_out[:, start : start + size] = value[hidden : hidden + channels, :size]
    named = [
        lax.dot_general(
            source, name_mat[b * 48 : (b + 1) * 48], contract, preferred_element_type=F32
        )
        for b, source in enumerate((lead, lead, last))
    ]
    value = named[0][:hidden] + named[1][hidden:] + named[2][:hidden]
    grad_in[...] = value[:, : grad_in.shape[1]]


def body(perturbation, mean_velocity, mean_shear, cotangent, kernel_in, kernel_mid, kernel_out):
    channels, size_x, size_yz = perturbation.shape
    hidden = kernel_in.shape[0]
    count_x, count_y = lax.axis_size("gx"), lax.axis_size("gy")
    total = count_x * count_y
    span_x, span_y = span_of(count_x, REACH_X)[0], span_of(count_y, REACH_Y)[0]
    held = span_x * span_y
    grid_x, grid_yz = span_x * size_x, span_y * size_yz
    planes = size_x + 2 * RIM
    operands = (
        perturbation, mean_velocity, mean_shear, cotangent, kernel_in, kernel_mid, kernel_out,
    )
    results = (perturbation,) + operands[4:]
    used = 1024
    unit = total * 16
    height = -(-used // unit) * unit
    deep, wide = 3 * hidden, size_x * LANES
    taps = -(-kernel_mid.shape[1] // LANES) * LANES
    b16 = jnp.bfloat16
    vmem = pltpu.VMEM
    scratch = [vmem(a.shape, a.dtype) for a in operands] + [
        vmem((5, BLOCK_ROWS, LANES), WIRE),
        vmem((6, held, BLOCK_ROWS, LANES), WIRE),
        vmem((held, 2, BLOCK_ROWS, LANES), WIRE),
        vmem((channels * grid_x, grid_yz), F32),
        vmem((channels * grid_x, grid_yz), F32),
        vmem(((channels + 2) * grid_x, grid_yz), F32),
        vmem((channels * grid_x, grid_yz), F32),
        vmem((planes * 16, LANES), b16),
        vmem((planes * 16, LANES), b16),
        vmem((planes * deep, LANES), b16),
        vmem((planes * deep, LANES), b16),
        vmem((planes * deep, LANES), b16),
        vmem((planes * deep, LANES), b16),
        vmem((planes * 16, LANES), b16),
        vmem((planes * deep, LANES), b16),
        vmem((planes * deep, LANES), b16),
        vmem((deep, wide), b16),
        vmem((deep, wide), b16),
        vmem((16, wide), b16),
        vmem((channels * grid_x, grid_yz), b16),
        vmem((2, BLOCK_ROWS, LANES), F32),
        vmem((LANES, taps + 2 * LANES), F32),
        vmem((taps + 2 * LANES, LANES), F32),
        vmem((deep, 48), b16),
        vmem((2 * LANES, 3 * deep), b16),
        vmem((deep, 48), b16),
        vmem((deep, 3 * deep), b16),
        vmem((32, 3 * deep), b16),
        vmem((2 * FIELD_ROWS * grid_x, 2 * span_x * BLOCK_ROWS), b16),
        vmem((grid_yz, LANES), b16),
        vmem((planes * 16, 3 * channels * grid_x), b16),
        vmem((2 * LANES, LANES), b16),
        vmem((used, LANES), F32),
        vmem((height, LANES), WIRE),
        vmem((height // 2, LANES), WIRE),
        vmem((height // 2, LANES), WIRE),
        vmem((total // 2 - 1, height // total, LANES), WIRE),
        pltpu.SemaphoreType.DMA((6, held - 1)),
        pltpu.SemaphoreType.DMA((6, held - 1)),
        pltpu.SemaphoreType.DMA((4,)),
        pltpu.SemaphoreType.DMA((4, total // 2 - 1)),
        pltpu.SemaphoreType.DMA((6,)),
        pltpu.SemaphoreType.DMA((len(operands),)),
    ]
    whole = pl.BlockSpec(memory_space=pltpu.VMEM)
    state, table = pl.pallas_call(
        functools.partial(whole_kernel, (count_x, count_y, channels, hidden, size_x, size_yz)),
        out_shape=[
            jax.ShapeDtypeStruct(perturbation.shape, F32),
            jax.ShapeDtypeStruct((height, LANES), WIRE),
        ],
        in_specs=[pl.BlockSpec(memory_space=pltpu.HBM)] * len(operands),
        out_specs=[whole] * 2,
        scratch_shapes=scratch,
        compiler_params=pltpu.CompilerParams(
            collective_id=0, has_side_effects=True, vmem_limit_bytes=56 * 2**20
        ),
    )(*operands)
    return tuple(
        pl.pallas_call(
            functools.partial(unpack_kernel, (channels, hidden)),
            out_shape=[jax.ShapeDtypeStruct(r.shape, F32) for r in results],
            in_specs=[whole] * 2,
            out_specs=[whole] * len(results),
            scratch_shapes=[
                vmem((3 * 48, 2 * LANES), b16),
                vmem((3 * 16, LANES), b16),
                vmem((taps, LANES), F32),
            ],
            compiler_params=pltpu.CompilerParams(vmem_limit_bytes=56 * 2**20),
        )(state, table)
    )


def solution(mesh):
    return jax.shard_map(
        body,
        mesh=mesh,
        in_specs=(
            P(None, "gx", "gy"),
            P("gx", "gy"),
            P("gx", "gy"),
            P(None, "gx", "gy"),
            P(),
            P(),
            P(),
        ),
        out_specs=(P(None, "gx", "gy"), P(), P(), P()),
        check_vma=False,
    )
```

```python
import functools
import math

import jax
import jax.numpy as jnp
from jax import lax
from jax.experimental import pallas as pl
from jax.experimental.pallas import tpu as pltpu
from jax.sharding import PartitionSpec as P

NZ = 8
LANES = 128
FIELD_ROWS = 8
BLOCK_ROWS = 2 * FIELD_ROWS
RIM = 4
REACH_X = 5
REACH_Y = 3
NEAR, FIRST_SOURCE, LAST_SOURCE = 3, 15, 8

TIME_STEP = 0.25
STENCIL_WEIGHTS = (0.75, -0.15, 1.0 / 60.0)
MESH = pl.DeviceIdType.MESH
WIRE = jnp.bfloat16
F32 = jnp.float32


def dot(a, b):
    return lax.dot_general(a, b, (((1,), (0,)), ((), ())), preferred_element_type=F32)


def dot_nt(a, b):
    return lax.dot_general(a, b, (((1,), (1,)), ((), ())), preferred_element_type=F32)


def iota(shape, axis):
    return lax.broadcasted_iota(jnp.int32, shape, axis)


def shifted_by(values, size):
    return lax.shift_right_logical(values, size.bit_length() - 1)


def steps_of(values, size, count):
    return sum((values >= size * n).astype(jnp.int32) for n in range(1, count))


def one_hot(condition):
    return jnp.where(condition, 1.0, 0.0).astype(jnp.bfloat16)


def span_of(count, reach):
    span = min(count, 2 * reach + 2)
    return span, span // 2


def slopes(origin_x, origin_yz, grid_x, grid_yz, shape):
    row = iota(shape, 0) + origin_x
    lane = iota(shape, 1) + origin_yz
    depth = lane & (NZ - 1)

    def moved(field, offset, axis):
        return pltpu.roll(field, (-offset) % field.shape[axis], axis)

    def edged(field, axis, position, unit):
        size = (grid_x, grid_yz)[axis]
        result = None
        for offset, weight in zip((1, 2, 3), STENCIL_WEIGHTS):
            step = offset * unit
            upper = jnp.where(position < size - step, moved(field, step, axis), 0.0)
            lower = jnp.where(position >= step, moved(field, -step, axis), 0.0)
            contrib = weight * (upper - lower)
            result = contrib if result is None else result + contrib
        return result

    def along_x(field):
        return edged(field, 0, row, 1)

    def along_y(field):
        return edged(field, 1, lane, NZ)

    def along_z(field):
        result = None
        for offset, weight in zip((1, 2, 3), STENCIL_WEIGHTS):
            upper = jnp.where(
                depth < NZ - offset, moved(field, offset, 1), moved(field, offset - NZ, 1)
            )
            lower = jnp.where(depth >= offset, moved(field, -offset, 1), moved(field, NZ - offset, 1))
            contrib = weight * (upper - lower)
            result = contrib if result is None else result + contrib
        return result

    return along_x, along_y, along_z


def advance(now, velocity, shear, source, channels, slope, write):
    fields = range(channels)
    dx, dy, dz = slope

    def rates(f):
        across = [dx(c) for c in f]
        divergence = across[1] + dy(f[2]) + dz(f[3])
        return (
            -velocity * across[0] - divergence,
            -velocity * across[1] - shear * f[2] - across[4],
            -velocity * across[2] - dy(f[4]),
            -velocity * across[3] - dz(f[4]),
            -velocity * across[4] - divergence,
        )

    rate = rates([now(i) for i in fields])
    one = [now(i) + TIME_STEP * (rate[i] + source(i)) for i in fields]
    rate = rates(one)
    two = [0.75 * now(i) + 0.25 * (one[i] + TIME_STEP * (rate[i] + source(i))) for i in fields]
    rate = rates(two)
    for i in fields:
        write(i, 1.0 / 3.0 * now(i) + 2.0 / 3.0 * (two[i] + TIME_STEP * (rate[i] + source(i))))


def retreat(last, velocity, shear, channels, slope, write_error, write_carried):
    fields = range(channels)
    dx, dy, dz = slope

    def rates(g):
        acoustic = g[0] + g[4]
        return (
            dx(velocity * g[0]),
            dx(velocity * g[1] + acoustic),
            dx(velocity * g[2]) - shear * g[1] + dy(acoustic),
            dx(velocity * g[3]) + dz(acoustic),
            dx(velocity * g[4] + g[1]) + dy(g[2]) + dz(g[3]),
        )

    rate = rates(last)
    second = [2.0 / 3.0 * last[i] + 2.0 / 3.0 * TIME_STEP * rate[i] for i in fields]
    rate = rates(second)
    first = [0.25 * second[i] + 0.25 * TIME_STEP * rate[i] for i in fields]
    for i in fields:
        write_error(i, TIME_STEP * (2.0 / 3.0 * last[i] + 0.25 * second[i] + first[i]))
    if write_carried is None:
        return
    rate = rates(first)
    for i in fields:
        write_carried(i, 1.0 / 3.0 * last[i] + 0.75 * second[i] + first[i] + TIME_STEP * rate[i])


def for_peers(total, body):
    lax.fori_loop(1, total, lambda k, c: (body(k), c)[1], 0, unroll=total <= 32)


def whole_kernel(
    plan, state_from, velocity_from, shear_from, cotangent_from, in_from, mid_from, out_from,
    out_state, out_table,
    state_ref, velocity_ref, shear_ref, cotangent_ref, kernel_in, kernel_mid, kernel_out,
    block, arrived, fields, sources, flow, carried, zx0, zx1, z1s0, z1s1, z2s0, z2s1, zin, ze2, ze1,
    e1s, e2s, e3s, xs, packs, laid, turned_kernels, w1, w23, w3t, w2t, w1t, spread_mat, enter_mat, pick_mat, leave_mat, table, wire, from_core, halved, from_rest,
    send_sems, recv_sems, core_sems, rest_sems, pass_sems, own_sems, load_sems,
):
    count_x, count_y, channels, hidden, size_x, size_yz = plan
    total = count_x * count_y
    span_x, lead_x = span_of(count_x, REACH_X)
    span_y, lead_y = span_of(count_y, REACH_Y)
    held = span_x * span_y
    all_x, all_y = count_x * size_x, count_y * size_yz // NZ
    grid_x, grid_yz = span_x * size_x, span_y * size_yz
    size_y = size_yz // NZ
    width = size_y + 2 * RIM
    planes = size_x + 2 * RIM
    index_x, index_y = lax.axis_index("gx"), lax.axis_index("gy")
    me = index_y * count_x + index_x
    origin_x = 0 if span_x == count_x else index_x - lead_x
    origin_y = 0 if span_y == count_y else index_y - lead_y
    tiles = grid_yz // LANES
    tile_rows = 2 * span_x * BLOCK_ROWS
    flat = channels * grid_x

    def device(place):
        return {"gx": lax.rem(place, count_x), "gy": lax.div(place, count_x)}

    loads = [
        pltpu.make_async_copy(source, target, load_sems.at[n])
        for n, (source, target) in enumerate(
            (
                (state_from, state_ref),
                (velocity_from, velocity_ref),
                (shear_from, shear_ref),
                (cotangent_from, cotangent_ref),
                (in_from, kernel_in),
                (mid_from, kernel_mid),
                (out_from, kernel_out),
            )
        )
    ]
    for load in loads:
        load.start()
    arrived[...] = jnp.zeros(arrived.shape, WIRE)
    barrier = pltpu.get_barrier_semaphore()
    for_peers(
        total,
        lambda k: pl.semaphore_signal(
            barrier, inc=1, device_id=device(lax.rem(me + k, total)), device_id_type=MESH
        ),
    )

    rows = FIELD_ROWS * grid_x
    r, k = iota((rows, tile_rows), 0), iota((rows, tile_rows), 1)
    field = steps_of(r, grid_x, FIELD_ROWS)
    at_x = r - field * grid_x
    part = steps_of(k, tile_rows // 2, 2)
    rest = k - part * (tile_rows // 2)
    owner = shifted_by(rest, BLOCK_ROWS)
    inner = rest & (BLOCK_ROWS - 1)
    odd = at_x & 1
    row = (shifted_by(at_x, 2) & 1) * FIELD_ROWS + field
    same = (owner == shifted_by(at_x, size_x)) & (inner == row)
    spread_mat[:rows] = one_hot(same & (part == odd))
    spread_mat[rows:] = one_hot(same & (part != odd))
    r, k = iota((grid_yz, LANES), 0), iota((grid_yz, LANES), 1)
    enter_mat[...] = one_hot(
        ((r & (NZ - 1)) == shifted_by(k, width))
        & (shifted_by(r, NZ) + origin_y * size_y == index_y * size_y - RIM + (k & (width - 1)))
        & (shifted_by(r, NZ) + origin_y * size_y >= 0)
        & (shifted_by(r, NZ) + origin_y * size_y < all_y)
    )
    r, k = iota((planes * 16, 3 * flat), 0), iota((planes * 16, 3 * flat), 1)
    inner = r & 15
    side = steps_of(inner, channels, 3)
    part = steps_of(k, flat, 3)
    rest = k - part * flat
    field = steps_of(rest, grid_x, channels)
    pick_mat[...] = one_hot(
        (inner < 3 * channels)
        & (part == side)
        & (field == inner - channels * side)
        & (
            rest - field * grid_x + origin_x * size_x
            == index_x * size_x - RIM + shifted_by(r, 16)
        )
        & (rest - field * grid_x + origin_x * size_x >= 0)
        & (rest - field * grid_x + origin_x * size_x < all_x)
    )
    r, k = iota((2 * LANES, LANES), 0), iota((2 * LANES, LANES), 1)
    inner, lane = r & (LANES - 1), k & (size_yz - 1)
    leave_mat[...] = one_hot(
        (shifted_by(r, LANES) == steps_of(k, size_yz, 2))
        & (shifted_by(inner, width) == (lane & (NZ - 1)))
        & ((inner & (width - 1)) == shifted_by(lane, NZ) + RIM)
    )
    place = iota((8, LANES), 1) & (width - 1)
    at_y = place + (index_y * size_y - RIM)
    valid_y = jnp.where((at_y >= 0) & (at_y < all_y), 1.0, 0.0)
    mine = jnp.where((place >= RIM) & (place < RIM + size_y), 1.0, 0.0)

    def inside(p):
        at = index_x * size_x - RIM + p
        scale = jnp.where((at >= 0) & (at < all_x), 1.0, 0.0).astype(F32)
        return (valid_y * scale)[:1]

    def pack(turn, rows_of):
        packs[...] = jnp.zeros(packs.shape, F32)
        for f, at_row in enumerate(rows_of):
            for x in range(size_x):
                spot = (x // 2) * FIELD_ROWS + f
                packs[x % 2, spot : spot + 1, :size_yz] = at_row(x)
        block[turn] = (packs[0] + pltpu.roll(packs[1], size_yz, 1)).astype(WIRE)

    for load in loads[:4]:
        load.wait()
    pack(0, [lambda x, f=f: state_ref[f, x : x + 1, :] for f in range(channels)])
    scale = 1.0 / math.sqrt(total * size_x * size_yz)
    pack(
        1,
        [lambda x: velocity_ref[x : x + 1, :], lambda x: shear_ref[x : x + 1, :]]
        + [lambda x, f=f: cotangent_ref[f, x : x + 1, :] * scale for f in range(channels)],
    )
    pl.semaphore_wait(barrier, total - 1)

    own_slot = (index_y - origin_y) * span_x + index_x - origin_x

    def around(cells):
        reach_x, reach_y = -(-cells // size_x), -(-cells // size_y)
        return [
            (x, y)
            for y in range(-lead_y, span_y - lead_y)
            for x in range(-lead_x, span_x - lead_x)
            if abs(x) <= reach_x and abs(y) <= reach_y and (x or y)
        ]

    everyone = around(max(all_x, all_y))
    near = around(NEAR)
    shifts = [
        [shift for shift in everyone if shift not in near],
        everyone,
        around(FIRST_SOURCE),
        around(LAST_SOURCE),
        around(LAST_SOURCE),
        near,
    ]

    def remote(turn, k):
        shift_x, shift_y = shifts[turn][k]
        slot_x = index_x if span_x == count_x else lead_x - shift_x
        slot_y = index_y if span_y == count_y else lead_y - shift_y
        return pltpu.make_async_remote_copy(
            src_ref=block.at[turn % 5],
            dst_ref=arrived.at[turn, slot_y * span_x + slot_x],
            send_sem=send_sems.at[turn, k],
            recv_sem=recv_sems.at[turn, k],
            device_id={
                "gx": lax.rem(index_x + shift_x + count_x, count_x),
                "gy": lax.rem(index_y + shift_y + count_y, count_y),
            },
            device_id_type=MESH,
        )

    def keep_own(turn):
        return pltpu.make_async_copy(
            block.at[turn % 5], arrived.at[turn, own_slot], own_sems.at[turn]
        )

    def send(turn):
        for k in range(len(shifts[turn])):
            remote(turn, k).start()
        if turn > 0:
            keep_own(turn).start()

    def receive(turn, number, target):
        for k in range(len(shifts[turn])):
            remote(turn, k).wait_recv()
        if turn > 0:
            keep_own(turn).wait()
        height = number * grid_x
        half = steps_of(iota((height, LANES), 1), size_yz, 2)
        keep = half == (iota((height, LANES), 0) & 1)
        matrix = jnp.concatenate([spread_mat[:height], spread_mat[rows : rows + height]], axis=0)
        for t in range(tiles):
            slots = arrived[turn, t * 2 * span_x : (t + 1) * 2 * span_x].reshape(tile_rows, LANES)
            both = dot(matrix, slots)
            value = jnp.where(keep, both[:height], pltpu.roll(both[height:], size_yz, 1))
            part = slice(t * LANES, (t + 1) * LANES)
            if turn == 0:
                value = value + target[:height, part]
            target[:height, part] = value

    def at(ref, i, start=0):
        return ref[(start + i) * grid_x : (start + i + 1) * grid_x, :]

    def put(ref):
        def write(i, value):
            ref[i * grid_x : (i + 1) * grid_x, :] = value.astype(ref.dtype)

        return write

    def enter(values):
        return dot(values, enter_mat[...])

    def stacked(window, target):
        three = jnp.concatenate(
            [pltpu.roll(window, width, 1), window, pltpu.roll(window, LANES - width, 1)], axis=0
        )
        target[...] = dot(pick_mat[...], three.astype(jnp.bfloat16)).astype(jnp.bfloat16)

    def conv(weights, outs, source, unit, first, count, emit):
        matrix = weights[...]
        for p in range(first, first + count, 2):
            columns = jnp.concatenate(
                [source[(p - 1 + q) * unit : (p + 2 + q) * unit, :] for q in (0, 1)], axis=1
            )
            product = dot(matrix, columns)
            for q in (0, 1):
                part = product[:, q * LANES : (q + 1) * LANES]
                emit(
                    p + q,
                    pltpu.roll(part[:outs], 1, 1)
                    + part[outs : 2 * outs]
                    + pltpu.roll(part[2 * outs : 3 * outs], LANES - 1, 1),
                )

    def store_stack(target, p, value):
        base = p * 3 * hidden
        for c, turned in enumerate((width, 0, LANES - width)):
            moved = pltpu.roll(value, turned, 1) if turned else value
            target[base + c * hidden : base + (c + 1) * hidden, :] = moved.astype(jnp.bfloat16)

    def middle(source, p):
        return source[(3 * p + 1) * hidden : (3 * p + 2) * hidden, :].astype(F32)

    def store_error(target, p, value):
        if not RIM <= p < RIM + size_x:
            return
        kept = value * mine[:1]
        for b, turned in enumerate((LANES - 1, 0, 1)):
            moved = pltpu.roll(kept, turned, 1) if turned else kept
            target[
                b * hidden : (b + 1) * hidden, (p - RIM) * LANES : (p - RIM + 1) * LANES
            ] = moved.astype(jnp.bfloat16)

    def forward(zx, z1, z2, margin, turn):
        conv(
            w1, hidden, zx, 16, RIM - margin + 1, size_x + 2 * margin - 2,
            lambda p, v: store_stack(z1, p, jnp.tanh(v) * inside(p)),
        )
        conv(
            w23.at[: 3 * hidden], hidden, z1, 3 * hidden, RIM - margin + 2, size_x + 2 * margin - 4,
            lambda p, v: store_stack(z2, p, jnp.tanh(v) * inside(p)),
        )
        leave(w23.at[3 * hidden : 3 * hidden + 32], z2, turn)

    def leave(weights, source, turn):
        kept = {}
        conv(
            weights, FIELD_ROWS, source, 3 * hidden, RIM, size_x, lambda p, v: kept.update({p - RIM: v}),
        )
        sides = [
            jnp.concatenate([kept[q + 2 * i] for i in range(size_x // 2)], axis=0) for q in (0, 1)
        ]
        both = jnp.concatenate(sides, axis=1).astype(jnp.bfloat16)
        block[turn] = dot(both, leave_mat[...]).astype(WIRE)

    def backward(ref, zx, z1, z2, margin):
        window = enter(ref[...])
        stacked(window, zin)
        kept = window * mine[:1]
        three = jnp.concatenate(
            [pltpu.roll(kept, LANES - 1, 1), kept, pltpu.roll(kept, 1, 1)], axis=0
        )
        own = dot(
            pick_mat[RIM * 16 : (RIM + size_x) * 16, :], three.astype(jnp.bfloat16)
        ).astype(jnp.bfloat16)
        for p in range(size_x):
            e3s[:, p * LANES : (p + 1) * LANES] = own[p * 16 : (p + 1) * 16]
        span = margin - 2

        def second(p, v):
            slope = 1.0 - jnp.square(middle(z2, p))
            value = v * slope * inside(p)
            store_stack(ze2, p, value)
            store_error(e2s, p, value)

        def first(p, v):
            slope = 1.0 - jnp.square(middle(z1, p))
            value = v * slope * inside(p)
            if span > 1:
                store_stack(ze1, p, value)
            store_error(e1s, p, value)

        conv(w3t, hidden, zin, 16, RIM - span, size_x + 2 * span, second)
        conv(w2t, hidden, ze2, 3 * hidden, RIM - span + 1, size_x + 2 * span - 2, first)

    def gradients(zx, z1, z2, save):
        def wide(source, unit, low, high):
            return jnp.concatenate(
                [
                    source[(RIM + p - 1) * unit + low : (RIM + p - 1) * unit + high, :]
                    for p in range(size_x)
                ],
                axis=1,
            )

        deep = 9 * hidden
        zero = jnp.zeros((hidden, size_x * LANES), jnp.bfloat16)
        e2 = e2s[...]
        values = wide(z1, 3 * hidden, 0, deep)
        save(0, dot_nt(values, e2[: 2 * hidden]))
        last = e2[2 * hidden :]
        save(
            deep,
            dot_nt(values[: deep // 2], jnp.concatenate([last, zero], axis=0))
            + dot_nt(values[deep // 2 :], jnp.concatenate([zero, last], axis=0)),
        )
        start = deep + deep // 2
        e1 = e1s[...]
        values = wide(zx, 16, 0, 48)
        save(start, dot_nt(values, e1[: 2 * hidden]))
        start += 48
        tail = dot_nt(values, jnp.concatenate([e1[2 * hidden :], zero], axis=0))
        e3 = e3s[...]
        product = dot_nt(e3, wide(z2, 3 * hidden, 0, 8 * hidden))
        for j in range(8 * hidden // LANES):
            save(start, product[:, j * LANES : (j + 1) * LANES])
            start += 16
        late = dot_nt(
            e3, jnp.concatenate([zero, wide(z2, 3 * hidden, 8 * hidden, deep)], axis=0)
        )
        save(start, tail[:16] + late)
        save(start + 16, tail[16:])

    slope = slopes(
        origin_x * size_x, origin_y * size_yz, all_x, all_y * NZ, (grid_x, grid_yz)
    )
    def prepare():
        first_in = turned_kernels.shape[0] - 2 * LANES
        long = kernel_mid.shape[1]
        laid[hidden:, :] = jnp.zeros((laid.shape[0] - hidden, laid.shape[1]), F32)
        laid[:hidden, long // LANES * LANES :] = jnp.zeros(
            (hidden, laid.shape[1] - long // LANES * LANES), F32
        )
        laid[:hidden, :long] = kernel_mid[...].astype(F32)
        laid[hidden : hidden + channels, :long] = kernel_out[...].astype(F32)
        laid[:hidden, first_in : first_in + kernel_in.shape[1]] = kernel_in[...].astype(F32)
        for j in range(laid.shape[1] // LANES):
            part = slice(j * LANES, (j + 1) * LANES)
            turned_kernels[part, :] = jnp.transpose(laid[:, part])
        lane = iota((hidden, LANES), 1)
        low = lane < hidden

        def tap(a, b, c):
            return turned_kernels[pl.ds(a * 9 + b * 3 + c, hidden, stride=27), :]

        def tap_in(a, b, c):
            return turned_kernels[pl.ds(first_in + a * 9 + b * 3 + c, FIELD_ROWS, stride=27), :]

        def two(left, right):
            return jnp.where(
                iota(left.shape, 1) < hidden, left, pltpu.roll(right, hidden, 1)
            )

        empty = jnp.zeros((hidden, LANES), F32)
        for n in range(0, 9, 2):
            tops, ends = [], []
            for m in (n, n + 1):
                if m > 8:
                    tops.append(empty)
                    ends.append(empty)
                    continue
                taps = [tap(m // 3, b, m % 3) for b in range(3)]
                tops.append(two(taps[0], taps[1]))
                late = jnp.where(
                    lane < hidden + 8,
                    taps[0],
                    jnp.where(
                        lane < hidden + 16,
                        pltpu.roll(taps[1], 8, 1),
                        jnp.where(lane < hidden + 24, pltpu.roll(taps[2], 16, 1), 0.0),
                    ),
                )
                ends.append(jnp.where(low, taps[2], late))
            stop = min((n + 2) * hidden, 9 * hidden)
            for start, halves in ((0, tops), (LANES, ends)):
                value = jnp.transpose(jnp.concatenate(halves, axis=0)).astype(jnp.bfloat16)
                w23[start : start + LANES, n * hidden : stop] = value[:, : stop - n * hidden]
        for b in range(3):
            for n in range(0, 9, 2):
                ours = [tap(2 - m // 3, 2 - b, 2 - m % 3) for m in range(n, min(n + 2, 9))]
                value = two(*ours) if len(ours) == 2 else ours[0][:, :hidden]
                w2t[b * hidden : (b + 1) * hidden, n * hidden : n * hidden + value.shape[1]] = (
                    value.astype(jnp.bfloat16)
                )
            placed = None
            for m in range(9):
                value = jnp.where(low, 0.0, tap(2 - m // 3, 2 - b, 2 - m % 3))
                goal = (m // 3) * 16 + (m % 3) * channels
                value = pltpu.roll(value, (goal - hidden) % LANES, 1)
                placed = value if placed is None else placed + value
            w3t[b * hidden : (b + 1) * hidden, :] = placed[:, :48].astype(jnp.bfloat16)
        for n in range(0, 9, 2):
            bands = []
            for b in range(3):
                ours = [tap_in(2 - m // 3, 2 - b, 2 - m % 3) for m in range(n, min(n + 2, 9))]
                bands.append(two(*ours) if len(ours) == 2 else ours[0])
            bands.append(jnp.zeros((FIELD_ROWS, LANES), F32))
            stop = min((n + 2) * hidden, 9 * hidden)
            value = jnp.concatenate(bands, axis=0).astype(jnp.bfloat16)
            w1t[:, n * hidden : stop] = value[:, : stop - n * hidden]
        tops, ends = [], []
        for a in range(3):
            bands = []
            for b in range(3):
                band = None
                for c in range(3):
                    value = jnp.concatenate(
                        [tap_in(a, b, c), jnp.zeros((FIELD_ROWS, LANES), F32)], axis=0
                    )
                    value = pltpu.roll(value, c * channels, 0) if c else value
                    band = value if band is None else band + value
                bands.append(band)
            tops.append(two(bands[0], bands[1]))
            ends.append(bands[2])
        for start, parts in ((0, tops), (LANES, ends)):
            value = jnp.concatenate(parts + [jnp.zeros((LANES - 48, LANES), F32)], axis=0)
            value = jnp.transpose(value)[: min(LANES, 3 * hidden - start), :48]
            w1[start : start + value.shape[0], :] = value.astype(jnp.bfloat16)

    send(5)
    send(1)
    send(0)
    for load in loads[4:]:
        load.wait()
    prepare()
    receive(5, channels, fields)
    stacked(enter(fields[...].astype(jnp.bfloat16)), zx0)
    forward(zx0, z1s0, z2s0, 3, 2)
    send(2)

    receive(0, channels, fields)
    receive(1, channels + 2, flow)
    velocity, shear = at(flow, 0), at(flow, 1)
    error = xs
    retreat(
        [at(flow, i, 2) for i in range(channels)], velocity, shear, channels, slope,
        put(error), put(carried),
    )
    receive(2, channels, sources)
    advance(
        lambda i: at(fields, i), velocity, shear, lambda i: at(sources, i), channels, slope,
        put(fields),
    )
    stacked(enter(fields[...].astype(jnp.bfloat16)), zx1)
    forward(zx1, z1s1, z2s1, 4, 3)
    backward(error, zx1, z1s1, z2s1, 4)
    leave(w1t, ze1, 4)
    send(4)
    send(3)

    def save(start, value):
        table[start : start + value.shape[0], :] = value

    gradients(zx1, z1s1, z2s1, save)
    receive(4, channels, sources)
    retreat(
        [at(carried, i) + at(sources, i) for i in range(channels)],
        velocity, shear, channels, slope, put(error), None,
    )
    backward(error, zx0, z1s0, z2s0, 3)

    def finish(start, value):
        wire[start : start + value.shape[0], :] = (
            table[start : start + value.shape[0], :] + value
        ).astype(WIRE)

    height = wire.shape[0]
    used = table.shape[0]
    if height > used:
        wire[used:, :] = jnp.zeros((height - used, LANES), WIRE)
    gradients(zx0, z1s0, z2s0, finish)

    pairs = total // 2
    chunk = height // total
    core = lax.rem(index_x, 2)
    pair = index_y * (count_x // 2) + lax.div(index_x, 2)

    def at_pair(place, side):
        return {
            "gx": lax.rem(place, count_x // 2) * 2 + side, "gy": lax.div(place, count_x // 2)
        }

    half = height // 2
    copy = pltpu.make_async_remote_copy(
        src_ref=wire.at[pl.ds(pl.multiple_of((1 - core) * half, 16), half)],
        dst_ref=from_core,
        send_sem=core_sems.at[0],
        recv_sem=core_sems.at[1],
        device_id=at_pair(pair, 1 - core),
        device_id_type=MESH,
    )
    copy.start()
    receive(3, channels, sources)
    advance(
        lambda i: at(fields, i), velocity, shear, lambda i: at(sources, i), channels, slope,
        put(fields),
    )
    slot = index_y - origin_y
    tile = lax.div(slot, 2)
    for i in range(channels):
        value = fields[i * grid_x : (i + 1) * grid_x, pl.ds(pl.multiple_of(tile * LANES, LANES), LANES)]
        value = jnp.where(lax.rem(slot, 2) == 0, value, pltpu.roll(value, size_yz, 1))
        value = pltpu.roll(value, lax.rem(grid_x - (index_x - origin_x) * size_x, grid_x), 0)
        out_state[i] = value[:size_x, :size_yz]
    copy.wait()
    halved[...] = (
        wire[pl.ds(pl.multiple_of(core * half, 16), half), :].astype(F32)
        + from_core[...].astype(F32)
    ).astype(WIRE)

    def scatter(k):
        other = lax.rem(pair + k, pairs)
        return pltpu.make_async_remote_copy(
            src_ref=halved.at[pl.ds(pl.multiple_of(other * chunk, 16), chunk)],
            dst_ref=from_rest.at[k - 1],
            send_sem=rest_sems.at[0, k - 1],
            recv_sem=rest_sems.at[1, k - 1],
            device_id=at_pair(other, core),
            device_id_type=MESH,
        )

    for_peers(pairs, lambda k: scatter(k).start())
    for_peers(pairs, lambda k: scatter(k).wait_recv())
    summed = halved[pl.ds(pl.multiple_of(pair * chunk, 16), chunk), :].astype(F32)
    for k in range(pairs - 1):
        summed = summed + from_rest[k].astype(F32)
    spot = pl.ds(pl.multiple_of(core * half + pair * chunk, 16), chunk)
    out_table[spot, :] = summed.astype(WIRE)

    def gather(k):
        other = lax.rem(pair + k, pairs)
        return pltpu.make_async_remote_copy(
            src_ref=out_table.at[spot],
            dst_ref=out_table.at[spot],
            send_sem=rest_sems.at[2, k - 1],
            recv_sem=rest_sems.at[3, k - 1],
            device_id=at_pair(other, core),
            device_id_type=MESH,
        )

    def forward_part(k):
        source = lax.rem(pair + pairs - k, pairs)
        part = pl.ds(pl.multiple_of(core * half + source * chunk, 16), chunk)
        return pltpu.make_async_remote_copy(
            src_ref=out_table.at[part],
            dst_ref=out_table.at[part],
            send_sem=pass_sems.at[0, k],
            recv_sem=pass_sems.at[1, k],
            device_id=at_pair(pair, 1 - core),
            device_id_type=MESH,
        )

    def pass_on(k):
        gather(k).wait_recv()
        forward_part(k).start()

    for_peers(pairs, lambda k: gather(k).start())
    forward_part(0).start()
    for_peers(pairs, pass_on)
    forward_part(0).wait()
    for_peers(pairs, lambda k: forward_part(k).wait())
    for_peers(pairs, lambda k: scatter(k).wait_send())
    for_peers(pairs, lambda k: gather(k).wait_send())
    for turn in range(6):
        for k in range(len(shifts[turn])):
            remote(turn, k).wait_send()


def unpack_kernel(
    plan, state_ref, table_ref, out_state, grad_in, grad_mid, grad_out, name_mat, place_mat, turned
):
    channels, hidden = plan
    out_state[...] = state_ref[...]
    r, k = iota((48, 256), 0), iota((48, 256), 1)
    inner = r & 15
    side = steps_of(inner, channels, 3)
    for b in range(3):
        goal = (inner - channels * side) * 27 + shifted_by(r, 16) * 9 + b * 3 + side
        name_mat[b * 48 : (b + 1) * 48] = one_hot((inner < 3 * channels) & (goal == k))
    r, k = iota((16, LANES), 0), iota((16, LANES), 1)
    for b in range(3):
        place_mat[b * 16 : (b + 1) * 16] = one_hot(
            (r >= b * channels) & (r < (b + 1) * channels) & (k == r - b * channels + hidden)
        )

    deep = 9 * hidden
    folded = table_ref[deep : deep + deep // 2, :].astype(F32)
    behind = jnp.concatenate([folded, pltpu.roll(folded, hidden, 1)], axis=0)
    start = deep + deep // 2
    lead = table_ref[start : start + 48, :]
    start += 48
    parts = []
    for j in range(8 * hidden // LANES):
        parts.append(table_ref[start : start + 16, :])
        start += 16
    last = table_ref[start : start + 48, :]
    parts.append(pltpu.roll(last[:16].astype(F32), hidden, 1).astype(WIRE)[:, :hidden])
    trail = jnp.concatenate(parts, axis=1)
    contract = (((0,), (0,)), ((), ()))
    low = iota((hidden, LANES), 1) < hidden
    for b in range(3):
        placed = lax.dot_general(
            trail, place_mat[b * 16 : (b + 1) * 16], contract, preferred_element_type=F32
        )
        for n in range(9):
            rows_of = slice(n * hidden, (n + 1) * hidden)
            if b == 2:
                value = behind[rows_of]
            else:
                value = table_ref[rows_of, :].astype(F32)
                value = pltpu.roll(value, hidden, 1) if b == 1 else value
            turned[pl.ds((n // 3) * 9 + b * 3 + n % 3, hidden, stride=27), :] = (
                jnp.where(low, value, placed[rows_of])
            )
    long = grad_mid.shape[1]
    for start in range(0, long, LANES):
        size = min(LANES, long - start)
        value = jnp.transpose(turned[start : start + LANES, :])
        grad_mid[:, start : start + size] = value[:hidden, :size]
        grad_out[:, start : start + size] = value[hidden : hidden + channels, :size]
    named = [
        lax.dot_general(
            source, name_mat[b * 48 : (b + 1) * 48], contract, preferred_element_type=F32
        )
        for b, source in enumerate((lead, lead, last))
    ]
    value = named[0][:hidden] + named[1][hidden:] + named[2][:hidden]
    grad_in[...] = value[:, : grad_in.shape[1]]


def body(perturbation, mean_velocity, mean_shear, cotangent, kernel_in, kernel_mid, kernel_out):
    channels, size_x, size_yz = perturbation.shape
    hidden = kernel_in.shape[0]
    count_x, count_y = lax.axis_size("gx"), lax.axis_size("gy")
    total = count_x * count_y
    span_x, span_y = span_of(count_x, REACH_X)[0], span_of(count_y, REACH_Y)[0]
    held = span_x * span_y
    grid_x, grid_yz = span_x * size_x, span_y * size_yz
    planes = size_x + 2 * RIM
    operands = (
        perturbation, mean_velocity, mean_shear, cotangent, kernel_in, kernel_mid, kernel_out,
    )
    results = (perturbation,) + operands[4:]
    used = 1024
    unit = total * 16
    height = -(-used // unit) * unit
    deep, wide = 3 * hidden, size_x * LANES
    taps = -(-kernel_mid.shape[1] // LANES) * LANES
    b16 = jnp.bfloat16
    vmem = pltpu.VMEM
    scratch = [vmem(a.shape, a.dtype) for a in operands] + [
        vmem((5, BLOCK_ROWS, LANES), WIRE),
        vmem((6, held, BLOCK_ROWS, LANES), WIRE),
        vmem((channels * grid_x, grid_yz), F32),
        vmem((channels * grid_x, grid_yz), F32),
        vmem(((channels + 2) * grid_x, grid_yz), F32),
        vmem((channels * grid_x, grid_yz), F32),
        vmem((planes * 16, LANES), b16),
        vmem((planes * 16, LANES), b16),
        vmem((planes * deep, LANES), b16),
        vmem((planes * deep, LANES), b16),
        vmem((planes * deep, LANES), b16),
        vmem((planes * deep, LANES), b16),
        vmem((planes * 16, LANES), b16),
        vmem((planes * deep, LANES), b16),
        vmem((planes * deep, LANES), b16),
        vmem((deep, wide), b16),
        vmem((deep, wide), b16),
        vmem((16, wide), b16),
        vmem((channels * grid_x, grid_yz), b16),
        vmem((2, BLOCK_ROWS, LANES), F32),
        vmem((LANES, taps + 2 * LANES), F32),
        vmem((taps + 2 * LANES, LANES), F32),
        vmem((deep, 48), b16),
        vmem((2 * LANES, 3 * deep), b16),
        vmem((deep, 48), b16),
        vmem((deep, 3 * deep), b16),
        vmem((32, 3 * deep), b16),
        vmem((2 * FIELD_ROWS * grid_x, 2 * span_x * BLOCK_ROWS), b16),
        vmem((grid_yz, LANES), b16),
        vmem((planes * 16, 3 * channels * grid_x), b16),
        vmem((2 * LANES, LANES), b16),
        vmem((used, LANES), F32),
        vmem((height, LANES), WIRE),
        vmem((height // 2, LANES), WIRE),
        vmem((height // 2, LANES), WIRE),
        vmem((total // 2 - 1, height // total, LANES), WIRE),
        pltpu.SemaphoreType.DMA((6, held - 1)),
        pltpu.SemaphoreType.DMA((6, held - 1)),
        pltpu.SemaphoreType.DMA((4,)),
        pltpu.SemaphoreType.DMA((4, total // 2 - 1)),
        pltpu.SemaphoreType.DMA((2, total // 2)),
        pltpu.SemaphoreType.DMA((6,)),
        pltpu.SemaphoreType.DMA((len(operands),)),
    ]
    whole = pl.BlockSpec(memory_space=pltpu.VMEM)
    state, table = pl.pallas_call(
        functools.partial(whole_kernel, (count_x, count_y, channels, hidden, size_x, size_yz)),
        out_shape=[
            jax.ShapeDtypeStruct(perturbation.shape, F32),
            jax.ShapeDtypeStruct((height, LANES), WIRE),
        ],
        in_specs=[pl.BlockSpec(memory_space=pltpu.HBM)] * len(operands),
        out_specs=[whole] * 2,
        scratch_shapes=scratch,
        compiler_params=pltpu.CompilerParams(
            collective_id=0, has_side_effects=True, vmem_limit_bytes=56 * 2**20
        ),
    )(*operands)
    return tuple(
        pl.pallas_call(
            functools.partial(unpack_kernel, (channels, hidden)),
            out_shape=[jax.ShapeDtypeStruct(r.shape, F32) for r in results],
            in_specs=[whole] * 2,
            out_specs=[whole] * len(results),
            scratch_shapes=[
                vmem((3 * 48, 2 * LANES), b16),
                vmem((3 * 16, LANES), b16),
                vmem((taps, LANES), F32),
            ],
            compiler_params=pltpu.CompilerParams(vmem_limit_bytes=56 * 2**20),
        )(state, table)
    )


def solution(mesh):
    return jax.shard_map(
        body,
        mesh=mesh,
        in_specs=(
            P(None, "gx", "gy"),
            P("gx", "gy"),
            P("gx", "gy"),
            P(None, "gx", "gy"),
            P(),
            P(),
            P(),
        ),
        out_specs=(P(None, "gx", "gy"), P(), P(), P()),
        check_vma=False,
    )
```
